256 devices in a mesh: slab: 64 (over y, z, core), batch: 4 (over x).
Axes of the slice: x: 4, y: 4, z: 8, core: 2. Of those that a mesh axis runs over, the one named last changes fastest.
Arguments:
- velocity_old: float32 [512, 64, 2, 3, 128], P('slab', 'batch'), may hold values from -6 to 6
- traction: bfloat16 [49152, 3, 169], P(('slab', 'batch')), may hold values from -6 to 6
- offsets: bfloat16 [49152, 3, 338], P(('slab', 'batch')), may hold values from -1 to 2
- owner_slab: int32 [49152, 1], P(('slab', 'batch')), may hold values from 0 to 63; in each aligned block of 192 rows (0 to 191, 192 to 383, ...) at most 6 rows name the same one
- anchor: int32 [49152, 3], P(('slab', 'batch')), may hold values from 1 to 253, as said below
- blocks: int32 [49152, 16], P(('slab', 'batch')), may hold values from 0 to 1023, as said below
- block_count: int32 [49152], P(('slab', 'batch')), may hold values from 8 to 16, as said below
- synthesis: bfloat16 [169, 338], replicated, may hold values from -0.5 to 0.5
- analysis: bfloat16 [169, 338], replicated, may hold values from -0.3125 to 0.3125
Outputs:
- velocity_new: float32 [512, 64, 2, 3, 128], P('slab', 'batch')
- velocity_coef: bfloat16 [49152, 3, 169], P(('slab', 'batch'))
The draws below stay inside these ranges and needn't reach their ends.
Inputs may be any that keep to these rules, and one draw needn't show every extreme that they name: `owner_slab`: among the 192 cells of one device at most 6 name the same slab, and that bound is reached. `anchor`: in the owner's slab: first coordinate 1 to 5, second 1 to 61, third 1 to 125 within its tile of 128 points. `blocks`: the first block_count entries of a cell are distinct lines within two cells of its anchor in the first two dimensions, in its anchor's tile along the third; the remaining entries are padding with any tile number. `block_count`: some cells of every device use all 16 blocks.
All inputs are finite; a program needn't handle non-finite values.
Results may differ from the reference program's by a relative error of at most 0.012.
Values may be sent and summed in bfloat16 or wider, within the bound.
A program may use at most 64 MiB of HBM per device.

```python
import math
import jax
import jax.numpy as jnp
import numpy as np
from jax import lax

L = 169
Q = 338
B = 16
SWEEPS = 2
GX = 8
NY = 64
NZ = 256
CELLS_DEV = 192
CAP = 6
NX = 512
CELLS = 49152
N_SLAB = 64


def stencil_layout(key):
    base = jax.random.fold_in(key, 11)
    subkeys = jax.random.split(base, 7)
    layers = NZ // 128
    tiles_dev = GX * NY * layers
    anchor_x = jax.random.randint(subkeys[0], (CELLS,), 1, GX - 2)
    anchor_y = jax.random.randint(subkeys[1], (CELLS,), 1, NY - 2)
    tile_z = jax.random.randint(subkeys[2], (CELLS,), 0, layers)
    anchor_z = tile_z * 128 + jax.random.randint(subkeys[3], (CELLS,), 1, 126)
    line_index = jnp.arange(16)
    shift_x = line_index // 4 - 1
    shift_y = line_index % 4 - 1
    scores = jax.random.randint(subkeys[4], (CELLS, 16), 0, 4096) * 16 + line_index[None, :]
    chosen = jnp.argsort(scores, axis=1)[:, :B]
    tile_ids = ((anchor_x[:, None] + shift_x[chosen]) * NY + anchor_y[:, None] + shift_y[chosen]) * layers + tile_z[:, None]
    drawn_count = jax.random.randint(subkeys[5], (CELLS,), B // 2, B + 1)
    pinned = jnp.arange(CELLS) % 4 == 0
    count = jnp.where(pinned, B, drawn_count)
    filler = jax.random.randint(subkeys[6], (CELLS, B), 0, tiles_dev)
    blocks = jnp.where(jnp.arange(B)[None, :] < count[:, None], tile_ids, filler)
    anchor = jnp.stack([anchor_x, anchor_y, anchor_z], axis=1)
    return (anchor.astype(jnp.int32), blocks.astype(jnp.int32), count.astype(jnp.int32))


def draw_anchor(key, part):
    return stencil_layout(key)[0]


def draw_blocks(key, part):
    return stencil_layout(key)[1]


def draw_block_count(key, part):
    return stencil_layout(key)[2]


def block_levels(own_key, extent, shards, least, high):
    def one(axis_at, shards_of):
        steps = jax.random.uniform(jax.random.fold_in(jax.random.fold_in(own_key, 6), axis_at), (shards_of,), jnp.float32, least / len(shards), high / len(shards))
        return jnp.repeat(jnp.exp(steps), extent[axis_at] // shards_of).reshape((-1,) + (1,) * (len(extent) - axis_at - 1))

    gain = one(*shards[0])
    for cut in shards[1:]:
        gain = gain * one(*cut)
    return gain


def routed_block(rng, own, number, rows, count, top, most, slope):
    sequence = jax.random.permutation(rng, count)
    heavy_load, usual = load_shares(count, rows * top, most, slope, True), load_shares(count, rows * top, most, slope, False)
    places = jnp.arange(count)

    def named(tallies, turn):
        used = int((tallies > 0).sum())
        fixed = max(1, used // 4)
        shifted = fixed + (places - fixed + turn * (used - fixed)) % max(1, count - fixed)
        return jnp.zeros((count,), jnp.int32).at[sequence[jnp.where(places < fixed, places, shifted)]].set(jnp.asarray(tallies, jnp.int32))

    tallies = jnp.where(number % 4 == 0, named(heavy_load, number // 4), named(usual, number - number // 4 - 1))
    mixed = jax.random.permutation(jax.random.fold_in(own, 3), count)
    giver, taker = mixed[0:count // 2 * 2:2], mixed[1:count // 2 * 2:2]
    room = jnp.minimum(tallies[giver] - 1, most - tallies[taker]) // 2
    room = jnp.where((giver == sequence[0]) | (taker == sequence[0]) | (tallies[taker] == 0), 0, jnp.maximum(room, 0))
    shifted = jax.random.randint(jax.random.fold_in(own, 4), (count // 2,), 0, 1 << 20) % (room + 1)
    tallies = tallies.at[giver].add(-shifted).at[taker].add(shifted)
    members = jnp.searchsorted(jnp.cumsum(tallies), jnp.arange(rows * top), side="right").astype(jnp.int32)
    table = members.reshape(top, rows).T
    table = table[jax.random.permutation(jax.random.fold_in(own, 1), rows)]
    turn = jax.random.randint(jax.random.fold_in(own, 2), (rows, 1), 0, top)
    return jnp.take_along_axis(table, (jnp.arange(top)[None, :] + turn) % top, axis=1)


def load_shares(count, total, bound, lean, full):
    portions = [(1 << 20) // math.isqrt(grade ** lean) + 1 for grade in range(1, count + 1)]
    largest = bound if full else min(bound, max(-(-total // count), total * portions[0] // sum(portions)))
    least = 1 if total - largest >= count - 1 else 0
    given, rest = [largest] + [least] * (count - 1), total - largest - least * (count - 1)
    while rest > 0:
        movable = [i for i in range(1, count) if given[i] < largest] or [i for i in range(1, count) if given[i] < bound]
        whole, budget = sum([portions[i] for i in movable]), rest
        for i in movable:
            more = min(bound - given[i], max(1, budget * portions[i] // whole), rest)
            given[i] = given[i] + more
            rest = rest - more
    return np.array(given)


def centred(own_key, shape, scale, most, cuts=(), kind=jnp.bfloat16):
    level = block_levels(own_key, shape, cuts, -0.22, 0.18) if cuts else 1.0
    values = jax.random.normal(own_key, shape, jnp.float32) * scale * level
    return jnp.minimum(jnp.maximum(values, -most), most).astype(kind)


def setup_inputs(seed: int = 0) -> dict:
    arg_keys = jax.random.split(jax.random.key(seed), 10)
    velocity_old = centred(arg_keys[0], (NX, NY, NZ // 128, 3, 128), 1.0, 6.0, ((0, 64), (1, 4)), jnp.float32)
    traction = centred(arg_keys[1], (CELLS, 3, L), 1.0, 6.0, ((0, 256),))
    offsets = jnp.clip(-1.0 + 3.0 * jax.random.uniform(arg_keys[2], (CELLS, 3, Q), jnp.float32) ** block_levels(arg_keys[2], (CELLS, 3, Q), ((0, 256),), -0.2, 0.2), -1.0, 2.0).astype(jnp.bfloat16)
    owner_slab_keys = jax.random.split(jax.random.fold_in(arg_keys[3], 1), CELLS // CELLS_DEV)
    owner_slab_turns = jax.random.permutation(jax.random.fold_in(arg_keys[3], 3), CELLS // CELLS_DEV)
    owner_slab = jax.vmap(lambda own, number: routed_block(jax.random.fold_in(arg_keys[3], 2), own, number, CELLS_DEV, N_SLAB, 1, CAP, 2))(owner_slab_keys, owner_slab_turns).reshape((CELLS, 1))
    anchor = draw_anchor(jax.random.fold_in(arg_keys[9], 71), 0)
    blocks = draw_blocks(jax.random.fold_in(arg_keys[9], 71), 0)
    block_count = draw_block_count(jax.random.fold_in(arg_keys[9], 71), 0)
    synthesis = centred(arg_keys[7], (L, Q), L ** -0.5, 0.5)
    analysis = centred(arg_keys[8], (L, Q), Q ** -0.5, 0.3125)
    return {"velocity_old": velocity_old, "traction": traction, "offsets": offsets, "owner_slab": owner_slab, "anchor": anchor, "blocks": blocks, "block_count": block_count, "synthesis": synthesis, "analysis": analysis}


kernel_width = 0.8
kernel_norm = 1.0 / (0.8 * math.sqrt(2.0 * math.pi))
coupling = 2.0

def kernel_value(distance):
    scaled = distance / kernel_width
    return jnp.exp(-0.5 * scaled * scaled) * kernel_norm

def stencil_weights(anchor_part, offset_part, block_part, count_part):
    layers = NZ // 128
    points = anchor_part[:, :, None].astype(jnp.float32) + offset_part.astype(jnp.float32)
    tile_x = (block_part // (NY * layers)).astype(jnp.float32)
    tile_y = (block_part // layers % NY).astype(jnp.float32)
    live_mask = (jnp.arange(block_part.shape[1])[None, :] < count_part[:, None]).astype(jnp.float32)
    weight_xy = kernel_value(points[:, 0, None, :] - tile_x[:, :, None]) * kernel_value(points[:, 1, None, :] - tile_y[:, :, None]) * live_mask[:, :, None]
    z_root = (anchor_part[:, 2] // 128 * 128).astype(jnp.float32)
    heights = z_root[:, None, None] + jnp.arange(128, dtype=jnp.float32)[None, None, :]
    weight_z = kernel_value(points[:, 2, :, None] - heights).astype(jnp.bfloat16)
    return (weight_xy, weight_z)

def neighbours(padded):
    centre = padded[1:-1, 1:-1]
    total = padded[2:, 1:-1] + padded[:-2, 1:-1] + padded[1:-1, 2:] + padded[1:-1, :-2]
    zero_edge = jnp.zeros(centre.shape[:2] + (1, centre.shape[3], 1), centre.dtype)
    after = jnp.concatenate([centre[:, :, 1:, :, :1], zero_edge], axis=2)
    before = jnp.concatenate([zero_edge, centre[:, :, :-1, :, -1:]], axis=2)
    upper = jnp.concatenate([centre[..., 1:], after], axis=-1)
    lower = jnp.concatenate([before, centre[..., :-1]], axis=-1)
    return total + upper + lower

def relax(drive, widen):
    state = drive
    for sweep_index in range(SWEEPS):
        state = (drive + coupling * neighbours(widen(state))) / (1.0 + 6.0 * coupling)
    return state

def reference(velocity_old, traction, offsets, owner_slab, anchor, blocks, block_count, synthesis, analysis):
    layers = NZ // 128
    tiles_dev = GX * NY * layers
    groups = CELLS // CELLS_DEV

    def split_cells(values):
        return values.reshape((groups, CELLS_DEV) + values.shape[1:])
    cell_data = tuple((split_cells(values) for values in (traction, offsets, owner_slab[:, 0], anchor, blocks, block_count)))

    def spread_step(grid_sum, piece):
        coef_part, offset_part, owner_part, anchor_part, block_part, count_part = piece
        weight_xy, weight_z = stencil_weights(anchor_part, offset_part, block_part, count_part)
        forces = jnp.einsum('ckl,lq->ckq', coef_part.astype(jnp.float32), synthesis.astype(jnp.float32))
        weighted = (forces[:, None] * weight_xy[:, :, None]).astype(jnp.bfloat16)
        tile_terms = jnp.einsum('cbkq,cqi->cbki', weighted.astype(jnp.float32), weight_z.astype(jnp.float32))
        targets = (owner_part[:, None] * tiles_dev + block_part).reshape(-1)
        return (grid_sum.at[targets].add(tile_terms.reshape(-1, 3, 128)), None)
    start = jnp.zeros((NX * NY * layers, 3, 128), jnp.float32)
    forcing, ignored = lax.scan(spread_step, start, cell_data)
    drive = velocity_old + forcing.reshape(velocity_old.shape)

    def widen(state):
        return jnp.pad(state, ((1, 1), (1, 1), (0, 0), (0, 0), (0, 0)))
    velocity_new = relax(drive, widen)
    flat_velocity = velocity_new.astype(jnp.bfloat16).reshape(-1, 3, 128)

    def sample_step(piece):
        coef_part, offset_part, owner_part, anchor_part, block_part, count_part = piece
        weight_xy, weight_z = stencil_weights(anchor_part, offset_part, block_part, count_part)
        targets = owner_part[:, None] * tiles_dev + block_part
        gathered = flat_velocity[targets]
        projected = jnp.einsum('cbki,cqi->cbkq', gathered.astype(jnp.float32), weight_z.astype(jnp.float32))
        point_velocity = lax.optimization_barrier(jnp.sum(projected * weight_xy[:, :, None, :], axis=1)).astype(jnp.bfloat16)
        return jnp.einsum('ckq,lq->ckl', point_velocity.astype(jnp.float32), analysis.astype(jnp.float32)).astype(jnp.bfloat16)
    coefs = lax.map(sample_step, cell_data)
    return (velocity_new, coefs.reshape(CELLS, 3, analysis.shape[0]))
```

```python
import math

import jax
import jax.numpy as jnp
from jax import lax
from jax.experimental import pallas as pl
from jax.experimental.pallas import tpu as pltpu
from jax.sharding import PartitionSpec as P

SWEEPS = 2
GX = 8
NY = 64
NZ = 256
LAYERS = NZ // 128

L = 169
Q = 338
B = 16
REM = L - 128

CAP = 6
PLANES = 13
OUT_PLANES = 4
QP = 384

TILES = GX * NY * LAYERS
ROWS = TILES * 3
DUMMY = ROWS

kernel_width = 0.8
coupling = 2.0
SCALE = math.sqrt(0.5 * math.log2(math.e)) / kernel_width
LOG_NORM = -math.log2(0.8 * math.sqrt(2.0 * math.pi))
FAR = 1.0e4

F32 = jnp.float32
BF16 = jnp.bfloat16
NT = (((1,), (1,)), ((), ()))
NN = (((1,), (0,)), ((), ()))
TN = (((0,), (0,)), ((), ()))

VMEM_SPEC = pl.BlockSpec(memory_space=pltpu.VMEM)
ANY_SPEC = pl.BlockSpec(memory_space=pl.ANY)


def dot(a, b, dims):
    return lax.dot_general(a, b, dims, preferred_element_type=F32)


def slot_onehot(row_ref, col_ref, slots):
    cells = row_ref.shape[1]
    row, col = row_ref[...], col_ref[...]
    before = lax.broadcasted_iota(jnp.int32, (cells, cells), 0) < lax.broadcasted_iota(
        jnp.int32, (cells, cells), 1
    )
    same = jnp.where((col == row) & before, 1.0, 0.0)
    rank = jnp.sum(same, axis=0, keepdims=True)
    slot = row * CAP + rank.astype(jnp.int32)
    at = lax.broadcasted_iota(jnp.int32, (slots, cells), 0)
    return jnp.where(at == slot, 1.0, 0.0).astype(BF16)


def pack_kernel(row_ref, col_ref, coef_ref, offs_ref, ints_ref, out_ref, x_ref, blk_ref):
    slab_count = out_ref.shape[0]
    slots = slab_count * CAP
    hot = slot_onehot(row_ref, col_ref, slots)
    for r in range(4):
        x_ref[r] = dot(hot, coef_ref[r], NT)
    tail = jnp.zeros((slots, QP - Q), F32)
    for k in range(3):
        got = dot(hot, offs_ref[k], NN)
        x_ref[4 + 3 * k] = got[:, :128]
        x_ref[5 + 3 * k] = got[:, 128:256]
        x_ref[6 + 3 * k] = jnp.concatenate([got[:, 256:], tail], axis=1) + dot(
            hot, ints_ref[k], NT
        )

    def step(target, carry):
        for r in range(PLANES):
            blk_ref[pl.ds(r * CAP, CAP), :] = x_ref[r, pl.ds(target * CAP, CAP), :]
        out_ref[target] = blk_ref[...].astype(BF16)
        return carry

    blk_ref[...] = jnp.zeros_like(blk_ref)
    lax.fori_loop(0, slab_count, step, 0)


def pack(row, col, coef_t, offs, ints_t, slab_count):
    block_rows = -(-PLANES * CAP // 16) * 16
    return pl.pallas_call(
        pack_kernel,
        out_shape=jax.ShapeDtypeStruct((slab_count, block_rows, 128), BF16),
        in_specs=[VMEM_SPEC] * 5,
        out_specs=VMEM_SPEC,
        scratch_shapes=[
            pltpu.VMEM((PLANES, slab_count * CAP, 128), F32),
            pltpu.VMEM((block_rows, 128), F32),
        ],
        name="pack",
    )(row, col, coef_t, offs, ints_t)


def unpack_kernel(row_ref, col_ref, back_ref, out_ref, blk_ref, r_ref):
    slab_count = back_ref.shape[0]
    slots = slab_count * CAP
    hot = slot_onehot(row_ref, col_ref, slots)

    def step(source, carry):
        blk_ref[...] = back_ref[source].astype(F32)
        for r in range(OUT_PLANES):
            r_ref[r, pl.ds(source * CAP, CAP), :] = blk_ref[pl.ds(r * CAP, CAP), :]
        return carry

    lax.fori_loop(0, slab_count, step, 0)
    rem = dot(r_ref[3].astype(BF16), hot, TN)
    for k in range(3):
        main = dot(r_ref[k].astype(BF16), hot, TN)
        out_ref[k] = jnp.concatenate([main, rem[k * REM : (k + 1) * REM]], axis=0).astype(BF16)


def unpack(row, col, back):
    slab_count, block_rows, _ = back.shape
    cells = row.shape[1]
    return pl.pallas_call(
        unpack_kernel,
        out_shape=jax.ShapeDtypeStruct((3, L, cells), BF16),
        in_specs=[VMEM_SPEC] * 3,
        out_specs=VMEM_SPEC,
        scratch_shapes=[
            pltpu.VMEM((block_rows, 128), F32),
            pltpu.VMEM((OUT_PLANES, slab_count * CAP, 128), F32),
        ],
        name="unpack",
    )(row, col, back)


def exchange_kernel(x_ref, out_ref, send_sem, recv_sem, local_sem):
    count = x_ref.shape[0]
    me = lax.axis_index("slab")
    barrier = pltpu.get_barrier_semaphore()

    def peer_of(step):
        y = (me // 16 + step // 16) % 4
        z = (me // 2 % 8 + step // 2 % 8) % 8
        core = (me % 2 + step % 2) % 2
        return y * 16 + z * 2 + core

    def greet(step, carry):
        pl.semaphore_signal(
            barrier, inc=1, device_id={"slab": peer_of(step)},
            device_id_type=pl.DeviceIdType.MESH,
        )
        return carry

    lax.fori_loop(1, count, greet, 0)
    pl.semaphore_wait(barrier, count - 1)

    def send(step, carry):
        peer = peer_of(step)
        pltpu.make_async_remote_copy(
            src_ref=x_ref.at[peer],
            dst_ref=out_ref.at[me],
            send_sem=send_sem,
            recv_sem=recv_sem,
            device_id={"slab": peer},
            device_id_type=pl.DeviceIdType.MESH,
        ).start()
        return carry

    lax.fori_loop(1, count, send, 0)
    own = pltpu.make_async_copy(x_ref.at[me], out_ref.at[me], local_sem)
    own.start()
    own.wait()
    others = pl.ds(0, count - 1)
    pltpu.make_async_copy(x_ref.at[others], x_ref.at[others], send_sem).wait()
    pltpu.make_async_copy(out_ref.at[others], out_ref.at[others], recv_sem).wait()


def exchange(x, collective_id):
    return pl.pallas_call(
        exchange_kernel,
        out_shape=jax.ShapeDtypeStruct(x.shape, x.dtype),
        in_specs=[ANY_SPEC],
        out_specs=ANY_SPEC,
        scratch_shapes=[pltpu.SemaphoreType.DMA] * 3,
        compiler_params=pltpu.CompilerParams(collective_id=collective_id, has_side_effects=True),
        name="exchange",
    )(x)


def z_weights(pz):
    step = lax.broadcasted_iota(jnp.int32, (8, QP), 0).astype(F32) * SCALE
    base = pz - step
    parts = []
    for g in range(16):
        d = base - (8.0 * g * SCALE)
        parts.append(jnp.exp2(LOG_NORM - d * d))
    return jnp.concatenate(parts, axis=0).astype(BF16)


def xy_weights(px, py, tx, ty):
    dx = px - tx
    dy = py - ty
    return jnp.exp2(2.0 * LOG_NORM - (dx * dx + dy * dy))


def prepare_kernel_part(recv_ref, blk_ref, r_ref, p_ref, tx_ref, ty_ref, idx_ref):
    slab_count = recv_ref.shape[0]

    def step(source, carry):
        blk_ref[...] = recv_ref[source].astype(F32)
        for r in range(PLANES):
            r_ref[r, pl.ds(source * CAP, CAP), :] = blk_ref[pl.ds(r * CAP, CAP), :]
        return carry

    lax.fori_loop(0, slab_count, step, 0)
    line = lax.broadcasted_iota(jnp.int32, (B, 128), 0)
    for m in range(tx_ref.shape[0]):
        rows = pl.ds(m * 128, 128)
        for k in range(3):
            anchor = r_ref[6 + 3 * k, rows, :][:, 112:113]
            for t in range(3):
                p_ref[k, rows, pl.ds(t * 128, 128)] = (
                    r_ref[4 + 3 * k + t, rows, :] + anchor
                ) * SCALE
        first = jnp.transpose(r_ref[6, rows, :])
        second = jnp.transpose(r_ref[9, rows, :])
        x = first[96:112]
        live = line.astype(F32) < first[113:114]
        v = second[96:112]
        y = jnp.floor(v * 0.5)
        tx_ref[m] = jnp.where(live, x * SCALE, FAR)
        ty_ref[m] = y * SCALE
        row = (x * NY + y) * (3 * LAYERS) + (v - 2.0 * y)
        idx_ref[m] = jnp.where(live, row.astype(jnp.int32), DUMMY + 8 * line)


def group_columns(tx_ref, ty_ref, g):
    m = g // 16
    shift = (128 - (g % 16) * 8) % 128
    return pltpu.roll(tx_ref[m], shift, 1), pltpu.roll(ty_ref[m], shift, 1)


def spread_kernel(
    recv_ref, syn_ref, out_ref, p_ref, tx_ref, ty_ref, idx_ref,
    blk_ref, r_ref, f_ref, acc_ref, t_ref, idx_smem,
):
    prepare_kernel_part(recv_ref, blk_ref, r_ref, p_ref, tx_ref, ty_ref, idx_ref)
    pltpu.sync_copy(idx_ref, idx_smem)
    for k in range(3):
        coef = jnp.concatenate([r_ref[k], r_ref[3]], axis=1).astype(BF16)
        f_ref[k] = dot(coef, syn_ref[k], NN)
    acc_ref[...] = jnp.zeros_like(acc_ref)

    def group(g, carry):
        txs, tys = group_columns(tx_ref, ty_ref, g)
        for u in range(8):
            c = g * 8 + u
            wxy = xy_weights(
                p_ref[0, pl.ds(c, 1), :], p_ref[1, pl.ds(c, 1), :],
                txs[:, u : u + 1], tys[:, u : u + 1],
            )
            weighted = jnp.concatenate(
                [wxy * f_ref[k, pl.ds(c, 1), :] for k in range(3)], axis=0
            ).astype(BF16)
            wz = z_weights(p_ref[2, pl.ds(c, 1), :])
            t_ref[u] = dot(weighted, wz, NT)
        for u in range(8):
            m, lane = g // 16, (g % 16) * 8 + u
            starts = [idx_smem[m, j, lane] for j in range(B)]
            sums = [
                acc_ref[pl.ds(starts[j], 3, stride=2), :] + t_ref[u, pl.ds(j, 3, stride=B), :]
                for j in range(B)
            ]
            for j in range(B):
                acc_ref[pl.ds(starts[j], 3, stride=2), :] = sums[j]
        return carry

    lax.fori_loop(0, recv_ref.shape[0] * CAP // 8, group, 0)
    out_ref[...] = acc_ref[:ROWS, :].astype(BF16)


def spread(recv, syn):
    slab_count, block_rows, _ = recv.shape
    slots = slab_count * CAP
    chunks = slots // 128
    return pl.pallas_call(
        spread_kernel,
        out_shape=(
            jax.ShapeDtypeStruct((ROWS, 128), BF16),
            jax.ShapeDtypeStruct((3, slots, QP), F32),
            jax.ShapeDtypeStruct((chunks, B, 128), F32),
            jax.ShapeDtypeStruct((chunks, B, 128), F32),
            jax.ShapeDtypeStruct((chunks, B, 128), jnp.int32),
        ),
        in_specs=[VMEM_SPEC] * 2,
        out_specs=(VMEM_SPEC,) * 5,
        scratch_shapes=[
            pltpu.VMEM((block_rows, 128), F32),
            pltpu.VMEM((PLANES, slots, 128), F32),
            pltpu.VMEM((3, slots, QP), F32),
            pltpu.VMEM((ROWS + 8 * B, 128), F32),
            pltpu.VMEM((8, 3 * B, 128), F32),
            pltpu.SMEM((chunks, B, 128), jnp.int32),
        ],
        name="spread",
    )(recv, syn)


def sample_kernel(
    vel_ref, p_ref, tx_ref, ty_ref, idx_smem, ana_ref, out_ref,
    v_ref, g_ref, pv_ref, c_ref, blk_ref,
):
    v_ref[:ROWS, :] = vel_ref[...].astype(F32)
    v_ref[ROWS:, :] = jnp.zeros((v_ref.shape[0] - ROWS, 128), F32)
    slots = p_ref.shape[1]

    def group(g, carry):
        txs, tys = group_columns(tx_ref, ty_ref, g)
        for u in range(8):
            m, lane = g // 16, (g % 16) * 8 + u
            for j in range(B):
                start = idx_smem[m, j, lane]
                g_ref[u, pl.ds(j, 3, stride=B), :] = v_ref[pl.ds(start, 3, stride=2), :]
        for u in range(8):
            c = g * 8 + u
            wxy = xy_weights(
                p_ref[0, pl.ds(c, 1), :], p_ref[1, pl.ds(c, 1), :],
                txs[:, u : u + 1], tys[:, u : u + 1],
            )
            wz = z_weights(p_ref[2, pl.ds(c, 1), :])
            projected = dot(g_ref[u].astype(BF16), wz, NN)
            for k in range(3):
                pv_ref[k, pl.ds(c, 1), :] = jnp.sum(
                    projected[k * B : (k + 1) * B] * wxy, axis=0, keepdims=True
                )
        return carry

    lax.fori_loop(0, slots // 8, group, 0)
    rem = jnp.zeros((slots, 128), F32)
    for k in range(3):
        got = dot(pv_ref[k].astype(BF16), ana_ref[k], NN)
        c_ref[k] = got[:, :128]
        rem = rem + got[:, 128:]
    c_ref[3] = rem

    def step(target, carry):
        for r in range(OUT_PLANES):
            blk_ref[pl.ds(r * CAP, CAP), :] = c_ref[r, pl.ds(target * CAP, CAP), :]
        out_ref[target] = blk_ref[...].astype(BF16)
        return carry

    lax.fori_loop(0, out_ref.shape[0], step, 0)


def sample(vel, p, tx, ty, idx, ana, slab_count):
    slots = p.shape[1]
    block_rows = OUT_PLANES * CAP
    return pl.pallas_call(
        sample_kernel,
        out_shape=jax.ShapeDtypeStruct((slab_count, block_rows, 128), BF16),
        in_specs=[VMEM_SPEC] * 4 + [pl.BlockSpec(memory_space=pltpu.SMEM), VMEM_SPEC],
        out_specs=VMEM_SPEC,
        scratch_shapes=[
            pltpu.VMEM((ROWS + 8 * B, 128), F32),
            pltpu.VMEM((8, 3 * B, 128), F32),
            pltpu.VMEM((3, slots, QP), F32),
            pltpu.VMEM((OUT_PLANES, slots, 128), F32),
            pltpu.VMEM((block_rows, 128), F32),
        ],
        name="sample",
    )(vel, p, tx, ty, idx, ana)


def padded_2(block, sides, width):
    for axis, dim in sides:
        count = lax.axis_size(axis)
        forward = [(i, i + 1) for i in range(count - 1)]
        backward = [(target, source) for source, target in forward]
        low = lax.ppermute(
            lax.slice_in_dim(block, block.shape[dim] - width, None, axis=dim), axis, forward
        )
        high = lax.ppermute(lax.slice_in_dim(block, 0, width, axis=dim), axis, backward)
        block = jnp.concatenate([low, block, high], axis=dim)
    return block


def neighbours(padded):
    centre = padded[1:-1, 1:-1]
    total = padded[2:, 1:-1] + padded[:-2, 1:-1] + padded[1:-1, 2:] + padded[1:-1, :-2]
    zero_edge = jnp.zeros(centre.shape[:3] + (1, 1), centre.dtype)
    after = jnp.concatenate([centre[:, :, :, 1:, :1], zero_edge], axis=3)
    before = jnp.concatenate([zero_edge, centre[:, :, :, :-1, -1:]], axis=3)
    upper = jnp.concatenate([centre[..., 1:], after], axis=-1)
    lower = jnp.concatenate([before, centre[..., :-1]], axis=-1)
    return total + upper + lower


def relax(drive, widen):
    state = drive
    for sweep_index in range(SWEEPS):
        state = (drive + coupling * neighbours(widen(state))) / (1.0 + 6.0 * coupling)
    return state


def coef_planes(values):
    n = values.shape[2]
    rest = jnp.concatenate(
        [values[0, 128:], values[1, 128:], values[2, 128:], jnp.zeros((128 - 3 * REM, n), values.dtype)],
        axis=0,
    )
    return jnp.concatenate([values[:, :128], rest[None]], axis=0)


def basis_planes(basis):
    wide = jnp.pad(basis, ((0, 0), (0, QP - Q)))
    return jnp.stack(
        [
            jnp.concatenate(
                [wide[:128], jnp.pad(wide[128:], ((k * REM, 128 - (k + 1) * REM), (0, 0)))], axis=0
            )
            for k in range(3)
        ]
    )


def int_planes(anchor, blocks, count):
    cells = count.shape[0]
    anchor_t, blocks_t = anchor.T, blocks.T
    width = NY * LAYERS
    lists = (blocks_t // width, blocks_t % width, jnp.zeros_like(blocks_t))
    places = (anchor_t[0:1], anchor_t[1:2], anchor_t[2:3] % 128)
    planes = []
    for k in range(3):
        rows = [
            jnp.zeros((96, cells), jnp.int32), lists[k], places[k], count[None],
            jnp.zeros((14, cells), jnp.int32),
        ]
        planes.append(jnp.concatenate(rows, axis=0))
    return jnp.stack(planes).astype(BF16)


def local(
    velocity_old, traction, offsets, owner_slab, anchor, blocks, block_count, synthesis, analysis
):
    slab_count = lax.axis_size("slab")
    row = owner_slab[:, 0][None, :]
    sent = pack(
        row,
        owner_slab,
        coef_planes(traction.transpose(1, 2, 0)),
        offsets.transpose(1, 0, 2),
        int_planes(anchor, blocks, block_count),
        slab_count,
    )
    received = exchange(sent, 0)
    partial_value, p, tx, ty, idx = spread(received, basis_planes(synthesis))
    partial_value = partial_value.reshape(GX, NY, 3, LAYERS, 128)
    drive = velocity_old.transpose(0, 1, 3, 2, 4) + lax.psum_scatter(
        partial_value, "batch", scatter_dimension=1, tiled=True
    ).astype(F32)

    def widen(state):
        return padded_2(state.astype(BF16), (("slab", 0), ("batch", 1)), 1).astype(state.dtype)

    velocity_new = relax(drive, widen)
    slab_velocity = lax.all_gather(velocity_new.astype(BF16), "batch", axis=1, tiled=True)
    coefs = sample(
        slab_velocity.reshape(ROWS, 128), p, tx, ty, idx,
        basis_planes(analysis).transpose(0, 2, 1), slab_count,
    )
    velocity_coef = unpack(row, owner_slab, exchange(coefs, 1))
    return (velocity_new.transpose(0, 1, 3, 2, 4), velocity_coef.transpose(2, 0, 1))


def solution(mesh):
    in_specs = (
        P("slab", "batch", None, None, None),
        P(("slab", "batch"), None, None),
        P(("slab", "batch"), None, None),
        P(("slab", "batch"), None),
        P(("slab", "batch"), None),
        P(("slab", "batch"), None),
        P(("slab", "batch")),
        P(),
        P(),
    )
    out_specs = (P("slab", "batch", None, None, None), P(("slab", "batch"), None, None))
    return jax.shard_map(local, mesh=mesh, in_specs=in_specs, out_specs=out_specs, check_vma=False)
```

```python
import math

import jax
import jax.numpy as jnp
from jax import lax
from jax.experimental import pallas as pl
from jax.experimental.pallas import tpu as pltpu
from jax.sharding import PartitionSpec as P

SWEEPS = 2
GX = 8
NY = 64
NZ = 256
LAYERS = NZ // 128

L = 169
Q = 338
B = 16
REM = L - 128

CAP = 6
PLANES = 13
OUT_PLANES = 4
QP = 384

TILES = GX * NY * LAYERS
ROWS = TILES * 3
DUMMY = ROWS

kernel_width = 0.8
coupling = 2.0
SCALE = math.sqrt(0.5 * math.log2(math.e)) / kernel_width
LOG_NORM = -math.log2(0.8 * math.sqrt(2.0 * math.pi))
FAR = 1.0e4

F32 = jnp.float32
BF16 = jnp.bfloat16
NT = (((1,), (1,)), ((), ()))
NN = (((1,), (0,)), ((), ()))
TN = (((0,), (0,)), ((), ()))

VMEM_SPEC = pl.BlockSpec(memory_space=pltpu.VMEM)
ANY_SPEC = pl.BlockSpec(memory_space=pl.ANY)


def dot(a, b, dims):
    return lax.dot_general(a, b, dims, preferred_element_type=F32)


def slot_onehot(owner_ref, slab_count):
    cells = owner_ref.shape[1]
    owner = owner_ref[...]
    slab_at = lax.broadcasted_iota(jnp.int32, (slab_count, cells), 0)
    member = jnp.where(slab_at == owner, 1.0, 0.0)
    first = lax.broadcasted_iota(jnp.int32, (cells, cells), 0)
    second = lax.broadcasted_iota(jnp.int32, (cells, cells), 1)
    before = jnp.where(first < second, 1.0, 0.0).astype(BF16)
    rank = jnp.sum(member * dot(member.astype(BF16), before, NN), axis=0, keepdims=True)
    slot = owner * CAP + rank.astype(jnp.int32)
    at = lax.broadcasted_iota(jnp.int32, (slab_count * CAP, cells), 0)
    return jnp.where(at == slot, 1.0, 0.0).astype(BF16)


def pack_kernel(
    owner_ref, coef_ref, offs_ref, anchor_ref, blocks_ref, count_ref, out_ref,
    x_ref, blk_ref, rows_ref,
):
    slab_count = out_ref.shape[0]
    slots = slab_count * CAP
    hot = slot_onehot(owner_ref, slab_count)
    rows_ref[...] = jnp.zeros_like(rows_ref)
    for k in range(3):
        x_ref[k] = dot(hot, coef_ref[k, :128, :], NT)
        rows_ref[k * REM : (k + 1) * REM] = coef_ref[k, 128:, :].astype(F32)
    x_ref[3] = dot(hot, rows_ref[...].astype(BF16), NT)
    rows_ref[...] = jnp.zeros_like(rows_ref)
    tail = jnp.zeros((slots, QP - Q), F32)
    width = NY * LAYERS
    lists = (blocks_ref[...] // width, blocks_ref[...] % width, None)
    for k in range(3):
        if lists[k] is not None:
            rows_ref[96:112] = lists[k].astype(F32)
        place = anchor_ref[k : k + 1, :]
        rows_ref[112:113] = (place % 128 if k == 2 else place).astype(F32)
        rows_ref[113:114] = count_ref[...].astype(F32)
        got = dot(hot, offs_ref[k], NN)
        x_ref[4 + 3 * k] = got[:, :128]
        x_ref[5 + 3 * k] = got[:, 128:256]
        x_ref[6 + 3 * k] = jnp.concatenate([got[:, 256:], tail], axis=1) + dot(
            hot, rows_ref[...].astype(BF16), NT
        )

    def step(target, carry):
        for r in range(PLANES):
            blk_ref[pl.ds(r * CAP, CAP), :] = x_ref[r, pl.ds(target * CAP, CAP), :]
        out_ref[target] = blk_ref[...].astype(BF16)
        return carry

    blk_ref[...] = jnp.zeros_like(blk_ref)
    lax.fori_loop(0, slab_count, step, 0)


def pack(owner, coef, offs, anchor, blocks, count, slab_count):
    block_rows = -(-PLANES * CAP // 16) * 16
    return pl.pallas_call(
        pack_kernel,
        out_shape=jax.ShapeDtypeStruct((slab_count, block_rows, 128), BF16),
        in_specs=[VMEM_SPEC] * 6,
        out_specs=VMEM_SPEC,
        scratch_shapes=[
            pltpu.VMEM((PLANES, slab_count * CAP, 128), F32),
            pltpu.VMEM((block_rows, 128), F32),
            pltpu.VMEM((128, owner.shape[1]), F32),
        ],
        name="pack",
    )(owner, coef, offs, anchor, blocks, count)


def unpack_kernel(owner_ref, back_ref, out_ref, blk_ref, r_ref):
    slab_count = back_ref.shape[0]
    hot = slot_onehot(owner_ref, slab_count)

    def step(source, carry):
        blk_ref[...] = back_ref[source].astype(F32)
        for r in range(OUT_PLANES):
            r_ref[r, pl.ds(source * CAP, CAP), :] = blk_ref[pl.ds(r * CAP, CAP), :]
        return carry

    lax.fori_loop(0, slab_count, step, 0)
    rem = dot(r_ref[3].astype(BF16), hot, TN)
    for k in range(3):
        main = dot(r_ref[k].astype(BF16), hot, TN)
        out_ref[k] = jnp.concatenate([main, rem[k * REM : (k + 1) * REM]], axis=0).astype(BF16)


def unpack(owner, back):
    slab_count, block_rows, _ = back.shape
    cells = owner.shape[1]
    return pl.pallas_call(
        unpack_kernel,
        out_shape=jax.ShapeDtypeStruct((3, L, cells), BF16),
        in_specs=[VMEM_SPEC] * 2,
        out_specs=VMEM_SPEC,
        scratch_shapes=[
            pltpu.VMEM((block_rows, 128), F32),
            pltpu.VMEM((OUT_PLANES, slab_count * CAP, 128), F32),
        ],
        name="unpack",
    )(owner, back)


def exchange_kernel(x_ref, out_ref, send_sem, recv_sem, local_sem):
    count = x_ref.shape[0]
    me = lax.axis_index("slab")
    barrier = pltpu.get_barrier_semaphore()

    def peer_of(step):
        y = (me // 16 + step // 16) % 4
        z = (me // 2 % 8 + step // 2 % 8) % 8
        core = (me % 2 + step % 2) % 2
        return y * 16 + z * 2 + core

    def greet(step, carry):
        pl.semaphore_signal(
            barrier, inc=1, device_id={"slab": peer_of(step)},
            device_id_type=pl.DeviceIdType.MESH,
        )
        return carry

    lax.fori_loop(1, count, greet, 0)
    pl.semaphore_wait(barrier, count - 1)

    def send(step, carry):
        peer = peer_of(step)
        pltpu.make_async_remote_copy(
            src_ref=x_ref.at[peer],
            dst_ref=out_ref.at[me],
            send_sem=send_sem,
            recv_sem=recv_sem,
            device_id={"slab": peer},
            device_id_type=pl.DeviceIdType.MESH,
        ).start()
        return carry

    lax.fori_loop(1, count, send, 0)
    own = pltpu.make_async_copy(x_ref.at[me], out_ref.at[me], local_sem)
    own.start()
    own.wait()
    others = pl.ds(0, count - 1)
    pltpu.make_async_copy(x_ref.at[others], x_ref.at[others], send_sem).wait()
    pltpu.make_async_copy(out_ref.at[others], out_ref.at[others], recv_sem).wait()


def exchange(x, collective_id):
    return pl.pallas_call(
        exchange_kernel,
        out_shape=jax.ShapeDtypeStruct(x.shape, x.dtype),
        in_specs=[ANY_SPEC],
        out_specs=ANY_SPEC,
        scratch_shapes=[pltpu.SemaphoreType.DMA] * 3,
        compiler_params=pltpu.CompilerParams(collective_id=collective_id, has_side_effects=True),
        name="exchange",
    )(x)


def basis_plane(basis_ref, wide_ref, k):
    if k == 0:
        wide_ref[...] = jnp.zeros_like(wide_ref)
        wide_ref[:128, :Q] = basis_ref[:128, :].astype(F32)
    else:
        wide_ref[128 + (k - 1) * REM : 128 + k * REM, :Q] = jnp.zeros((REM, Q), F32)
    wide_ref[128 + k * REM : 128 + (k + 1) * REM, :Q] = basis_ref[128:, :].astype(F32)
    return wide_ref[...].astype(BF16)


def z_weights(pz):
    step = lax.broadcasted_iota(jnp.int32, (8, QP), 0).astype(F32) * SCALE
    base = pz - step
    parts = []
    for g in range(16):
        d = base - (8.0 * g * SCALE)
        parts.append(jnp.exp2(LOG_NORM - d * d))
    return jnp.concatenate(parts, axis=0).astype(BF16)


def xy_weights(px, py, tx, ty):
    dx = px - tx
    dy = py - ty
    return jnp.exp2(2.0 * LOG_NORM - (dx * dx + dy * dy))


def prepare_kernel_part(recv_ref, blk_ref, r_ref, p_ref, tx_ref, ty_ref, idx_ref):
    slab_count = recv_ref.shape[0]

    def step(source, carry):
        blk_ref[...] = recv_ref[source].astype(F32)
        for r in range(PLANES):
            r_ref[r, pl.ds(source * CAP, CAP), :] = blk_ref[pl.ds(r * CAP, CAP), :]
        return carry

    lax.fori_loop(0, slab_count, step, 0)
    line = lax.broadcasted_iota(jnp.int32, (B, 128), 0)
    for m in range(tx_ref.shape[0]):
        rows = pl.ds(m * 128, 128)
        for k in range(3):
            anchor = r_ref[6 + 3 * k, rows, :][:, 112:113]
            for t in range(3):
                p_ref[k, rows, pl.ds(t * 128, 128)] = (
                    r_ref[4 + 3 * k + t, rows, :] + anchor
                ) * SCALE
        first = jnp.transpose(r_ref[6, rows, :])
        second = jnp.transpose(r_ref[9, rows, :])
        x = first[96:112]
        live = line.astype(F32) < first[113:114]
        v = second[96:112]
        y = jnp.floor(v * 0.5)
        tx_ref[m] = jnp.where(live, x * SCALE, FAR)
        ty_ref[m] = y * SCALE
        row = (x * NY + y) * (3 * LAYERS) + (v - 2.0 * y)
        idx_ref[m] = jnp.where(live, row.astype(jnp.int32), DUMMY + 8 * line)


def group_columns(tx_ref, ty_ref, g):
    m = g // 16
    shift = (128 - (g % 16) * 8) % 128
    return pltpu.roll(tx_ref[m], shift, 1), pltpu.roll(ty_ref[m], shift, 1)


def spread_kernel(
    recv_ref, syn_ref, out_ref, p_ref, tx_ref, ty_ref, idx_ref,
    blk_ref, r_ref, f_ref, acc_ref, t_ref, idx_smem, wide_ref,
):
    prepare_kernel_part(recv_ref, blk_ref, r_ref, p_ref, tx_ref, ty_ref, idx_ref)
    pltpu.sync_copy(idx_ref, idx_smem)
    for k in range(3):
        coef = jnp.concatenate([r_ref[k], r_ref[3]], axis=1).astype(BF16)
        f_ref[k] = dot(coef, basis_plane(syn_ref, wide_ref, k), NN)
    acc_ref[...] = jnp.zeros_like(acc_ref)

    def group(g, carry):
        txs, tys = group_columns(tx_ref, ty_ref, g)
        for u in range(8):
            c = g * 8 + u
            wxy = xy_weights(
                p_ref[0, pl.ds(c, 1), :], p_ref[1, pl.ds(c, 1), :],
                txs[:, u : u + 1], tys[:, u : u + 1],
            )
            weighted = jnp.concatenate(
                [wxy * f_ref[k, pl.ds(c, 1), :] for k in range(3)], axis=0
            ).astype(BF16)
            wz = z_weights(p_ref[2, pl.ds(c, 1), :])
            t_ref[u] = dot(weighted, wz, NT)
        for u in range(8):
            m, lane = g // 16, (g % 16) * 8 + u
            starts = [idx_smem[m, j, lane] for j in range(B)]
            sums = [
                acc_ref[pl.ds(starts[j], 3, stride=2), :] + t_ref[u, pl.ds(j, 3, stride=B), :]
                for j in range(B)
            ]
            for j in range(B):
                acc_ref[pl.ds(starts[j], 3, stride=2), :] = sums[j]
        return carry

    lax.fori_loop(0, recv_ref.shape[0] * CAP // 8, group, 0)
    out_ref[...] = acc_ref[:ROWS, :].astype(BF16)


def spread(recv, syn):
    slab_count, block_rows, _ = recv.shape
    slots = slab_count * CAP
    chunks = slots // 128
    return pl.pallas_call(
        spread_kernel,
        out_shape=(
            jax.ShapeDtypeStruct((ROWS, 128), BF16),
            jax.ShapeDtypeStruct((3, slots, QP), F32),
            jax.ShapeDtypeStruct((chunks, B, 128), F32),
            jax.ShapeDtypeStruct((chunks, B, 128), F32),
            jax.ShapeDtypeStruct((chunks, B, 128), jnp.int32),
        ),
        in_specs=[VMEM_SPEC] * 2,
        out_specs=(VMEM_SPEC,) * 5,
        scratch_shapes=[
            pltpu.VMEM((block_rows, 128), F32),
            pltpu.VMEM((PLANES, slots, 128), F32),
            pltpu.VMEM((3, slots, QP), F32),
            pltpu.VMEM((ROWS + 8 * B, 128), F32),
            pltpu.VMEM((8, 3 * B, 128), F32),
            pltpu.SMEM((chunks, B, 128), jnp.int32),
            pltpu.VMEM((256, QP), F32),
        ],
        name="spread",
    )(recv, syn)


def sample_kernel(
    vel_ref, p_ref, tx_ref, ty_ref, idx_smem, ana_ref, out_ref,
    v_ref, g_ref, pv_ref, c_ref, blk_ref, wide_ref,
):
    v_ref[:ROWS, :] = vel_ref[...].astype(F32)
    v_ref[ROWS:, :] = jnp.zeros((v_ref.shape[0] - ROWS, 128), F32)
    slots = p_ref.shape[1]

    def group(g, carry):
        txs, tys = group_columns(tx_ref, ty_ref, g)
        for u in range(8):
            m, lane = g // 16, (g % 16) * 8 + u
            for j in range(B):
                start = idx_smem[m, j, lane]
                g_ref[u, pl.ds(j, 3, stride=B), :] = v_ref[pl.ds(start, 3, stride=2), :]
        for u in range(8):
            c = g * 8 + u
            wxy = xy_weights(
                p_ref[0, pl.ds(c, 1), :], p_ref[1, pl.ds(c, 1), :],
                txs[:, u : u + 1], tys[:, u : u + 1],
            )
            wz = z_weights(p_ref[2, pl.ds(c, 1), :])
            projected = dot(g_ref[u].astype(BF16), wz, NN)
            for k in range(3):
                pv_ref[k, pl.ds(c, 1), :] = jnp.sum(
                    projected[k * B : (k + 1) * B] * wxy, axis=0, keepdims=True
                )
        return carry

    lax.fori_loop(0, slots // 8, group, 0)
    rem = jnp.zeros((slots, 128), F32)
    for k in range(3):
        got = dot(pv_ref[k].astype(BF16), basis_plane(ana_ref, wide_ref, k), NT)
        c_ref[k] = got[:, :128]
        rem = rem + got[:, 128:]
    c_ref[3] = rem

    def step(target, carry):
        for r in range(OUT_PLANES):
            blk_ref[pl.ds(r * CAP, CAP), :] = c_ref[r, pl.ds(target * CAP, CAP), :]
        out_ref[target] = blk_ref[...].astype(BF16)
        return carry

    lax.fori_loop(0, out_ref.shape[0], step, 0)


def sample(vel, p, tx, ty, idx, ana, slab_count):
    slots = p.shape[1]
    block_rows = OUT_PLANES * CAP
    return pl.pallas_call(
        sample_kernel,
        out_shape=jax.ShapeDtypeStruct((slab_count, block_rows, 128), BF16),
        in_specs=[VMEM_SPEC] * 4 + [pl.BlockSpec(memory_space=pltpu.SMEM), VMEM_SPEC],
        out_specs=VMEM_SPEC,
        scratch_shapes=[
            pltpu.VMEM((ROWS + 8 * B, 128), F32),
            pltpu.VMEM((8, 3 * B, 128), F32),
            pltpu.VMEM((3, slots, QP), F32),
            pltpu.VMEM((OUT_PLANES, slots, 128), F32),
            pltpu.VMEM((block_rows, 128), F32),
            pltpu.VMEM((256, QP), F32),
        ],
        name="sample",
    )(vel, p, tx, ty, idx, ana)


LINE = 3 * LAYERS


def grid_kernel(
    part_ref, vel_ref, new_ref, all_ref,
    hop_ref, got_ref, summed_ref, drive_ref, st_ref, own_ref,
    xs_ref, xr_ref, ys_ref, yr_ref, y32_ref, send_sem, recv_sem, local_sem,
):
    planes, mine, _ = vel_ref.shape
    half = planes // 2
    batches, slabs = lax.axis_size("batch"), lax.axis_size("slab")
    b, s = lax.axis_index("batch"), lax.axis_index("slab")
    right, far, left = [lax.rem(b + i, batches) for i in (1, 2, 3)]
    above, below = lax.rem(s + 1, slabs), lax.rem(s + slabs - 1, slabs)

    barrier = pltpu.get_barrier_semaphore()
    for device in ({"batch": right}, {"batch": left}, {"slab": above}, {"slab": below}):
        pl.semaphore_signal(
            barrier, inc=1, device_id=device, device_id_type=pl.DeviceIdType.MESH
        )
    pl.semaphore_wait(barrier, 4)

    def rows(part):
        return pl.ds(pl.multiple_of(part * mine, mine), mine)

    started = []

    def send(src, dst, **device):
        n = len(started)
        copy = pltpu.make_async_remote_copy(
            src_ref=src, dst_ref=dst, send_sem=send_sem.at[n], recv_sem=recv_sem.at[n],
            device_id=device, device_id_type=pl.DeviceIdType.MESH,
        )
        copy.start()
        started.append(copy)
        return copy

    low, high = pl.ds(0, half), pl.ds(half, half)

    hop_r = send(part_ref.at[low, rows(far)], hop_ref.at[0], batch=right)
    hop_l = send(part_ref.at[high, rows(far)], hop_ref.at[1], batch=left)
    near_r = send(part_ref.at[high, rows(right)], got_ref.at[0], batch=right)
    near_l = send(part_ref.at[low, rows(left)], got_ref.at[1], batch=left)
    hop_r.wait_recv()
    summed_ref[0] = (
        part_ref[low, rows(right), :].astype(F32) + hop_ref[0].astype(F32)
    ).astype(BF16)
    far_r = send(summed_ref.at[0], got_ref.at[2], batch=right)
    hop_l.wait_recv()
    summed_ref[1] = (
        part_ref[high, rows(left), :].astype(F32) + hop_ref[1].astype(F32)
    ).astype(BF16)
    far_l = send(summed_ref.at[1], got_ref.at[3], batch=left)
    drive_ref[...] = vel_ref[...] + part_ref[:, rows(b), :].astype(F32)
    near_r.wait_recv()
    near_l.wait_recv()
    far_r.wait_recv()
    far_l.wait_recv()
    drive_ref[:half] += got_ref[1].astype(F32) + got_ref[2].astype(F32)
    drive_ref[half:] += got_ref[0].astype(F32) + got_ref[3].astype(F32)

    lane = lax.broadcasted_iota(jnp.int32, (mine, 128), 1)
    layer = lax.broadcasted_iota(jnp.int32, (mine, 128), 0) % LAYERS
    at_end, at_start = lane == 127, lane == 0
    has_next, has_previous = layer < LAYERS - 1, layer > 0
    inside = slice(8, 8 + mine)
    for sweep in range(SWEEPS):
        for x in range(planes):
            st_ref[1 + x, inside, :] = drive_ref[x] if sweep == 0 else new_ref[x]
        xs_ref[sweep, 0] = st_ref[planes, inside, :].astype(BF16)
        xs_ref[sweep, 1] = st_ref[1, inside, :].astype(BF16)
        for x in range(planes):
            y32_ref[0, x * LINE : (x + 1) * LINE] = st_ref[1 + x, 2 + mine : 8 + mine, :]
            y32_ref[1, x * LINE : (x + 1) * LINE] = st_ref[1 + x, 8 : 8 + LINE, :]
        for side in range(2):
            ys_ref[sweep, side] = y32_ref[side].astype(BF16)
        copies = [
            send(xs_ref.at[sweep, 0], xr_ref.at[sweep, 0], slab=above),
            send(xs_ref.at[sweep, 1], xr_ref.at[sweep, 1], slab=below),
            send(ys_ref.at[sweep, 0], yr_ref.at[sweep, 0], batch=right),
            send(ys_ref.at[sweep, 1], yr_ref.at[sweep, 1], batch=left),
        ]
        for copy in copies:
            copy.wait_recv()
        x_low, x_high = xr_ref[sweep, 0].astype(F32), xr_ref[sweep, 1].astype(F32)
        st_ref[0, inside, :] = jnp.where(s > 0, x_low, 0.0)
        st_ref[planes + 1, inside, :] = jnp.where(s < slabs - 1, x_high, 0.0)
        y32_ref[0] = jnp.where(b > 0, yr_ref[sweep, 0].astype(F32), 0.0)
        y32_ref[1] = jnp.where(b < batches - 1, yr_ref[sweep, 1].astype(F32), 0.0)
        for x in range(planes):
            st_ref[1 + x, 8 - LINE : 8, :] = y32_ref[0, x * LINE : (x + 1) * LINE]
            st_ref[1 + x, 8 + mine : 8 + mine + LINE, :] = y32_ref[1, x * LINE : (x + 1) * LINE]
        for x in range(planes):
            total = (
                st_ref[x, inside, :]
                + st_ref[x + 2, inside, :]
                + st_ref[x + 1, 8 - LINE : 8 - LINE + mine, :]
                + st_ref[x + 1, 8 + LINE : 8 + LINE + mine, :]
            )
            centre = st_ref[x + 1, inside, :]
            after = jnp.where(has_next, st_ref[x + 1, 9 : 9 + mine, :], 0.0)
            before = jnp.where(has_previous, st_ref[x + 1, 7 : 7 + mine, :], 0.0)
            upper = pltpu.roll(jnp.where(at_start, after, centre), 127, 1)
            lower = pltpu.roll(jnp.where(at_end, before, centre), 1, 1)
            total = total + upper + lower
            new_ref[x] = (drive_ref[x] + coupling * total) * (1.0 / (1.0 + 6.0 * coupling))

    own_ref[...] = new_ref[...].astype(BF16)
    at_right_low = send(own_ref.at[low], all_ref.at[low, rows(b)], batch=right)
    at_left_high = send(own_ref.at[high], all_ref.at[high, rows(b)], batch=left)
    at_right_high = send(own_ref.at[high], all_ref.at[high, rows(b)], batch=right)
    at_left_low = send(own_ref.at[low], all_ref.at[low, rows(b)], batch=left)
    local = pltpu.make_async_copy(own_ref, all_ref.at[:, rows(b)], local_sem)
    local.start()
    at_right_low.wait_recv()
    on_r = send(all_ref.at[low, rows(left)], all_ref.at[low, rows(left)], batch=right)
    at_left_high.wait_recv()
    on_l = send(all_ref.at[high, rows(right)], all_ref.at[high, rows(right)], batch=left)
    for copy in (at_right_high, at_left_low, on_r, on_l):
        copy.wait_recv()
    local.wait()
    for copy in started:
        copy.wait_send()


def grid_step(part, vel, collective_id):
    planes, mine, _ = vel.shape
    half = planes // 2
    copies = 6 + 4 * SWEEPS + 6
    return pl.pallas_call(
        grid_kernel,
        out_shape=(
            jax.ShapeDtypeStruct(vel.shape, F32),
            jax.ShapeDtypeStruct(part.shape, BF16),
        ),
        in_specs=[VMEM_SPEC] * 2,
        out_specs=(VMEM_SPEC, ANY_SPEC),
        scratch_shapes=[
            pltpu.VMEM((2, half, mine, 128), BF16),
            pltpu.VMEM((4, half, mine, 128), BF16),
            pltpu.VMEM((2, half, mine, 128), BF16),
            pltpu.VMEM((planes, mine, 128), F32),
            pltpu.VMEM((planes + 2, mine + 16, 128), F32),
            pltpu.VMEM((planes, mine, 128), BF16),
            pltpu.VMEM((SWEEPS, 2, mine, 128), BF16),
            pltpu.VMEM((SWEEPS, 2, mine, 128), BF16),
            pltpu.VMEM((SWEEPS, 2, planes * LINE, 128), BF16),
            pltpu.VMEM((SWEEPS, 2, planes * LINE, 128), BF16),
            pltpu.VMEM((2, planes * LINE, 128), F32),
            pltpu.SemaphoreType.DMA((copies,)),
            pltpu.SemaphoreType.DMA((copies,)),
            pltpu.SemaphoreType.DMA,
        ],
        compiler_params=pltpu.CompilerParams(collective_id=collective_id, has_side_effects=True),
        name="grid_step",
    )(part, vel)


def local(
    velocity_old, traction, offsets, owner_slab, anchor, blocks, block_count, synthesis, analysis
):
    slab_count = lax.axis_size("slab")
    owner = owner_slab.T
    sent = pack(
        owner,
        traction.transpose(1, 2, 0),
        offsets.transpose(1, 0, 2),
        anchor.T,
        blocks.T,
        block_count[None],
        slab_count,
    )
    received = exchange(sent, 0)
    part, p, tx, ty, idx = spread(received, synthesis)
    planes, lines = velocity_old.shape[:2]
    velocity = velocity_old.transpose(0, 1, 3, 2, 4).reshape(planes, lines * LINE, 128)
    velocity_new, slab_velocity = grid_step(part.reshape(planes, NY * LINE, 128), velocity, 2)
    coefs = sample(slab_velocity.reshape(ROWS, 128), p, tx, ty, idx, analysis, slab_count)
    velocity_coef = unpack(owner, exchange(coefs, 1))
    velocity_new = velocity_new.reshape(planes, lines, 3, LAYERS, 128)
    return (velocity_new.transpose(0, 1, 3, 2, 4), velocity_coef.transpose(2, 0, 1))


def solution(mesh):
    in_specs = (
        P("slab", "batch", None, None, None),
        P(("slab", "batch"), None, None),
        P(("slab", "batch"), None, None),
        P(("slab", "batch"), None),
        P(("slab", "batch"), None),
        P(("slab", "batch"), None),
        P(("slab", "batch")),
        P(),
        P(),
    )
    out_specs = (P("slab", "batch", None, None, None), P(("slab", "batch"), None, None))
    return jax.shard_map(local, mesh=mesh, in_specs=in_specs, out_specs=out_specs, check_vma=False)
```

```python
import math

import jax
import jax.numpy as jnp
from jax import lax
from jax.experimental import pallas as pl
from jax.experimental.pallas import tpu as pltpu
from jax.sharding import PartitionSpec as P

SWEEPS = 2
GX = 8
NY = 64
NZ = 256
LAYERS = NZ // 128

L = 169
Q = 338
B = 16
REM = L - 128

CAP = 6
PLANES = 13
OUT_PLANES = 4
QP = 384

LINE = 3 * LAYERS
TILES = GX * NY * LAYERS
ROWS = TILES * 3

kernel_width = 0.8
coupling = 2.0
SCALE = math.sqrt(0.5 * math.log2(math.e)) / kernel_width
LOG_NORM = -math.log2(0.8 * math.sqrt(2.0 * math.pi))

F32 = jnp.float32
BF16 = jnp.bfloat16
NT = (((1,), (1,)), ((), ()))
NN = (((1,), (0,)), ((), ()))
TN = (((0,), (0,)), ((), ()))

VMEM_SPEC = pl.BlockSpec(memory_space=pltpu.VMEM)
ANY_SPEC = pl.BlockSpec(memory_space=pl.ANY)


def dot(a, b, dims):
    return lax.dot_general(a, b, dims, preferred_element_type=F32)


GROUP = 4
LINES = CAP * B
DEAD = 255


def relative(owner, me):
    y = (owner // 16 - me // 16 + 4) % 4
    z = (owner // 2 % 8 - me // 2 % 8 + 8) % 8
    core = (owner % 2 - me % 2 + 2) % 2
    return y * 16 + z * 2 + core


def peer_of(me, step):
    y = (me // 16 + step // 16) % 4
    z = (me // 2 % 8 + step // 2 % 8) % 8
    core = (me % 2 + step % 2) % 2
    return y * 16 + z * 2 + core


def slot_onehot(owner_ref, slab_count, me):
    cells = owner_ref.shape[1]
    owner = relative(owner_ref[...], me)
    slab_at = lax.broadcasted_iota(jnp.int32, (slab_count, cells), 0)
    member = jnp.where(slab_at == owner, 1.0, 0.0)
    first = lax.broadcasted_iota(jnp.int32, (cells, cells), 0)
    second = lax.broadcasted_iota(jnp.int32, (cells, cells), 1)
    before = jnp.where(first < second, 1.0, 0.0).astype(BF16)
    rank = jnp.sum(member * dot(member.astype(BF16), before, NN), axis=0, keepdims=True)
    slot = owner * CAP + rank.astype(jnp.int32)
    at = lax.broadcasted_iota(jnp.int32, (slab_count * CAP, cells), 0)
    return jnp.where(at == slot, 1.0, 0.0).astype(BF16)


def greet_all(me, count):
    barrier = pltpu.get_barrier_semaphore()

    def greet(step, carry):
        pl.semaphore_signal(
            barrier, inc=1, device_id={"slab": peer_of(me, step)},
            device_id_type=pl.DeviceIdType.MESH,
        )
        return carry

    lax.fori_loop(1, count, greet, 0)
    return barrier


def pack_blocks(
    hot, coef_ref, offs_ref, anchor_ref, blocks_ref, count_ref, send_ref, x_ref, blk_ref, rows_ref
):
    slab_count = send_ref.shape[0]
    slots = slab_count * CAP
    rows_ref[...] = jnp.zeros_like(rows_ref)
    for k in range(3):
        x_ref[k] = dot(hot, coef_ref[k, :128, :], NT)
        rows_ref[k * REM : (k + 1) * REM] = coef_ref[k, 128:, :].astype(F32)
    x_ref[3] = dot(hot, rows_ref[...].astype(BF16), NT)
    tail = jnp.zeros((slots, QP - Q), F32)
    rows_ref[...] = jnp.zeros_like(rows_ref)
    for k in range(3):
        place = anchor_ref[k : k + 1, :]
        rows_ref[112:113] = (place % 128 if k == 2 else place).astype(F32)
        got = dot(hot, offs_ref[k], NN)
        x_ref[4 + 3 * k] = got[:, :128]
        x_ref[5 + 3 * k] = got[:, 128:256]
        x_ref[6 + 3 * k] = jnp.concatenate([got[:, 256:], tail], axis=1) + dot(
            hot, rows_ref[...].astype(BF16), NT
        )
    live = lax.broadcasted_iota(jnp.int32, blocks_ref.shape, 0) < count_ref[...]
    tile = blocks_ref[...]
    y = tile // LAYERS % NY + (tile % LAYERS) * NY
    lists = (tile // (NY * LAYERS), y)
    lane = lax.broadcasted_iota(jnp.int32, (slots, 128), 1) // B
    slot = lax.broadcasted_iota(jnp.int32, (slots, 128), 0) % CAP
    for n in range(2):
        values = jnp.where(live, lists[n], DEAD).astype(F32)
        for i in range(128 // B):
            rows_ref[i * B : (i + 1) * B] = values
        x_ref[PLANES + n] = jnp.where(lane == slot, dot(hot, rows_ref[...].astype(BF16), NT), 0.0)

    def step(target, carry):
        for r in range(PLANES):
            blk_ref[pl.ds(r * CAP, CAP), :] = x_ref[r, pl.ds(target * CAP, CAP), :]
        for n in range(2):
            blk_ref[pl.ds(PLANES * CAP + n, 1), :] = jnp.sum(
                x_ref[PLANES + n, pl.ds(target * CAP, CAP), :], axis=0, keepdims=True
            )
        send_ref[target] = blk_ref[...].astype(BF16)
        return carry

    lax.fori_loop(0, slab_count, step, 0)


def basis_planes(basis_ref, wide_ref, planes_ref):
    wide_ref[...] = jnp.zeros_like(wide_ref)
    wide_ref[:128, :Q] = basis_ref[:128, :].astype(F32)
    for k in range(3):
        if k > 0:
            wide_ref[128 + (k - 1) * REM : 128 + k * REM, :Q] = jnp.zeros((REM, Q), F32)
        wide_ref[128 + k * REM : 128 + (k + 1) * REM, :Q] = basis_ref[128:, :].astype(F32)
        planes_ref[k] = wide_ref[...].astype(BF16)


def z_weights(pz):
    step = lax.broadcasted_iota(jnp.int32, (8, QP), 0).astype(F32) * SCALE
    base = pz - step
    parts = []
    for g in range(16):
        d = base - (8.0 * g * SCALE)
        parts.append(jnp.exp2(LOG_NORM - d * d))
    return jnp.concatenate(parts, axis=0).astype(BF16)


def columns(row):
    first = lax.broadcasted_iota(jnp.int32, (128, 128), 0)
    second = lax.broadcasted_iota(jnp.int32, (128, 128), 1)
    diagonal = jnp.where(first == second, row, 0.0).astype(BF16)
    return dot(diagonal, jnp.ones((128, 128), BF16), NN)


def split_y(row):
    layer = jnp.where(row >= NY, 1.0, 0.0)
    return row - NY * layer, layer


def stencil_columns(x_row, y_row, tx_ref, ty_ref):
    for n in range(QP // 128):
        tx_ref[:, n * 128 : (n + 1) * 128] = columns(x_row) * SCALE
        ty_ref[:, n * 128 : (n + 1) * 128] = columns(split_y(y_row)[0]) * SCALE


def xy_weights(px, py, tx, ty):
    dx = px - tx
    dy = py - ty
    return jnp.exp2(2.0 * LOG_NORM - (dx * dx + dy * dy))


def spread_kernel(
    owner_ref, coef_ref, offs_ref, anchor_ref, blocks_ref, count_ref, syn_ref,
    part_ref, p_ref, lists_ref, idx_ref,
    x_ref, blk_ref, rows_ref, send_ref, recv_ref, r_ref, f_ref, tx_ref, ty_ref,
    t_ref, acc_ref, part32_ref, wide_ref, basis_ref, send_sem, recv_sem,
):
    slab_count = send_ref.shape[0]
    me = lax.axis_index("slab")
    barrier = greet_all(me, slab_count)
    hot = slot_onehot(owner_ref, slab_count, me)
    pack_blocks(
        hot, coef_ref, offs_ref, anchor_ref, blocks_ref, count_ref,
        send_ref, x_ref, blk_ref, rows_ref,
    )
    pl.semaphore_wait(barrier, slab_count - 1)

    def send(step, carry):
        pltpu.make_async_remote_copy(
            src_ref=send_ref.at[step],
            dst_ref=recv_ref.at[step],
            send_sem=send_sem,
            recv_sem=recv_sem.at[step],
            device_id={"slab": peer_of(me, step)},
            device_id_type=pl.DeviceIdType.MESH,
        ).start()
        return carry

    lax.fori_loop(1, slab_count, send, 0)
    recv_ref[0] = send_ref[0]
    basis_planes(syn_ref, wide_ref, basis_ref)
    acc_ref[...] = jnp.zeros_like(acc_ref)
    t_ref[...] = jnp.zeros_like(t_ref)

    def wait(step):
        pltpu.make_async_copy(recv_ref.at[step], recv_ref.at[step], recv_sem.at[step]).wait()

    def take(g, h, wait_for):
        step = g * GROUP + h
        if wait_for:
            wait(step)
        blk_ref[...] = recv_ref[step].astype(F32)
        for r in range(PLANES):
            r_ref[r, pl.ds(h * CAP, CAP), :] = blk_ref[r * CAP : (r + 1) * CAP, :]
        lists_ref[pl.ds(step * 2, 2), :] = blk_ref[PLANES * CAP : PLANES * CAP + 2, :]

    def work(g):
        rows = pl.ds(pl.multiple_of(g * GROUP * CAP, 8), GROUP * CAP)
        for k in range(3):
            anchor = r_ref[6 + 3 * k][:, 112:113]
            for t in range(3):
                p_ref[k, rows, t * 128 : (t + 1) * 128] = (r_ref[4 + 3 * k + t] + anchor) * SCALE
            coef = jnp.concatenate([r_ref[k], r_ref[3]], axis=1).astype(BF16)
            f_ref[k] = dot(coef, basis_ref[k], NN)

        def source(h, carry):
            step = g * GROUP + h
            x_row, y_row = lists_ref[pl.ds(step * 2, 1), :], lists_ref[pl.ds(step * 2 + 1, 1), :]
            stencil_columns(x_row, y_row, tx_ref, ty_ref)
            y, layer = split_y(y_row)
            place = jnp.where(x_row < DEAD, (x_row * NY + y) * LINE + layer, 0.0)
            idx_ref[pl.ds(step, 1), :] = place.astype(jnp.int32)
            for i in range(CAP):
                c = step * CAP + i
                lines = slice(i * B, (i + 1) * B)
                wxy = xy_weights(
                    p_ref[0, pl.ds(c, 1), :], p_ref[1, pl.ds(c, 1), :],
                    tx_ref[lines], ty_ref[lines],
                )
                weighted = jnp.concatenate(
                    [wxy * f_ref[k, pl.ds(h * CAP + i, 1), :] for k in range(3)], axis=0
                ).astype(BF16)
                terms = dot(weighted, z_weights(p_ref[2, pl.ds(c, 1), :]), NT).astype(BF16)
                at = pl.ds(pl.multiple_of(h * 128 + i * B, B), B)
                for k in range(3):
                    t_ref[at, k * 128 : (k + 1) * 128] = terms[k * B : (k + 1) * B]
            return carry

        lax.fori_loop(0, GROUP, source, 0)
        tile = lax.broadcasted_iota(jnp.int32, (NY * LAYERS, 128), 0).astype(F32)
        hits, x_rows = [], []
        for h in range(GROUP):
            step = g * GROUP + h
            x_rows.append(lists_ref[pl.ds(step * 2, 1), :])
            hits.append(jnp.where(tile == lists_ref[pl.ds(step * 2 + 1, 1), :], 1.0, 0.0).astype(BF16))
        for x in range(GX):
            picked = jnp.concatenate(
                [
                    hit * jnp.where(x_row == float(x), 1.0, 0.0).astype(BF16)
                    for hit, x_row in zip(hits, x_rows)
                ],
                axis=1,
            )
            acc_ref[x] += dot(picked, t_ref[...], NN)

    for h in range(GROUP):
        take(0, h, h > 0)
    work(0)

    def group(g, carry):
        for h in range(GROUP):
            take(g, h, True)
        work(g)
        return carry

    lax.fori_loop(1, slab_count // GROUP, group, 0)
    for x in range(GX):
        for layer in range(LAYERS):
            for k in range(3):
                part32_ref[pl.ds(x * NY * LINE + k * LAYERS + layer, NY, stride=LINE), :] = acc_ref[
                    x, layer * NY : (layer + 1) * NY, k * 128 : (k + 1) * 128
                ]
    part_ref[...] = part32_ref[...].astype(BF16)
    others = pl.ds(1, slab_count - 1)
    pltpu.make_async_copy(send_ref.at[others], send_ref.at[others], send_sem).wait()


def spread(owner, coef, offs, anchor, blocks, count, syn, slab_count, collective_id):
    block_rows = PLANES * CAP + 2
    slots = slab_count * CAP
    held = GROUP * CAP
    return pl.pallas_call(
        spread_kernel,
        out_shape=(
            jax.ShapeDtypeStruct((ROWS, 128), BF16),
            jax.ShapeDtypeStruct((3, slots, QP), F32),
            jax.ShapeDtypeStruct((2 * slab_count, 128), F32),
            jax.ShapeDtypeStruct((slab_count, 128), jnp.int32),
        ),
        in_specs=[VMEM_SPEC] * 7,
        out_specs=(VMEM_SPEC,) * 4,
        scratch_shapes=[
            pltpu.VMEM((PLANES + 2, slots, 128), F32),
            pltpu.VMEM((block_rows, 128), F32),
            pltpu.VMEM((128, owner.shape[1]), F32),
            pltpu.VMEM((slab_count, block_rows, 128), BF16),
            pltpu.VMEM((slab_count, block_rows, 128), BF16),
            pltpu.VMEM((PLANES, held, 128), F32),
            pltpu.VMEM((3, held, QP), F32),
            pltpu.VMEM((128, QP), F32),
            pltpu.VMEM((128, QP), F32),
            pltpu.VMEM((GROUP * 128, QP), BF16),
            pltpu.VMEM((GX, NY * LAYERS, QP), F32),
            pltpu.VMEM((ROWS, 128), F32),
            pltpu.VMEM((256, QP), F32),
            pltpu.VMEM((3, 256, QP), BF16),
            pltpu.SemaphoreType.DMA,
            pltpu.SemaphoreType.DMA((slab_count,)),
        ],
        compiler_params=pltpu.CompilerParams(collective_id=collective_id, has_side_effects=True),
        name="spread",
    )(owner, coef, offs, anchor, blocks, count, syn)


def sample_kernel(
    owner_ref, vel_ref, p_ref, lists_ref, idx_smem, ana_ref, out_ref,
    v_ref, g_ref, pv_ref, c_ref, blk_ref, tx_ref, ty_ref, send_ref, back_ref, r_ref,
    wide_ref, basis_ref, send_sem, recv_sem,
):
    slab_count = send_ref.shape[0]
    me = lax.axis_index("slab")
    barrier = greet_all(me, slab_count)
    v_ref[...] = vel_ref[...].astype(F32)
    basis_planes(ana_ref, wide_ref, basis_ref)

    def work(g):
        def source(h, carry):
            step = g * GROUP + h
            for i in range(CAP):
                for j in range(B):
                    start = idx_smem[step, i * B + j]
                    g_ref[i, pl.ds(j, 3, stride=B), :] = v_ref[pl.ds(start, 3, stride=LAYERS), :]
            x_row, y_row = lists_ref[pl.ds(step * 2, 1), :], lists_ref[pl.ds(step * 2 + 1, 1), :]
            stencil_columns(x_row, y_row, tx_ref, ty_ref)
            for i in range(CAP):
                c = step * CAP + i
                lines = slice(i * B, (i + 1) * B)
                wxy = xy_weights(
                    p_ref[0, pl.ds(c, 1), :], p_ref[1, pl.ds(c, 1), :],
                    tx_ref[lines], ty_ref[lines],
                )
                wz = z_weights(p_ref[2, pl.ds(c, 1), :])
                projected = dot(g_ref[i].astype(BF16), wz, NN)
                for k in range(3):
                    pv_ref[k, pl.ds(h * CAP + i, 1), :] = jnp.sum(
                        projected[k * B : (k + 1) * B] * wxy, axis=0, keepdims=True
                    )
            return carry

        lax.fori_loop(0, GROUP, source, 0)
        rem = jnp.zeros((GROUP * CAP, 128), F32)
        for k in range(3):
            got = dot(pv_ref[k].astype(BF16), basis_ref[k], NT)
            c_ref[k] = got[:, :128]
            rem = rem + got[:, 128:]
        c_ref[3] = rem
        for h in range(GROUP):
            for r in range(OUT_PLANES):
                blk_ref[r * CAP : (r + 1) * CAP, :] = c_ref[r, h * CAP : (h + 1) * CAP, :]
            send_ref[g * GROUP + h] = blk_ref[...].astype(BF16)

    def send(step):
        pltpu.make_async_remote_copy(
            src_ref=send_ref.at[step],
            dst_ref=back_ref.at[step],
            send_sem=send_sem,
            recv_sem=recv_sem,
            device_id={"slab": peer_of(me, relative(0, step))},
            device_id_type=pl.DeviceIdType.MESH,
        ).start()

    groups = slab_count // GROUP
    work(groups - 1)
    pl.semaphore_wait(barrier, slab_count - 1)

    def group(n, carry):
        g = groups - 2 - n
        for h in range(GROUP):
            send((g + 1) * GROUP + h)
        work(g)
        return carry

    lax.fori_loop(0, groups - 1, group, 0)
    for h in range(1, GROUP):
        send(h)
    back_ref[0] = send_ref[0]
    hot = slot_onehot(owner_ref, slab_count, me)
    others = pl.ds(1, slab_count - 1)
    pltpu.make_async_copy(back_ref.at[others], back_ref.at[others], recv_sem).wait()

    def take(step, carry):
        blk_ref[...] = back_ref[step].astype(F32)
        for r in range(OUT_PLANES):
            r_ref[r, pl.ds(step * CAP, CAP), :] = blk_ref[r * CAP : (r + 1) * CAP, :]
        return carry

    lax.fori_loop(0, slab_count, take, 0)
    rem = dot(r_ref[3].astype(BF16), hot, TN)
    for k in range(3):
        main = dot(r_ref[k].astype(BF16), hot, TN)
        out_ref[k] = jnp.concatenate([main, rem[k * REM : (k + 1) * REM]], axis=0).astype(BF16)
    pltpu.make_async_copy(send_ref.at[others], send_ref.at[others], send_sem).wait()


def sample(owner, vel, p, lists, idx, ana, slab_count, collective_id):
    slots = slab_count * CAP
    block_rows = OUT_PLANES * CAP
    held = GROUP * CAP
    return pl.pallas_call(
        sample_kernel,
        out_shape=jax.ShapeDtypeStruct((3, L, owner.shape[1]), BF16),
        in_specs=[VMEM_SPEC] * 4 + [pl.BlockSpec(memory_space=pltpu.SMEM), VMEM_SPEC],
        out_specs=VMEM_SPEC,
        scratch_shapes=[
            pltpu.VMEM((ROWS, 128), F32),
            pltpu.VMEM((CAP, 3 * B, 128), F32),
            pltpu.VMEM((3, held, QP), F32),
            pltpu.VMEM((OUT_PLANES, held, 128), F32),
            pltpu.VMEM((block_rows, 128), F32),
            pltpu.VMEM((128, QP), F32),
            pltpu.VMEM((128, QP), F32),
            pltpu.VMEM((slab_count, block_rows, 128), BF16),
            pltpu.VMEM((slab_count, block_rows, 128), BF16),
            pltpu.VMEM((OUT_PLANES, slots, 128), F32),
            pltpu.VMEM((256, QP), F32),
            pltpu.VMEM((3, 256, QP), BF16),
            pltpu.SemaphoreType.DMA,
            pltpu.SemaphoreType.DMA,
        ],
        compiler_params=pltpu.CompilerParams(collective_id=collective_id, has_side_effects=True),
        name="sample",
    )(owner, vel, p, lists, idx, ana)


def grid_kernel(
    part_ref, vel_ref, new_ref, all_ref,
    hop_ref, got_ref, summed_ref, drive_ref, st_ref, own_ref,
    xs_ref, xr_ref, ys_ref, yr_ref, y32_ref, send_sem, recv_sem, local_sem,
):
    planes, mine, _ = vel_ref.shape
    half = planes // 2
    batches, slabs = lax.axis_size("batch"), lax.axis_size("slab")
    b, s = lax.axis_index("batch"), lax.axis_index("slab")
    right, far, left = [lax.rem(b + i, batches) for i in (1, 2, 3)]
    above, below = lax.rem(s + 1, slabs), lax.rem(s + slabs - 1, slabs)

    barrier = pltpu.get_barrier_semaphore()
    for device in ({"batch": right}, {"batch": left}, {"slab": above}, {"slab": below}):
        pl.semaphore_signal(
            barrier, inc=1, device_id=device, device_id_type=pl.DeviceIdType.MESH
        )
    pl.semaphore_wait(barrier, 4)

    def rows(part):
        return pl.ds(pl.multiple_of(part * mine, mine), mine)

    started = []

    def send(src, dst, **device):
        n = len(started)
        copy = pltpu.make_async_remote_copy(
            src_ref=src, dst_ref=dst, send_sem=send_sem.at[n], recv_sem=recv_sem.at[n],
            device_id=device, device_id_type=pl.DeviceIdType.MESH,
        )
        copy.start()
        started.append(copy)
        return copy

    low, high = pl.ds(0, half), pl.ds(half, half)

    hop_r = send(part_ref.at[low, rows(far)], hop_ref.at[0], batch=right)
    hop_l = send(part_ref.at[high, rows(far)], hop_ref.at[1], batch=left)
    near_r = send(part_ref.at[high, rows(right)], got_ref.at[0], batch=right)
    near_l = send(part_ref.at[low, rows(left)], got_ref.at[1], batch=left)
    hop_r.wait_recv()
    summed_ref[0] = (
        part_ref[low, rows(right), :].astype(F32) + hop_ref[0].astype(F32)
    ).astype(BF16)
    far_r = send(summed_ref.at[0], got_ref.at[2], batch=right)
    hop_l.wait_recv()
    summed_ref[1] = (
        part_ref[high, rows(left), :].astype(F32) + hop_ref[1].astype(F32)
    ).astype(BF16)
    far_l = send(summed_ref.at[1], got_ref.at[3], batch=left)
    drive_ref[...] = vel_ref[...] + part_ref[:, rows(b), :].astype(F32)
    near_r.wait_recv()
    near_l.wait_recv()
    far_r.wait_recv()
    far_l.wait_recv()
    drive_ref[:half] += got_ref[1].astype(F32) + got_ref[2].astype(F32)
    drive_ref[half:] += got_ref[0].astype(F32) + got_ref[3].astype(F32)

    lane = lax.broadcasted_iota(jnp.int32, (mine, 128), 1)
    layer = lax.broadcasted_iota(jnp.int32, (mine, 128), 0) % LAYERS
    at_end, at_start = lane == 127, lane == 0
    has_next, has_previous = layer < LAYERS - 1, layer > 0
    inside = slice(8, 8 + mine)
    for sweep in range(SWEEPS):
        for x in range(planes):
            st_ref[1 + x, inside, :] = drive_ref[x] if sweep == 0 else new_ref[x]
        xs_ref[sweep, 0] = st_ref[planes, inside, :].astype(BF16)
        xs_ref[sweep, 1] = st_ref[1, inside, :].astype(BF16)
        for x in range(planes):
            y32_ref[0, x * LINE : (x + 1) * LINE] = st_ref[1 + x, 2 + mine : 8 + mine, :]
            y32_ref[1, x * LINE : (x + 1) * LINE] = st_ref[1 + x, 8 : 8 + LINE, :]
        for side in range(2):
            ys_ref[sweep, side] = y32_ref[side].astype(BF16)
        copies = [
            send(xs_ref.at[sweep, 0], xr_ref.at[sweep, 0], slab=above),
            send(xs_ref.at[sweep, 1], xr_ref.at[sweep, 1], slab=below),
            send(ys_ref.at[sweep, 0], yr_ref.at[sweep, 0], batch=right),
            send(ys_ref.at[sweep, 1], yr_ref.at[sweep, 1], batch=left),
        ]
        for copy in copies:
            copy.wait_recv()
        x_low, x_high = xr_ref[sweep, 0].astype(F32), xr_ref[sweep, 1].astype(F32)
        st_ref[0, inside, :] = jnp.where(s > 0, x_low, 0.0)
        st_ref[planes + 1, inside, :] = jnp.where(s < slabs - 1, x_high, 0.0)
        y32_ref[0] = jnp.where(b > 0, yr_ref[sweep, 0].astype(F32), 0.0)
        y32_ref[1] = jnp.where(b < batches - 1, yr_ref[sweep, 1].astype(F32), 0.0)
        for x in range(planes):
            st_ref[1 + x, 8 - LINE : 8, :] = y32_ref[0, x * LINE : (x + 1) * LINE]
            st_ref[1 + x, 8 + mine : 8 + mine + LINE, :] = y32_ref[1, x * LINE : (x + 1) * LINE]
        for x in range(planes):
            total = (
                st_ref[x, inside, :]
                + st_ref[x + 2, inside, :]
                + st_ref[x + 1, 8 - LINE : 8 - LINE + mine, :]
                + st_ref[x + 1, 8 + LINE : 8 + LINE + mine, :]
            )
            centre = st_ref[x + 1, inside, :]
            after = jnp.where(has_next, st_ref[x + 1, 9 : 9 + mine, :], 0.0)
            before = jnp.where(has_previous, st_ref[x + 1, 7 : 7 + mine, :], 0.0)
            upper = pltpu.roll(jnp.where(at_start, after, centre), 127, 1)
            lower = pltpu.roll(jnp.where(at_end, before, centre), 1, 1)
            total = total + upper + lower
            new_ref[x] = (drive_ref[x] + coupling * total) * (1.0 / (1.0 + 6.0 * coupling))

    own_ref[...] = new_ref[...].astype(BF16)
    at_right_low = send(own_ref.at[low], all_ref.at[low, rows(b)], batch=right)
    at_left_high = send(own_ref.at[high], all_ref.at[high, rows(b)], batch=left)
    at_right_high = send(own_ref.at[high], all_ref.at[high, rows(b)], batch=right)
    at_left_low = send(own_ref.at[low], all_ref.at[low, rows(b)], batch=left)
    local = pltpu.make_async_copy(own_ref, all_ref.at[:, rows(b)], local_sem)
    local.start()
    at_right_low.wait_recv()
    on_r = send(all_ref.at[low, rows(left)], all_ref.at[low, rows(left)], batch=right)
    at_left_high.wait_recv()
    on_l = send(all_ref.at[high, rows(right)], all_ref.at[high, rows(right)], batch=left)
    for copy in (at_right_high, at_left_low, on_r, on_l):
        copy.wait_recv()
    local.wait()
    for copy in started:
        copy.wait_send()


def grid_step(part, vel, collective_id):
    planes, mine, _ = vel.shape
    half = planes // 2
    copies = 6 + 4 * SWEEPS + 6
    return pl.pallas_call(
        grid_kernel,
        out_shape=(
            jax.ShapeDtypeStruct(vel.shape, F32),
            jax.ShapeDtypeStruct(part.shape, BF16),
        ),
        in_specs=[VMEM_SPEC] * 2,
        out_specs=(VMEM_SPEC, ANY_SPEC),
        scratch_shapes=[
            pltpu.VMEM((2, half, mine, 128), BF16),
            pltpu.VMEM((4, half, mine, 128), BF16),
            pltpu.VMEM((2, half, mine, 128), BF16),
            pltpu.VMEM((planes, mine, 128), F32),
            pltpu.VMEM((planes + 2, mine + 16, 128), F32),
            pltpu.VMEM((planes, mine, 128), BF16),
            pltpu.VMEM((SWEEPS, 2, mine, 128), BF16),
            pltpu.VMEM((SWEEPS, 2, mine, 128), BF16),
            pltpu.VMEM((SWEEPS, 2, planes * LINE, 128), BF16),
            pltpu.VMEM((SWEEPS, 2, planes * LINE, 128), BF16),
            pltpu.VMEM((2, planes * LINE, 128), F32),
            pltpu.SemaphoreType.DMA((copies,)),
            pltpu.SemaphoreType.DMA((copies,)),
            pltpu.SemaphoreType.DMA,
        ],
        compiler_params=pltpu.CompilerParams(collective_id=collective_id, has_side_effects=True),
        name="grid_step",
    )(part, vel)


def local(
    velocity_old, traction, offsets, owner_slab, anchor, blocks, block_count, synthesis, analysis
):
    slab_count = lax.axis_size("slab")
    owner = owner_slab.T
    part, p, lists, idx = spread(
        owner,
        traction.transpose(1, 2, 0),
        offsets.transpose(1, 0, 2),
        anchor.T,
        blocks.T,
        block_count[None],
        synthesis,
        slab_count,
        0,
    )
    planes, lines = velocity_old.shape[:2]
    velocity = velocity_old.transpose(0, 1, 3, 2, 4).reshape(planes, lines * LINE, 128)
    velocity_new, slab_velocity = grid_step(part.reshape(planes, NY * LINE, 128), velocity, 2)
    velocity_coef = sample(
        owner, slab_velocity.reshape(ROWS, 128), p, lists, idx, analysis, slab_count, 1
    )
    velocity_new = velocity_new.reshape(planes, lines, 3, LAYERS, 128)
    return (velocity_new.transpose(0, 1, 3, 2, 4), velocity_coef.transpose(2, 0, 1))


def solution(mesh):
    in_specs = (
        P("slab", "batch", None, None, None),
        P(("slab", "batch"), None, None),
        P(("slab", "batch"), None, None),
        P(("slab", "batch"), None),
        P(("slab", "batch"), None),
        P(("slab", "batch"), None),
        P(("slab", "batch")),
        P(),
        P(),
    )
    out_specs = (P("slab", "batch", None, None, None), P(("slab", "batch"), None, None))
    return jax.shard_map(local, mesh=mesh, in_specs=in_specs, out_specs=out_specs, check_vma=False)
```

```python
import math

import jax
import jax.numpy as jnp
from jax import lax
from jax.experimental import pallas as pl
from jax.experimental.pallas import tpu as pltpu
from jax.sharding import PartitionSpec as P

SWEEPS = 2
GX = 8
NY = 64
NZ = 256
LAYERS = NZ // 128

L = 169
Q = 338
B = 16
REM = L - 128

CAP = 6
PLANES = 13
OUT_PLANES = 4
QP = 384

LINE = 3 * LAYERS
TILES = GX * NY * LAYERS
ROWS = TILES * 3

kernel_width = 0.8
coupling = 2.0
SCALE = math.sqrt(0.5 * math.log2(math.e)) / kernel_width
LOG_NORM = -math.log2(0.8 * math.sqrt(2.0 * math.pi))

F32 = jnp.float32
BF16 = jnp.bfloat16
NT = (((1,), (1,)), ((), ()))
NN = (((1,), (0,)), ((), ()))
TN = (((0,), (0,)), ((), ()))

VMEM_SPEC = pl.BlockSpec(memory_space=pltpu.VMEM)


def dot(a, b, dims):
    return lax.dot_general(a, b, dims, preferred_element_type=F32)


GROUP = 4
LINES = CAP * B
DEAD = 255


def relative(owner, me):
    y = (owner // 16 - me // 16 + 4) % 4
    z = (owner // 2 % 8 - me // 2 % 8 + 8) % 8
    core = (owner % 2 - me % 2 + 2) % 2
    return y * 16 + z * 2 + core


def peer_of(me, step):
    y = (me // 16 + step // 16) % 4
    z = (me // 2 % 8 + step // 2 % 8) % 8
    core = (me % 2 + step % 2) % 2
    return y * 16 + z * 2 + core


def slot_onehot(owner_ref, slab_count, me):
    cells = owner_ref.shape[1]
    owner = relative(owner_ref[...], me)
    slab_at = lax.broadcasted_iota(jnp.int32, (slab_count, cells), 0)
    member = jnp.where(slab_at == owner, 1.0, 0.0)
    first = lax.broadcasted_iota(jnp.int32, (cells, cells), 0)
    second = lax.broadcasted_iota(jnp.int32, (cells, cells), 1)
    before = jnp.where(first < second, 1.0, 0.0).astype(BF16)
    rank = jnp.sum(member * dot(member.astype(BF16), before, NN), axis=0, keepdims=True)
    slot = owner * CAP + rank.astype(jnp.int32)
    at = lax.broadcasted_iota(jnp.int32, (slab_count * CAP, cells), 0)
    return jnp.where(at == slot, 1.0, 0.0).astype(BF16)


def greet_all(me, count):
    barrier = pltpu.get_barrier_semaphore()

    def greet(step, carry):
        pl.semaphore_signal(
            barrier, inc=1, device_id={"slab": peer_of(me, step)},
            device_id_type=pl.DeviceIdType.MESH,
        )
        return carry

    lax.fori_loop(1, count, greet, 0)
    return barrier


def pack_blocks(
    hot, coef_ref, offs_ref, anchor_ref, blocks_ref, count_ref, send_ref, x_ref, blk_ref, rows_ref
):
    slab_count = send_ref.shape[0]
    slots = slab_count * CAP
    rows_ref[...] = jnp.zeros_like(rows_ref)
    for k in range(3):
        x_ref[k] = dot(hot, coef_ref[k, :128, :], NT)
        rows_ref[k * REM : (k + 1) * REM] = coef_ref[k, 128:, :].astype(F32)
    x_ref[3] = dot(hot, rows_ref[...].astype(BF16), NT)
    tail = jnp.zeros((slots, QP - Q), F32)
    rows_ref[...] = jnp.zeros_like(rows_ref)
    for k in range(3):
        place = anchor_ref[k : k + 1, :]
        rows_ref[112:113] = (place % 128 if k == 2 else place).astype(F32)
        got = dot(hot, offs_ref[k], NN)
        x_ref[4 + 3 * k] = got[:, :128]
        x_ref[5 + 3 * k] = got[:, 128:256]
        x_ref[6 + 3 * k] = jnp.concatenate([got[:, 256:], tail], axis=1) + dot(
            hot, rows_ref[...].astype(BF16), NT
        )
    live = lax.broadcasted_iota(jnp.int32, blocks_ref.shape, 0) < count_ref[...]
    tile = blocks_ref[...]
    y = tile // LAYERS % NY + (tile % LAYERS) * NY
    lists = (tile // (NY * LAYERS), y)
    lane = lax.broadcasted_iota(jnp.int32, (slots, 128), 1) // B
    slot = lax.broadcasted_iota(jnp.int32, (slots, 128), 0) % CAP
    for n in range(2):
        values = jnp.where(live, lists[n], DEAD).astype(F32)
        for i in range(128 // B):
            rows_ref[i * B : (i + 1) * B] = values
        x_ref[PLANES + n] = jnp.where(lane == slot, dot(hot, rows_ref[...].astype(BF16), NT), 0.0)

    def step(target, carry):
        for r in range(PLANES):
            blk_ref[pl.ds(r * CAP, CAP), :] = x_ref[r, pl.ds(target * CAP, CAP), :]
        for n in range(2):
            blk_ref[pl.ds(PLANES * CAP + n, 1), :] = jnp.sum(
                x_ref[PLANES + n, pl.ds(target * CAP, CAP), :], axis=0, keepdims=True
            )
        send_ref[target] = blk_ref[...].astype(BF16)
        return carry

    lax.fori_loop(0, slab_count, step, 0)


def basis_planes(basis_ref, wide_ref, planes_ref):
    wide_ref[...] = jnp.zeros_like(wide_ref)
    wide_ref[:128, :Q] = basis_ref[:128, :].astype(F32)
    for k in range(3):
        if k > 0:
            wide_ref[128 + (k - 1) * REM : 128 + k * REM, :Q] = jnp.zeros((REM, Q), F32)
        wide_ref[128 + k * REM : 128 + (k + 1) * REM, :Q] = basis_ref[128:, :].astype(F32)
        planes_ref[k] = wide_ref[...].astype(BF16)


def z_weights(pz):
    step = lax.broadcasted_iota(jnp.int32, (8, QP), 0).astype(F32) * SCALE
    base = pz - step
    parts = []
    for g in range(16):
        d = base - (8.0 * g * SCALE)
        parts.append(jnp.exp2(LOG_NORM - d * d))
    return jnp.concatenate(parts, axis=0).astype(BF16)


def columns(row):
    first = lax.broadcasted_iota(jnp.int32, (128, 128), 0)
    second = lax.broadcasted_iota(jnp.int32, (128, 128), 1)
    diagonal = jnp.where(first == second, row, 0.0).astype(BF16)
    return dot(diagonal, jnp.ones((128, 128), BF16), NN)


def split_y(row):
    layer = jnp.where(row >= NY, 1.0, 0.0)
    return row - NY * layer, layer


def xy_weights(px, py, tx, ty):
    parts = []
    for n in range(QP // 128):
        lanes = slice(n * 128, (n + 1) * 128)
        dx = px[:, lanes] - tx
        dy = py[:, lanes] - ty
        parts.append(jnp.exp2(2.0 * LOG_NORM - (dx * dx + dy * dy)))
    return jnp.concatenate(parts, axis=1)


def spread_cells(
    me, syn_ref, send_ref, recv_ref, send_sem, recv_sem, part_ref, wz_ref, wxy_ref, idx_ref,
    blk_ref, r_ref, p_ref, f_ref, lists_ref, tx_ref, ty_ref,
    t_ref, t_old_ref, hit_ref, x_old_ref, acc_ref, part32_ref, wide_ref, basis_ref,
):
    slab_count = send_ref.shape[0]

    def send(step, carry):
        pltpu.make_async_remote_copy(
            src_ref=send_ref.at[step],
            dst_ref=recv_ref.at[step],
            send_sem=send_sem,
            recv_sem=recv_sem.at[step],
            device_id={"slab": peer_of(me, step)},
            device_id_type=pl.DeviceIdType.MESH,
        ).start()
        return carry

    lax.fori_loop(1, slab_count, send, 0)
    pltpu.make_async_copy(send_ref.at[0], recv_ref.at[0], recv_sem.at[0]).start()
    basis_planes(syn_ref, wide_ref, basis_ref)
    for ref in (acc_ref, t_ref, t_old_ref, hit_ref, x_old_ref):
        ref[...] = jnp.zeros_like(ref)

    per_source = GX // GROUP

    def group(g, carry):
        for h in range(GROUP):
            step = g * GROUP + h
            pltpu.make_async_copy(recv_ref.at[step], recv_ref.at[step], recv_sem.at[step]).wait()
            blk_ref[...] = recv_ref[step].astype(F32)
            for r in range(PLANES):
                r_ref[r, h * CAP : (h + 1) * CAP, :] = blk_ref[r * CAP : (r + 1) * CAP, :]
            lists_ref[h] = blk_ref[PLANES * CAP : PLANES * CAP + 2, :]
        for k in range(3):
            anchor = r_ref[6 + 3 * k][:, 112:113]
            for t in range(3):
                p_ref[k, :, t * 128 : (t + 1) * 128] = (r_ref[4 + 3 * k + t] + anchor) * SCALE
            coef = jnp.concatenate([r_ref[k], r_ref[3]], axis=1).astype(BF16)
            f_ref[k] = dot(coef, basis_ref[k], NN)

        def source(h, carry):
            step = g * GROUP + h
            x_row, y_row = lists_ref[h, 0:1, :], lists_ref[h, 1:2, :]
            y, layer = split_y(y_row)
            place = jnp.where(x_row < DEAD, (x_row * NY + y) * LINE + layer, 0.0)
            idx_ref[pl.ds(step, 1), :] = jnp.clip(place.astype(jnp.int32), 0, ROWS - LINE + LAYERS - 1)
            tx_ref[...] = columns(x_row) * SCALE
            ty_ref[...] = columns(y) * SCALE
            for d in range(per_source):
                x = h * per_source + d
                mask = jnp.where(x_old_ref[...] == x.astype(F32), 1.0, 0.0).astype(BF16)
                acc_ref[x] += dot(hit_ref[...] * mask, t_old_ref[...], NN)
            for i in range(CAP):
                c = step * CAP + i
                here = pl.ds(h * CAP + i, 1)
                lines = slice(i * B, (i + 1) * B)
                wxy = xy_weights(
                    p_ref[0, here, :], p_ref[1, here, :], tx_ref[lines], ty_ref[lines]
                )
                wxy_ref[c] = wxy
                weighted = jnp.concatenate(
                    [wxy * f_ref[k, here, :] for k in range(3)], axis=0
                ).astype(BF16)
                wz = z_weights(p_ref[2, here, :])
                wz_ref[c] = wz
                terms = dot(weighted, wz, NT).astype(BF16)
                at = pl.ds(pl.multiple_of(h * 128 + i * B, B), B)
                for k in range(3):
                    t_ref[at, k * 128 : (k + 1) * 128] = terms[k * B : (k + 1) * B]
            return carry

        lax.fori_loop(0, GROUP, source, 0)
        t_old_ref[...] = t_ref[...]
        tile = lax.broadcasted_iota(jnp.int32, (NY * LAYERS, 128), 0).astype(F32)
        for h in range(GROUP):
            lanes = slice(h * 128, (h + 1) * 128)
            x_old_ref[:, lanes] = lists_ref[h, 0:1, :]
            hit_ref[:, lanes] = jnp.where(tile == lists_ref[h, 1:2, :], 1.0, 0.0).astype(BF16)
        return carry

    lax.fori_loop(0, slab_count // GROUP, group, 0)
    for x in range(GX):
        mask = jnp.where(x_old_ref[...] == float(x), 1.0, 0.0).astype(BF16)
        acc_ref[x] += dot(hit_ref[...] * mask, t_old_ref[...], NN)
    for x in range(GX):
        for layer in range(LAYERS):
            for k in range(3):
                part32_ref[pl.ds(x * NY * LINE + k * LAYERS + layer, NY, stride=LINE), :] = acc_ref[
                    x, layer * NY : (layer + 1) * NY, k * 128 : (k + 1) * 128
                ]
    for x in range(GX):
        part_ref[x] = part32_ref[x * NY * LINE : (x + 1) * NY * LINE, :].astype(BF16)
    others = pl.ds(1, slab_count - 1)
    pltpu.make_async_copy(send_ref.at[others], send_ref.at[others], send_sem).wait()


def sample_cells(
    me, hot, all_ref, ana_ref, out_ref, wz_ref, wxy_ref, idx_smem,
    v_ref, g_ref, pv_ref, c_ref, blk_ref, send_ref, back_ref, r_ref,
    wide_ref, basis_ref, send_sem, recv_sem,
):
    slab_count = send_ref.shape[0]
    for x in range(GX):
        v_ref[x * NY * LINE : (x + 1) * NY * LINE, :] = all_ref[x].astype(F32)

    def work(g):
        def source(h, carry):
            step = g * GROUP + h
            for i in range(CAP):
                for j in range(B):
                    start = idx_smem[step, i * B + j]
                    g_ref[i, pl.ds(j, 3, stride=B), :] = v_ref[pl.ds(start, 3, stride=LAYERS), :]
            for i in range(CAP):
                c = step * CAP + i
                projected = dot(g_ref[i].astype(BF16), wz_ref[c], NN)
                wxy = wxy_ref[c]
                for k in range(3):
                    pv_ref[k, pl.ds(h * CAP + i, 1), :] = jnp.sum(
                        projected[k * B : (k + 1) * B] * wxy, axis=0, keepdims=True
                    )
            return carry

        lax.fori_loop(0, GROUP, source, 0)
        rem = jnp.zeros((GROUP * CAP, 128), F32)
        for k in range(3):
            got = dot(pv_ref[k].astype(BF16), basis_ref[k], NT)
            c_ref[k] = got[:, :128]
            rem = rem + got[:, 128:]
        c_ref[3] = rem
        for h in range(GROUP):
            for r in range(OUT_PLANES):
                blk_ref[r * CAP : (r + 1) * CAP, :] = c_ref[r, h * CAP : (h + 1) * CAP, :]
            send_ref[g * GROUP + h] = blk_ref[: OUT_PLANES * CAP, :].astype(BF16)

    def send(step):
        pltpu.make_async_remote_copy(
            src_ref=send_ref.at[step],
            dst_ref=back_ref.at[step],
            send_sem=send_sem,
            recv_sem=recv_sem,
            device_id={"slab": peer_of(me, relative(0, step))},
            device_id_type=pl.DeviceIdType.MESH,
        ).start()

    groups = slab_count // GROUP
    work(groups - 1)

    def group(n, carry):
        g = groups - 2 - n
        for h in range(GROUP):
            send((g + 1) * GROUP + h)
        work(g)
        return carry

    lax.fori_loop(0, groups - 1, group, 0)
    for h in range(1, GROUP):
        send(h)
    back_ref[0] = send_ref[0]
    others = pl.ds(1, slab_count - 1)
    pltpu.make_async_copy(back_ref.at[others], back_ref.at[others], recv_sem).wait()

    def take(step, carry):
        blk_ref[: OUT_PLANES * CAP, :] = back_ref[step].astype(F32)
        for r in range(OUT_PLANES):
            r_ref[r, pl.ds(step * CAP, CAP), :] = blk_ref[r * CAP : (r + 1) * CAP, :]
        return carry

    lax.fori_loop(0, slab_count, take, 0)
    rem = dot(r_ref[3].astype(BF16), hot, TN)
    for k in range(3):
        main = dot(r_ref[k].astype(BF16), hot, TN)
        out_ref[k] = jnp.concatenate([main, rem[k * REM : (k + 1) * REM]], axis=0).astype(BF16)
    pltpu.make_async_copy(send_ref.at[others], send_ref.at[others], send_sem).wait()


def batch_neighbours():
    batches, b = lax.axis_size("batch"), lax.axis_index("batch")
    return [lax.rem(b + i, batches) for i in range(1, batches)]


def grid_steps(
    part_ref, vel_ref, new_ref, all_ref,
    hop_ref, got_ref, summed_ref, drive_ref, st_ref, own_ref,
    xs_ref, xr_ref, ys_ref, yr_ref, y32_ref, send_sem, recv_sem, local_sem,
):
    planes, mine, _ = vel_ref.shape
    half = planes // 2
    batches, slabs = lax.axis_size("batch"), lax.axis_size("slab")
    b, s = lax.axis_index("batch"), lax.axis_index("slab")
    right, far, left = batch_neighbours()
    above, below = lax.rem(s + 1, slabs), lax.rem(s + slabs - 1, slabs)

    def rows(part):
        return pl.ds(pl.multiple_of(part * mine, mine), mine)

    started = []

    def send(src, dst, **device):
        n = len(started)
        copy = pltpu.make_async_remote_copy(
            src_ref=src, dst_ref=dst, send_sem=send_sem.at[n], recv_sem=recv_sem.at[n],
            device_id=device, device_id_type=pl.DeviceIdType.MESH,
        )
        copy.start()
        started.append(copy)
        return copy

    low, high = pl.ds(0, half), pl.ds(half, half)

    hop_r = send(part_ref.at[low, rows(far)], hop_ref.at[0], batch=right)
    hop_l = send(part_ref.at[high, rows(far)], hop_ref.at[1], batch=left)
    near_r = send(part_ref.at[high, rows(right)], got_ref.at[0], batch=right)
    near_l = send(part_ref.at[low, rows(left)], got_ref.at[1], batch=left)
    hop_r.wait_recv()
    summed_ref[0] = (
        part_ref[low, rows(right), :].astype(F32) + hop_ref[0].astype(F32)
    ).astype(BF16)
    far_r = send(summed_ref.at[0], got_ref.at[2], batch=right)
    hop_l.wait_recv()
    summed_ref[1] = (
        part_ref[high, rows(left), :].astype(F32) + hop_ref[1].astype(F32)
    ).astype(BF16)
    far_l = send(summed_ref.at[1], got_ref.at[3], batch=left)
    drive_ref[...] = vel_ref[...] + part_ref[:, rows(b), :].astype(F32)
    near_r.wait_recv()
    near_l.wait_recv()
    far_r.wait_recv()
    far_l.wait_recv()
    drive_ref[:half] += got_ref[1].astype(F32) + got_ref[2].astype(F32)
    drive_ref[half:] += got_ref[0].astype(F32) + got_ref[3].astype(F32)

    lane = lax.broadcasted_iota(jnp.int32, (mine, 128), 1)
    layer = lax.broadcasted_iota(jnp.int32, (mine, 128), 0) % LAYERS
    at_end, at_start = lane == 127, lane == 0
    has_next, has_previous = layer < LAYERS - 1, layer > 0
    inside = slice(8, 8 + mine)
    for sweep in range(SWEEPS):
        for x in range(planes):
            st_ref[1 + x, inside, :] = drive_ref[x] if sweep == 0 else new_ref[x]
        xs_ref[sweep, 0] = st_ref[planes, inside, :].astype(BF16)
        xs_ref[sweep, 1] = st_ref[1, inside, :].astype(BF16)
        for x in range(planes):
            y32_ref[0, x * LINE : (x + 1) * LINE] = st_ref[1 + x, 2 + mine : 8 + mine, :]
            y32_ref[1, x * LINE : (x + 1) * LINE] = st_ref[1 + x, 8 : 8 + LINE, :]
        for side in range(2):
            ys_ref[sweep, side] = y32_ref[side].astype(BF16)
        copies = [
            send(xs_ref.at[sweep, 0], xr_ref.at[sweep, 0], slab=above),
            send(xs_ref.at[sweep, 1], xr_ref.at[sweep, 1], slab=below),
            send(ys_ref.at[sweep, 0], yr_ref.at[sweep, 0], batch=right),
            send(ys_ref.at[sweep, 1], yr_ref.at[sweep, 1], batch=left),
        ]
        for copy in copies:
            copy.wait_recv()
        x_low, x_high = xr_ref[sweep, 0].astype(F32), xr_ref[sweep, 1].astype(F32)
        st_ref[0, inside, :] = jnp.where(s > 0, x_low, 0.0)
        st_ref[planes + 1, inside, :] = jnp.where(s < slabs - 1, x_high, 0.0)
        y32_ref[0] = jnp.where(b > 0, yr_ref[sweep, 0].astype(F32), 0.0)
        y32_ref[1] = jnp.where(b < batches - 1, yr_ref[sweep, 1].astype(F32), 0.0)
        for x in range(planes):
            st_ref[1 + x, 8 - LINE : 8, :] = y32_ref[0, x * LINE : (x + 1) * LINE]
            st_ref[1 + x, 8 + mine : 8 + mine + LINE, :] = y32_ref[1, x * LINE : (x + 1) * LINE]
        for x in range(planes):
            total = (
                st_ref[x, inside, :]
                + st_ref[x + 2, inside, :]
                + st_ref[x + 1, 8 - LINE : 8 - LINE + mine, :]
                + st_ref[x + 1, 8 + LINE : 8 + LINE + mine, :]
            )
            centre = st_ref[x + 1, inside, :]
            after = jnp.where(has_next, st_ref[x + 1, 9 : 9 + mine, :], 0.0)
            before = jnp.where(has_previous, st_ref[x + 1, 7 : 7 + mine, :], 0.0)
            upper = pltpu.roll(jnp.where(at_start, after, centre), 127, 1)
            lower = pltpu.roll(jnp.where(at_end, before, centre), 1, 1)
            total = total + upper + lower
            new_ref[x] = (drive_ref[x] + coupling * total) * (1.0 / (1.0 + 6.0 * coupling))

    own_ref[...] = new_ref[...].astype(BF16)
    at_right_low = send(own_ref.at[low], all_ref.at[low, rows(b)], batch=right)
    at_left_high = send(own_ref.at[high], all_ref.at[high, rows(b)], batch=left)
    at_right_high = send(own_ref.at[high], all_ref.at[high, rows(b)], batch=right)
    at_left_low = send(own_ref.at[low], all_ref.at[low, rows(b)], batch=left)
    local = pltpu.make_async_copy(own_ref, all_ref.at[:, rows(b)], local_sem)
    local.start()
    at_right_low.wait_recv()
    on_r = send(all_ref.at[low, rows(left)], all_ref.at[low, rows(left)], batch=right)
    at_left_high.wait_recv()
    on_l = send(all_ref.at[high, rows(right)], all_ref.at[high, rows(right)], batch=left)
    for copy in (at_right_high, at_left_low, on_r, on_l):
        copy.wait_recv()
    local.wait()
    for copy in started:
        copy.wait_send()


def step_kernel(
    owner_ref, coef_ref, offs_ref, anchor_ref, blocks_ref, count_ref, syn_ref, ana_ref, vel_ref,
    new_ref, out_ref,
    x_ref, blk_ref, rows_ref, hot_ref, send_ref, recv_ref, send_sem, recv_sem,
    part_ref, wz_ref, wxy_ref, idx_ref, idx_smem,
    r_ref, p_ref, f_ref, lists_ref, tx_ref, ty_ref, t_ref, t_old_ref, hit_ref, x_old_ref,
    acc_ref, part32_ref, wide_ref, basis_ref,
    all_ref, hop_ref, got_ref, summed_ref, drive_ref, st_ref, own_ref,
    xs_ref, xr_ref, ys_ref, yr_ref, y32_ref, grid_send_sem, grid_recv_sem, local_sem,
    g_ref, pv_ref, c_ref, coef_send_ref, back_ref, back_send_sem, back_recv_sem,
):
    slab_count = send_ref.shape[0]
    me = lax.axis_index("slab")
    barrier = greet_all(me, slab_count)
    right, _, left = batch_neighbours()
    for device in ({"batch": right}, {"batch": left}):
        pl.semaphore_signal(
            barrier, inc=1, device_id=device, device_id_type=pl.DeviceIdType.MESH
        )
    hot_ref[...] = slot_onehot(owner_ref, slab_count, me)
    pack_blocks(
        hot_ref[...], coef_ref, offs_ref, anchor_ref, blocks_ref, count_ref,
        send_ref, x_ref, blk_ref, rows_ref,
    )
    pl.semaphore_wait(barrier, slab_count + 1)
    spread_cells(
        me, syn_ref, send_ref, recv_ref, send_sem, recv_sem, part_ref, wz_ref, wxy_ref, idx_ref,
        blk_ref, r_ref, p_ref, f_ref, lists_ref, tx_ref, ty_ref,
        t_ref, t_old_ref, hit_ref, x_old_ref, acc_ref, part32_ref, wide_ref, basis_ref,
    )
    pltpu.sync_copy(idx_ref, idx_smem)
    basis_planes(ana_ref, wide_ref, basis_ref)
    grid_steps(
        part_ref, vel_ref, new_ref, all_ref,
        hop_ref, got_ref, summed_ref, drive_ref, st_ref, own_ref,
        xs_ref, xr_ref, ys_ref, yr_ref, y32_ref, grid_send_sem, grid_recv_sem, local_sem,
    )
    sample_cells(
        me, hot_ref[...], all_ref, ana_ref, out_ref, wz_ref, wxy_ref, idx_smem,
        part32_ref, g_ref, pv_ref, c_ref, blk_ref, coef_send_ref, back_ref, x_ref,
        wide_ref, basis_ref, back_send_sem, back_recv_sem,
    )


def whole_step(owner, coef, offs, anchor, blocks, count, syn, ana, vel, slab_count):
    planes, mine, _ = vel.shape
    half = planes // 2
    copies = 6 + 4 * SWEEPS + 6
    cells = owner.shape[1]
    slots = slab_count * CAP
    held = GROUP * CAP
    block_rows = PLANES * CAP + 2
    back_rows = OUT_PLANES * CAP
    dma = pltpu.SemaphoreType.DMA
    return pl.pallas_call(
        step_kernel,
        out_shape=(
            jax.ShapeDtypeStruct(vel.shape, F32),
            jax.ShapeDtypeStruct((3, L, cells), BF16),
        ),
        in_specs=[VMEM_SPEC] * 9,
        out_specs=(VMEM_SPEC, VMEM_SPEC),
        scratch_shapes=[
            pltpu.VMEM((PLANES + 2, slots, 128), F32),
            pltpu.VMEM((block_rows, 128), F32),
            pltpu.VMEM((128, cells), F32),
            pltpu.VMEM((slots, cells), BF16),
            pltpu.VMEM((slab_count, block_rows, 128), BF16),
            pltpu.VMEM((slab_count, block_rows, 128), BF16),
            dma,
            dma((slab_count,)),
            pltpu.VMEM((planes, NY * LINE, 128), BF16),
            pltpu.VMEM((slots, 128, QP), BF16),
            pltpu.VMEM((slots, B, QP), F32),
            pltpu.VMEM((slab_count, 128), jnp.int32),
            pltpu.SMEM((slab_count, 128), jnp.int32),
            pltpu.VMEM((PLANES, held, 128), F32),
            pltpu.VMEM((3, held, QP), F32),
            pltpu.VMEM((3, held, QP), F32),
            pltpu.VMEM((GROUP, 2, 128), F32),
            pltpu.VMEM((128, 128), F32),
            pltpu.VMEM((128, 128), F32),
            pltpu.VMEM((GROUP * 128, QP), BF16),
            pltpu.VMEM((GROUP * 128, QP), BF16),
            pltpu.VMEM((NY * LAYERS, GROUP * 128), BF16),
            pltpu.VMEM((1, GROUP * 128), F32),
            pltpu.VMEM((GX, NY * LAYERS, QP), F32),
            pltpu.VMEM((ROWS, 128), F32),
            pltpu.VMEM((256, QP), F32),
            pltpu.VMEM((3, 256, QP), BF16),
            pltpu.VMEM((planes, NY * LINE, 128), BF16),
            pltpu.VMEM((2, half, mine, 128), BF16),
            pltpu.VMEM((4, half, mine, 128), BF16),
            pltpu.VMEM((2, half, mine, 128), BF16),
            pltpu.VMEM((planes, mine, 128), F32),
            pltpu.VMEM((planes + 2, mine + 16, 128), F32),
            pltpu.VMEM((planes, mine, 128), BF16),
            pltpu.VMEM((SWEEPS, 2, mine, 128), BF16),
            pltpu.VMEM((SWEEPS, 2, mine, 128), BF16),
            pltpu.VMEM((SWEEPS, 2, planes * LINE, 128), BF16),
            pltpu.VMEM((SWEEPS, 2, planes * LINE, 128), BF16),
            pltpu.VMEM((2, planes * LINE, 128), F32),
            dma((copies,)),
            dma((copies,)),
            dma,
            pltpu.VMEM((CAP, 3 * B, 128), F32),
            pltpu.VMEM((3, held, QP), F32),
            pltpu.VMEM((OUT_PLANES, held, 128), F32),
            pltpu.VMEM((slab_count, back_rows, 128), BF16),
            pltpu.VMEM((slab_count, back_rows, 128), BF16),
            dma,
            dma,
        ],
        compiler_params=pltpu.CompilerParams(
            collective_id=0, has_side_effects=True, vmem_limit_bytes=67_043_328
        ),
        name="whole_step",
    )(owner, coef, offs, anchor, blocks, count, syn, ana, vel)


def local(
    velocity_old, traction, offsets, owner_slab, anchor, blocks, block_count, synthesis, analysis
):
    slab_count = lax.axis_size("slab")
    owner = owner_slab.T
    planes, lines = velocity_old.shape[:2]
    velocity_new, velocity_coef = whole_step(
        owner,
        traction.transpose(1, 2, 0),
        offsets.transpose(1, 0, 2),
        anchor.T,
        blocks.T,
        block_count[None],
        synthesis,
        analysis,
        velocity_old.transpose(0, 1, 3, 2, 4).reshape(planes, lines * LINE, 128),
        slab_count,
    )
    velocity_new = velocity_new.reshape(planes, lines, 3, LAYERS, 128)
    return (velocity_new.transpose(0, 1, 3, 2, 4), velocity_coef.transpose(2, 0, 1))


def solution(mesh):
    in_specs = (
        P("slab", "batch", None, None, None),
        P(("slab", "batch"), None, None),
        P(("slab", "batch"), None, None),
        P(("slab", "batch"), None),
        P(("slab", "batch"), None),
        P(("slab", "batch"), None),
        P(("slab", "batch")),
        P(),
        P(),
    )
    out_specs = (P("slab", "batch", None, None, None), P(("slab", "batch"), None, None))
    return jax.shard_map(local, mesh=mesh, in_specs=in_specs, out_specs=out_specs, check_vma=False)
```

```python
import math

import jax
import jax.numpy as jnp
from jax import lax
from jax.experimental import pallas as pl
from jax.experimental.pallas import tpu as pltpu
from jax.sharding import PartitionSpec as P

SWEEPS = 2
GX = 8
NY = 64
NZ = 256
LAYERS = NZ // 128

L = 169
Q = 338
B = 16
REM = L - 128

CAP = 6
PLANES = 13
OUT_PLANES = 4
QP = 384

LINE = 3 * LAYERS
TILES = GX * NY * LAYERS
ROWS = TILES * 3

kernel_width = 0.8
coupling = 2.0
SCALE = math.sqrt(0.5 * math.log2(math.e)) / kernel_width
LOG_NORM = -math.log2(0.8 * math.sqrt(2.0 * math.pi))

F32 = jnp.float32
BF16 = jnp.bfloat16
NT = (((1,), (1,)), ((), ()))
NN = (((1,), (0,)), ((), ()))
TN = (((0,), (0,)), ((), ()))

VMEM_SPEC = pl.BlockSpec(memory_space=pltpu.VMEM)


def dot(a, b, dims):
    return lax.dot_general(a, b, dims, preferred_element_type=F32)


GROUP = 4
LINES = CAP * B
DEAD = 255


def relative(owner, me):
    y = (owner // 16 - me // 16 + 4) % 4
    z = (owner // 2 % 8 - me // 2 % 8 + 8) % 8
    core = (owner % 2 - me % 2 + 2) % 2
    return y * 16 + z * 2 + core


def wrap(value, size):
    value = jnp.where(value >= size, value - size, value)
    return jnp.where(value < 0, value + size, value)


def each_peer(me, sign, count, visit):
    my_y, my_z, my_core = me // 16, me // 2 % 8, me % 2
    for dy in range(count // 16):
        for core in range(2):
            base = wrap(my_y + sign * dy, count // 16) * 16 + wrap(my_core + sign * core, 2)

            def along(dz, carry, dy=dy, core=core, base=base):
                visit(dy * 16 + dz * 2 + core, base + 2 * wrap(my_z + sign * dz, 8))
                return carry

            lax.fori_loop(1 if dy == core == 0 else 0, 8, along, 0)


def slot_onehot(owner_ref, slab_count, me):
    cells = owner_ref.shape[1]
    owner = relative(owner_ref[...], me)
    slab_at = lax.broadcasted_iota(jnp.int32, (slab_count, cells), 0)
    member = jnp.where(slab_at == owner, 1.0, 0.0)
    first = lax.broadcasted_iota(jnp.int32, (cells, cells), 0)
    second = lax.broadcasted_iota(jnp.int32, (cells, cells), 1)
    before = jnp.where(first < second, 1.0, 0.0).astype(BF16)
    rank = jnp.sum(member * dot(member.astype(BF16), before, NN), axis=0, keepdims=True)
    slot = owner * CAP + rank.astype(jnp.int32)
    at = lax.broadcasted_iota(jnp.int32, (slab_count * CAP, cells), 0)
    return jnp.where(at == slot, 1.0, 0.0).astype(BF16)


def greet_all(me, count):
    barrier = pltpu.get_barrier_semaphore()

    def greet(step, carry):
        pl.semaphore_signal(
            barrier, inc=1, device_id={"slab": wrap(me + step, count)},
            device_id_type=pl.DeviceIdType.MESH,
        )
        return carry

    lax.fori_loop(1, count, greet, 0)
    return barrier


def pack_blocks(
    hot, coef_ref, offs_ref, anchor_ref, blocks_ref, count_ref, send_ref, x_ref, blk_ref, rows_ref
):
    slab_count = send_ref.shape[0]
    slots = slab_count * CAP
    rows_ref[...] = jnp.zeros_like(rows_ref)
    for k in range(3):
        x_ref[k] = dot(hot, coef_ref[k, :128, :], NT)
        rows_ref[k * REM : (k + 1) * REM] = coef_ref[k, 128:, :].astype(F32)
    x_ref[3] = dot(hot, rows_ref[...].astype(BF16), NT)
    tail = jnp.zeros((slots, QP - Q), F32)
    rows_ref[...] = jnp.zeros_like(rows_ref)
    for k in range(3):
        place = anchor_ref[k : k + 1, :]
        rows_ref[112:113] = (place % 128 if k == 2 else place).astype(F32)
        got = dot(hot, offs_ref[k], NN)
        x_ref[4 + 3 * k] = got[:, :128]
        x_ref[5 + 3 * k] = got[:, 128:256]
        x_ref[6 + 3 * k] = jnp.concatenate([got[:, 256:], tail], axis=1) + dot(
            hot, rows_ref[...].astype(BF16), NT
        )
    live = lax.broadcasted_iota(jnp.int32, blocks_ref.shape, 0) < count_ref[...]
    tile = blocks_ref[...]
    y = tile // LAYERS % NY + (tile % LAYERS) * NY
    lists = (tile // (NY * LAYERS), y)
    lane = lax.broadcasted_iota(jnp.int32, (slots, 128), 1) // B
    slot = lax.broadcasted_iota(jnp.int32, (slots, 128), 0) % CAP
    for n in range(2):
        values = jnp.where(live, lists[n], DEAD).astype(F32)
        for i in range(128 // B):
            rows_ref[i * B : (i + 1) * B] = values
        x_ref[PLANES + n] = jnp.where(lane == slot, dot(hot, rows_ref[...].astype(BF16), NT), 0.0)

    def step(target, carry):
        for r in range(PLANES):
            blk_ref[pl.ds(r * CAP, CAP), :] = x_ref[r, pl.ds(target * CAP, CAP), :]
        for n in range(2):
            blk_ref[pl.ds(PLANES * CAP + n, 1), :] = jnp.sum(
                x_ref[PLANES + n, pl.ds(target * CAP, CAP), :], axis=0, keepdims=True
            )
        send_ref[target] = blk_ref[...].astype(BF16)
        return carry

    lax.fori_loop(0, slab_count, step, 0)


def basis_planes(basis_ref, wide_ref, planes_ref):
    wide_ref[...] = jnp.zeros_like(wide_ref)
    wide_ref[:128, :Q] = basis_ref[:128, :].astype(F32)
    for k in range(3):
        if k > 0:
            wide_ref[128 + (k - 1) * REM : 128 + k * REM, :Q] = jnp.zeros((REM, Q), F32)
        wide_ref[128 + k * REM : 128 + (k + 1) * REM, :Q] = basis_ref[128:, :].astype(F32)
        planes_ref[k] = wide_ref[...].astype(BF16)


def z_weights(pz):
    stride = 8.0 * SCALE
    step = lax.broadcasted_iota(jnp.int32, (8, QP), 0).astype(F32) * SCALE
    d = pz - step - 8.0 * stride
    middle = LOG_NORM - d * d
    twice = d * (2.0 * stride)
    powers = {8: middle}
    for sign, last in ((1, 15), (-1, 0)):
        value, change = middle, sign * twice - stride * stride
        for g in range(8 + sign, last + sign, sign):
            value = value + change
            change = change - 2.0 * stride * stride
            powers[g] = value
    return jnp.concatenate([jnp.exp2(powers[g]) for g in range(16)], axis=0).astype(BF16)


def columns(row):
    first = lax.broadcasted_iota(jnp.int32, (128, 128), 0)
    second = lax.broadcasted_iota(jnp.int32, (128, 128), 1)
    diagonal = jnp.where(first == second, row, 0.0).astype(BF16)
    return dot(diagonal, jnp.ones((128, 128), BF16), NN)


def split_y(row):
    layer = jnp.where(row >= NY, 1.0, 0.0)
    return row - NY * layer, layer


def xy_weights(px, py, tx, ty):
    parts = []
    for n in range(QP // 128):
        lanes = slice(n * 128, (n + 1) * 128)
        dx = px[:, lanes] - tx
        dy = py[:, lanes] - ty
        parts.append(jnp.exp2(2.0 * LOG_NORM - (dx * dx + dy * dy)))
    return jnp.concatenate(parts, axis=1)


def spread_cells(
    me, syn_ref, send_ref, recv_ref, send_sem, recv_sem, part_ref, wz_ref, wxy_ref, idx_ref,
    blk_ref, r_ref, p_ref, f_ref, lists_ref, next_ref, tx_ref, ty_ref,
    t_ref, t_old_ref, hit_ref, x_old_ref, acc_ref, part32_ref, wide_ref, basis_ref,
):
    slab_count = send_ref.shape[0]

    def send(step, peer):
        pltpu.make_async_remote_copy(
            src_ref=send_ref.at[step],
            dst_ref=recv_ref.at[step],
            send_sem=send_sem,
            recv_sem=recv_sem.at[step],
            device_id={"slab": peer},
            device_id_type=pl.DeviceIdType.MESH,
        ).start()

    each_peer(me, 1, slab_count, send)
    pltpu.make_async_copy(send_ref.at[0], recv_ref.at[0], recv_sem.at[0]).start()
    basis_planes(syn_ref, wide_ref, basis_ref)
    for ref in (acc_ref, t_ref, t_old_ref, hit_ref, x_old_ref):
        ref[...] = jnp.zeros_like(ref)

    per_source = GX // GROUP

    def take(step, h):
        pltpu.make_async_copy(recv_ref.at[step], recv_ref.at[step], recv_sem.at[step]).wait()
        blk_ref[...] = recv_ref[step].astype(F32)
        for r in range(PLANES):
            r_ref[r, pl.ds(h * CAP, CAP), :] = blk_ref[r * CAP : (r + 1) * CAP, :]
        next_ref[h] = blk_ref[PLANES * CAP : PLANES * CAP + 2, :]

    def group(g, take_next):
        lists_ref[...] = next_ref[...]
        for k in range(3):
            anchor = r_ref[6 + 3 * k][:, 112:113]
            for t in range(3):
                p_ref[k, :, t * 128 : (t + 1) * 128] = (r_ref[4 + 3 * k + t] + anchor) * SCALE
            coef = jnp.concatenate([r_ref[k], r_ref[3]], axis=1).astype(BF16)
            f_ref[k] = dot(coef, basis_ref[k], NN)

        def source(h, carry):
            step = g * GROUP + h
            if take_next:
                take(step + GROUP, h)
            x_row, y_row = lists_ref[h, 0:1, :], lists_ref[h, 1:2, :]
            y, layer = split_y(y_row)
            place = jnp.where(x_row < DEAD, (x_row * NY + y) * LINE + layer, 0.0)
            idx_ref[pl.ds(step, 1), :] = jnp.clip(place.astype(jnp.int32), 0, ROWS - LINE + LAYERS - 1)
            tx_ref[...] = columns(x_row) * SCALE
            ty_ref[...] = columns(y) * SCALE
            for d in range(per_source):
                x = h * per_source + d
                mask = jnp.where(x_old_ref[...] == x.astype(F32), 1.0, 0.0).astype(BF16)
                acc_ref[x] += dot(hit_ref[...] * mask, t_old_ref[...], NN)
            for i in range(CAP):
                c = step * CAP + i
                here = pl.ds(h * CAP + i, 1)
                lines = slice(i * B, (i + 1) * B)
                wxy = xy_weights(
                    p_ref[0, here, :], p_ref[1, here, :], tx_ref[lines], ty_ref[lines]
                )
                wxy_ref[c] = wxy
                weighted = jnp.concatenate(
                    [wxy * f_ref[k, here, :] for k in range(3)], axis=0
                ).astype(BF16)
                wz = z_weights(p_ref[2, here, :])
                wz_ref[c] = wz
                terms = dot(weighted, wz, NT).astype(BF16)
                at = pl.ds(pl.multiple_of(h * 128 + i * B, B), B)
                for k in range(3):
                    t_ref[at, k * 128 : (k + 1) * 128] = terms[k * B : (k + 1) * B]
            return carry

        lax.fori_loop(0, GROUP, source, 0)
        t_old_ref[...] = t_ref[...]
        tile = lax.broadcasted_iota(jnp.int32, (NY * LAYERS, 128), 0).astype(F32)
        for h in range(GROUP):
            lanes = slice(h * 128, (h + 1) * 128)
            x_old_ref[:, lanes] = lists_ref[h, 0:1, :]
            hit_ref[:, lanes] = jnp.where(tile == lists_ref[h, 1:2, :], 1.0, 0.0).astype(BF16)

    for h in range(GROUP):
        take(h, h)

    def all_but_last(g, carry):
        group(g, True)
        return carry

    lax.fori_loop(0, slab_count // GROUP - 1, all_but_last, 0)
    group(slab_count // GROUP - 1, False)
    for x in range(GX):
        mask = jnp.where(x_old_ref[...] == float(x), 1.0, 0.0).astype(BF16)
        acc_ref[x] += dot(hit_ref[...] * mask, t_old_ref[...], NN)
    for x in range(GX):
        for layer in range(LAYERS):
            for k in range(3):
                part32_ref[pl.ds(x * NY * LINE + k * LAYERS + layer, NY, stride=LINE), :] = acc_ref[
                    x, layer * NY : (layer + 1) * NY, k * 128 : (k + 1) * 128
                ]
    for x in range(GX):
        part_ref[x] = part32_ref[x * NY * LINE : (x + 1) * NY * LINE, :].astype(BF16)
    others = pl.ds(1, slab_count - 1)
    pltpu.make_async_copy(send_ref.at[others], send_ref.at[others], send_sem).wait()


def sample_cells(
    me, hot, all_ref, ana_ref, out_ref, wz_ref, wxy_ref, idx_smem,
    v_ref, even_ref, odd_ref, pv_ref, c_ref, blk_ref, send_ref, back_ref, r_ref,
    wide_ref, basis_ref, send_sem, recv_sem,
):
    slab_count = send_ref.shape[0]
    for x in range(GX):
        v_ref[x * NY * LINE : (x + 1) * NY * LINE, :] = all_ref[x].astype(F32)

    def gather(step, to_ref):
        for i in range(CAP):
            for j in range(B):
                start = idx_smem[step, i * B + j]
                to_ref[i, pl.ds(j, 3, stride=B), :] = v_ref[pl.ds(start, 3, stride=LAYERS), :]

    def project(step, h, from_ref):
        for i in range(CAP):
            c = step * CAP + i
            projected = dot(from_ref[i].astype(BF16), wz_ref[c], NN)
            wxy = wxy_ref[c]
            for k in range(3):
                pv_ref[k, pl.ds(h * CAP + i, 1), :] = jnp.sum(
                    projected[k * B : (k + 1) * B] * wxy, axis=0, keepdims=True
                )

    def work(g):
        def pair(n, carry):
            step = g * GROUP + 2 * n
            later = jnp.where(n < GROUP // 2 - 1, step + 2, (g - 1) * GROUP)
            gather(step + 1, odd_ref)
            project(step, 2 * n, even_ref)
            gather(jnp.where(later < 0, 0, later), even_ref)
            project(step + 1, 2 * n + 1, odd_ref)
            return carry

        lax.fori_loop(0, GROUP // 2, pair, 0)
        rem = jnp.zeros((GROUP * CAP, 128), F32)
        for k in range(3):
            got = dot(pv_ref[k].astype(BF16), basis_ref[k], NT)
            c_ref[k] = got[:, :128]
            rem = rem + got[:, 128:]
        c_ref[3] = rem
        for h in range(GROUP):
            for r in range(OUT_PLANES):
                blk_ref[r * CAP : (r + 1) * CAP, :] = c_ref[r, h * CAP : (h + 1) * CAP, :]
            send_ref[g * GROUP + h] = blk_ref[: OUT_PLANES * CAP, :].astype(BF16)

    my_y, my_z, my_core = me // 16, me // 2 % 8, me % 2

    def send(g, first=0):
        dy = g // (16 // GROUP)
        base = wrap(my_y - dy, slab_count // 16) * 16
        for h in range(first, GROUP):
            dz = (g - dy * (16 // GROUP)) * (GROUP // 2) + h // 2
            place = base + 2 * wrap(my_z - dz, 8) + wrap(my_core - h % 2, 2)
            pltpu.make_async_remote_copy(
                src_ref=send_ref.at[g * GROUP + h],
                dst_ref=back_ref.at[g * GROUP + h],
                send_sem=send_sem,
                recv_sem=recv_sem,
                device_id={"slab": place},
                device_id_type=pl.DeviceIdType.MESH,
            ).start()

    groups = slab_count // GROUP
    gather((groups - 1) * GROUP, even_ref)
    work(groups - 1)

    def group(n, carry):
        g = groups - 2 - n
        send(g + 1)
        work(g)
        return carry

    lax.fori_loop(0, groups - 1, group, 0)
    send(0, 1)
    back_ref[0] = send_ref[0]
    others = pl.ds(1, slab_count - 1)
    pltpu.make_async_copy(back_ref.at[others], back_ref.at[others], recv_sem).wait()

    def take(step, carry):
        blk_ref[: OUT_PLANES * CAP, :] = back_ref[step].astype(F32)
        for r in range(OUT_PLANES):
            r_ref[r, pl.ds(step * CAP, CAP), :] = blk_ref[r * CAP : (r + 1) * CAP, :]
        return carry

    lax.fori_loop(0, slab_count, take, 0)
    rem = dot(r_ref[3].astype(BF16), hot, TN)
    for k in range(3):
        main = dot(r_ref[k].astype(BF16), hot, TN)
        out_ref[k] = jnp.concatenate([main, rem[k * REM : (k + 1) * REM]], axis=0).astype(BF16)
    pltpu.make_async_copy(send_ref.at[others], send_ref.at[others], send_sem).wait()


def batch_neighbours():
    batches, b = lax.axis_size("batch"), lax.axis_index("batch")
    return [lax.rem(b + i, batches) for i in range(1, batches)]


def grid_steps(
    part_ref, vel_ref, new_ref, all_ref,
    hop_ref, got_ref, summed_ref, drive_ref, st_ref, own_ref,
    xs_ref, xr_ref, ys_ref, yr_ref, y32_ref, send_sem, recv_sem, local_sem,
):
    planes, mine, _ = vel_ref.shape
    half = planes // 2
    batches, slabs = lax.axis_size("batch"), lax.axis_size("slab")
    b, s = lax.axis_index("batch"), lax.axis_index("slab")
    right, far, left = batch_neighbours()
    above, below = lax.rem(s + 1, slabs), lax.rem(s + slabs - 1, slabs)

    def rows(part):
        return pl.ds(pl.multiple_of(part * mine, mine), mine)

    started = []

    def send(src, dst, **device):
        n = len(started)
        copy = pltpu.make_async_remote_copy(
            src_ref=src, dst_ref=dst, send_sem=send_sem.at[n], recv_sem=recv_sem.at[n],
            device_id=device, device_id_type=pl.DeviceIdType.MESH,
        )
        copy.start()
        started.append(copy)
        return copy

    low, high = pl.ds(0, half), pl.ds(half, half)

    hop_r = send(part_ref.at[low, rows(far)], hop_ref.at[0], batch=right)
    hop_l = send(part_ref.at[high, rows(far)], hop_ref.at[1], batch=left)
    near_r = send(part_ref.at[high, rows(right)], got_ref.at[0], batch=right)
    near_l = send(part_ref.at[low, rows(left)], got_ref.at[1], batch=left)
    hop_r.wait_recv()
    summed_ref[0] = (
        part_ref[low, rows(right), :].astype(F32) + hop_ref[0].astype(F32)
    ).astype(BF16)
    far_r = send(summed_ref.at[0], got_ref.at[2], batch=right)
    hop_l.wait_recv()
    summed_ref[1] = (
        part_ref[high, rows(left), :].astype(F32) + hop_ref[1].astype(F32)
    ).astype(BF16)
    far_l = send(summed_ref.at[1], got_ref.at[3], batch=left)
    drive_ref[...] = vel_ref[...] + part_ref[:, rows(b), :].astype(F32)
    near_r.wait_recv()
    near_l.wait_recv()
    far_r.wait_recv()
    far_l.wait_recv()
    drive_ref[:half] += got_ref[1].astype(F32) + got_ref[2].astype(F32)
    drive_ref[half:] += got_ref[0].astype(F32) + got_ref[3].astype(F32)

    lane = lax.broadcasted_iota(jnp.int32, (mine, 128), 1)
    layer = lax.broadcasted_iota(jnp.int32, (mine, 128), 0) % LAYERS
    at_end, at_start = lane == 127, lane == 0
    has_next, has_previous = layer < LAYERS - 1, layer > 0
    inside = slice(8, 8 + mine)
    for sweep in range(SWEEPS):
        for x in range(planes):
            st_ref[1 + x, inside, :] = drive_ref[x] if sweep == 0 else new_ref[x]
        xs_ref[sweep, 0] = st_ref[planes, inside, :].astype(BF16)
        xs_ref[sweep, 1] = st_ref[1, inside, :].astype(BF16)
        for x in range(planes):
            y32_ref[0, x * LINE : (x + 1) * LINE] = st_ref[1 + x, 2 + mine : 8 + mine, :]
            y32_ref[1, x * LINE : (x + 1) * LINE] = st_ref[1 + x, 8 : 8 + LINE, :]
        for side in range(2):
            ys_ref[sweep, side] = y32_ref[side].astype(BF16)
        copies = [
            send(xs_ref.at[sweep, 0], xr_ref.at[sweep, 0], slab=above),
            send(xs_ref.at[sweep, 1], xr_ref.at[sweep, 1], slab=below),
            send(ys_ref.at[sweep, 0], yr_ref.at[sweep, 0], batch=right),
            send(ys_ref.at[sweep, 1], yr_ref.at[sweep, 1], batch=left),
        ]
        for copy in copies:
            copy.wait_recv()
        x_low, x_high = xr_ref[sweep, 0].astype(F32), xr_ref[sweep, 1].astype(F32)
        st_ref[0, inside, :] = jnp.where(s > 0, x_low, 0.0)
        st_ref[planes + 1, inside, :] = jnp.where(s < slabs - 1, x_high, 0.0)
        y32_ref[0] = jnp.where(b > 0, yr_ref[sweep, 0].astype(F32), 0.0)
        y32_ref[1] = jnp.where(b < batches - 1, yr_ref[sweep, 1].astype(F32), 0.0)
        for x in range(planes):
            st_ref[1 + x, 8 - LINE : 8, :] = y32_ref[0, x * LINE : (x + 1) * LINE]
            st_ref[1 + x, 8 + mine : 8 + mine + LINE, :] = y32_ref[1, x * LINE : (x + 1) * LINE]
        for x in range(planes):
            total = (
                st_ref[x, inside, :]
                + st_ref[x + 2, inside, :]
                + st_ref[x + 1, 8 - LINE : 8 - LINE + mine, :]
                + st_ref[x + 1, 8 + LINE : 8 + LINE + mine, :]
            )
            centre = st_ref[x + 1, inside, :]
            after = jnp.where(has_next, st_ref[x + 1, 9 : 9 + mine, :], 0.0)
            before = jnp.where(has_previous, st_ref[x + 1, 7 : 7 + mine, :], 0.0)
            upper = pltpu.roll(jnp.where(at_start, after, centre), 127, 1)
            lower = pltpu.roll(jnp.where(at_end, before, centre), 1, 1)
            total = total + upper + lower
            new_ref[x] = (drive_ref[x] + coupling * total) * (1.0 / (1.0 + 6.0 * coupling))

    own_ref[...] = new_ref[...].astype(BF16)
    at_right_low = send(own_ref.at[low], all_ref.at[low, rows(b)], batch=right)
    at_left_high = send(own_ref.at[high], all_ref.at[high, rows(b)], batch=left)
    at_right_high = send(own_ref.at[high], all_ref.at[high, rows(b)], batch=right)
    at_left_low = send(own_ref.at[low], all_ref.at[low, rows(b)], batch=left)
    local = pltpu.make_async_copy(own_ref, all_ref.at[:, rows(b)], local_sem)
    local.start()
    at_right_low.wait_recv()
    on_r = send(all_ref.at[low, rows(left)], all_ref.at[low, rows(left)], batch=right)
    at_left_high.wait_recv()
    on_l = send(all_ref.at[high, rows(right)], all_ref.at[high, rows(right)], batch=left)
    for copy in (at_right_high, at_left_low, on_r, on_l):
        copy.wait_recv()
    local.wait()
    for copy in started:
        copy.wait_send()


def step_kernel(
    owner_ref, coef_ref, offs_ref, anchor_ref, blocks_ref, count_ref, syn_ref, ana_ref, vel_ref,
    new_ref, out_ref,
    x_ref, blk_ref, rows_ref, hot_ref, send_ref, recv_ref, send_sem, recv_sem,
    part_ref, wz_ref, wxy_ref, idx_ref, idx_smem,
    r_ref, p_ref, f_ref, lists_ref, next_ref, tx_ref, ty_ref, t_ref, t_old_ref, hit_ref, x_old_ref,
    acc_ref, part32_ref, wide_ref, basis_ref,
    all_ref, hop_ref, got_ref, summed_ref, drive_ref, st_ref, own_ref,
    xs_ref, xr_ref, ys_ref, yr_ref, y32_ref, grid_send_sem, grid_recv_sem, local_sem,
    even_ref, odd_ref, pv_ref, c_ref, coef_send_ref, back_ref, back_send_sem, back_recv_sem,
):
    slab_count = send_ref.shape[0]
    me = lax.axis_index("slab")
    barrier = greet_all(me, slab_count)
    right, _, left = batch_neighbours()
    for device in ({"batch": right}, {"batch": left}):
        pl.semaphore_signal(
            barrier, inc=1, device_id=device, device_id_type=pl.DeviceIdType.MESH
        )
    hot_ref[...] = slot_onehot(owner_ref, slab_count, me)
    pack_blocks(
        hot_ref[...], coef_ref, offs_ref, anchor_ref, blocks_ref, count_ref,
        send_ref, x_ref, blk_ref, rows_ref,
    )
    pl.semaphore_wait(barrier, slab_count + 1)
    spread_cells(
        me, syn_ref, send_ref, recv_ref, send_sem, recv_sem, part_ref, wz_ref, wxy_ref, idx_ref,
        blk_ref, r_ref, p_ref, f_ref, lists_ref, next_ref, tx_ref, ty_ref,
        t_ref, t_old_ref, hit_ref, x_old_ref, acc_ref, part32_ref, wide_ref, basis_ref,
    )
    pltpu.sync_copy(idx_ref, idx_smem)
    basis_planes(ana_ref, wide_ref, basis_ref)
    grid_steps(
        part_ref, vel_ref, new_ref, all_ref,
        hop_ref, got_ref, summed_ref, drive_ref, st_ref, own_ref,
        xs_ref, xr_ref, ys_ref, yr_ref, y32_ref, grid_send_sem, grid_recv_sem, local_sem,
    )
    sample_cells(
        me, hot_ref[...], all_ref, ana_ref, out_ref, wz_ref, wxy_ref, idx_smem,
        part32_ref, even_ref, odd_ref, pv_ref, c_ref, blk_ref, coef_send_ref, back_ref, x_ref,
        wide_ref, basis_ref, back_send_sem, back_recv_sem,
    )


def whole_step(owner, coef, offs, anchor, blocks, count, syn, ana, vel, slab_count):
    planes, mine, _ = vel.shape
    half = planes // 2
    copies = 6 + 4 * SWEEPS + 6
    cells = owner.shape[1]
    slots = slab_count * CAP
    held = GROUP * CAP
    block_rows = PLANES * CAP + 2
    back_rows = OUT_PLANES * CAP
    dma = pltpu.SemaphoreType.DMA
    return pl.pallas_call(
        step_kernel,
        out_shape=(
            jax.ShapeDtypeStruct(vel.shape, F32),
            jax.ShapeDtypeStruct((3, L, cells), BF16),
        ),
        in_specs=[VMEM_SPEC] * 9,
        out_specs=(VMEM_SPEC, VMEM_SPEC),
        scratch_shapes=[
            pltpu.VMEM((PLANES + 2, slots, 128), F32),
            pltpu.VMEM((block_rows, 128), F32),
            pltpu.VMEM((128, cells), F32),
            pltpu.VMEM((slots, cells), BF16),
            pltpu.VMEM((slab_count, block_rows, 128), BF16),
            pltpu.VMEM((slab_count, block_rows, 128), BF16),
            dma,
            dma((slab_count,)),
            pltpu.VMEM((planes, NY * LINE, 128), BF16),
            pltpu.VMEM((slots, 128, QP), BF16),
            pltpu.VMEM((slots, B, QP), F32),
            pltpu.VMEM((slab_count, 128), jnp.int32),
            pltpu.SMEM((slab_count, 128), jnp.int32),
            pltpu.VMEM((PLANES, held, 128), F32),
            pltpu.VMEM((3, held, QP), F32),
            pltpu.VMEM((3, held, QP), F32),
            pltpu.VMEM((GROUP, 2, 128), F32),
            pltpu.VMEM((GROUP, 2, 128), F32),
            pltpu.VMEM((128, 128), F32),
            pltpu.VMEM((128, 128), F32),
            pltpu.VMEM((GROUP * 128, QP), BF16),
            pltpu.VMEM((GROUP * 128, QP), BF16),
            pltpu.VMEM((NY * LAYERS, GROUP * 128), BF16),
            pltpu.VMEM((1, GROUP * 128), F32),
            pltpu.VMEM((GX, NY * LAYERS, QP), F32),
            pltpu.VMEM((ROWS, 128), F32),
            pltpu.VMEM((256, QP), F32),
            pltpu.VMEM((3, 256, QP), BF16),
            pltpu.VMEM((planes, NY * LINE, 128), BF16),
            pltpu.VMEM((2, half, mine, 128), BF16),
            pltpu.VMEM((4, half, mine, 128), BF16),
            pltpu.VMEM((2, half, mine, 128), BF16),
            pltpu.VMEM((planes, mine, 128), F32),
            pltpu.VMEM((planes + 2, mine + 16, 128), F32),
            pltpu.VMEM((planes, mine, 128), BF16),
            pltpu.VMEM((SWEEPS, 2, mine, 128), BF16),
            pltpu.VMEM((SWEEPS, 2, mine, 128), BF16),
            pltpu.VMEM((SWEEPS, 2, planes * LINE, 128), BF16),
            pltpu.VMEM((SWEEPS, 2, planes * LINE, 128), BF16),
            pltpu.VMEM((2, planes * LINE, 128), F32),
            dma((copies,)),
            dma((copies,)),
            dma,
            pltpu.VMEM((CAP, 3 * B, 128), F32),
            pltpu.VMEM((CAP, 3 * B, 128), F32),
            pltpu.VMEM((3, held, QP), F32),
            pltpu.VMEM((OUT_PLANES, held, 128), F32),
            pltpu.VMEM((slab_count, back_rows, 128), BF16),
            pltpu.VMEM((slab_count, back_rows, 128), BF16),
            dma,
            dma,
        ],
        compiler_params=pltpu.CompilerParams(
            collective_id=0, has_side_effects=True, vmem_limit_bytes=67_043_328
        ),
        name="whole_step",
    )(owner, coef, offs, anchor, blocks, count, syn, ana, vel)


def local(
    velocity_old, traction, offsets, owner_slab, anchor, blocks, block_count, synthesis, analysis
):
    slab_count = lax.axis_size("slab")
    owner = owner_slab.T
    planes, lines = velocity_old.shape[:2]
    velocity_new, velocity_coef = whole_step(
        owner,
        traction.transpose(1, 2, 0),
        offsets.transpose(1, 0, 2),
        anchor.T,
        blocks.T,
        block_count[None],
        synthesis,
        analysis,
        velocity_old.transpose(0, 1, 3, 2, 4).reshape(planes, lines * LINE, 128),
        slab_count,
    )
    velocity_new = velocity_new.reshape(planes, lines, 3, LAYERS, 128)
    return (velocity_new.transpose(0, 1, 3, 2, 4), velocity_coef.transpose(2, 0, 1))


def solution(mesh):
    in_specs = (
        P("slab", "batch", None, None, None),
        P(("slab", "batch"), None, None),
        P(("slab", "batch"), None, None),
        P(("slab", "batch"), None),
        P(("slab", "batch"), None),
        P(("slab", "batch"), None),
        P(("slab", "batch")),
        P(),
        P(),
    )
    out_specs = (P("slab", "batch", None, None, None), P(("slab", "batch"), None, None))
    return jax.shard_map(local, mesh=mesh, in_specs=in_specs, out_specs=out_specs, check_vma=False)
```

```python
import math

import jax
import jax.numpy as jnp
from jax import lax
from jax.experimental import pallas as pl
from jax.experimental.pallas import tpu as pltpu
from jax.sharding import PartitionSpec as P

SWEEPS = 2
GX = 8
NY = 64
NZ = 256
LAYERS = NZ // 128

L = 169
Q = 338
B = 16
REM = L - 128

CAP = 6
PLANES = 13
OUT_PLANES = 4
QP = 384

LINE = 3 * LAYERS
TILES = GX * NY * LAYERS
ROWS = TILES * 3

kernel_width = 0.8
coupling = 2.0
SCALE = math.sqrt(0.5 * math.log2(math.e)) / kernel_width
LOG_NORM = -math.log2(0.8 * math.sqrt(2.0 * math.pi))

F32 = jnp.float32
BF16 = jnp.bfloat16
NT = (((1,), (1,)), ((), ()))
NN = (((1,), (0,)), ((), ()))
TN = (((0,), (0,)), ((), ()))

VMEM_SPEC = pl.BlockSpec(memory_space=pltpu.VMEM)


def dot(a, b, dims):
    return lax.dot_general(a, b, dims, preferred_element_type=F32)


GROUP = 4
LINES = CAP * B
DEAD = 255


def relative(owner, me):
    y = (owner // 16 - me // 16 + 4) % 4
    z = (owner // 2 % 8 - me // 2 % 8 + 8) % 8
    core = (owner % 2 - me % 2 + 2) % 2
    return y * 16 + z * 2 + core


def wrap(value, size):
    value = jnp.where(value >= size, value - size, value)
    return jnp.where(value < 0, value + size, value)


def each_peer(me, sign, count, visit):
    my_y, my_z, my_core = me // 16, me // 2 % 8, me % 2
    for dy in range(count // 16):
        for core in range(2):
            base = wrap(my_y + sign * dy, count // 16) * 16 + wrap(my_core + sign * core, 2)

            def along(dz, carry, dy=dy, core=core, base=base):
                visit(dy * 16 + dz * 2 + core, base + 2 * wrap(my_z + sign * dz, 8))
                return carry

            lax.fori_loop(1 if dy == core == 0 else 0, 8, along, 0)


def slot_onehot(owner_ref, slab_count, me):
    cells = owner_ref.shape[1]
    owner = relative(owner_ref[...], me)
    slab_at = lax.broadcasted_iota(jnp.int32, (slab_count, cells), 0)
    member = jnp.where(slab_at == owner, 1.0, 0.0)
    first = lax.broadcasted_iota(jnp.int32, (cells, cells), 0)
    second = lax.broadcasted_iota(jnp.int32, (cells, cells), 1)
    before = jnp.where(first < second, 1.0, 0.0).astype(BF16)
    rank = jnp.sum(member * dot(member.astype(BF16), before, NN), axis=0, keepdims=True)
    slot = owner * CAP + rank.astype(jnp.int32)
    at = lax.broadcasted_iota(jnp.int32, (slab_count * CAP, cells), 0)
    return jnp.where(at == slot, 1.0, 0.0).astype(BF16)


def greet_all(me, count):
    barrier = pltpu.get_barrier_semaphore()

    def greet(step, carry):
        pl.semaphore_signal(
            barrier, inc=1, device_id={"slab": wrap(me + step, count)},
            device_id_type=pl.DeviceIdType.MESH,
        )
        return carry

    lax.fori_loop(1, count, greet, 0)
    return barrier


def pack_blocks(
    hot, coef_ref, offs_ref, anchor_ref, blocks_ref, count_ref, send_ref, x_ref, blk_ref, rows_ref
):
    slab_count = send_ref.shape[0]
    slots = slab_count * CAP
    rows_ref[...] = jnp.zeros_like(rows_ref)
    for k in range(3):
        x_ref[k] = dot(hot, coef_ref[k, :128, :], NT)
        rows_ref[k * REM : (k + 1) * REM] = coef_ref[k, 128:, :].astype(F32)
    x_ref[3] = dot(hot, rows_ref[...].astype(BF16), NT)
    tail = jnp.zeros((slots, QP - Q), F32)
    rows_ref[...] = jnp.zeros_like(rows_ref)
    for k in range(3):
        place = anchor_ref[k : k + 1, :]
        rows_ref[112:113] = (place % 128 if k == 2 else place).astype(F32)
        got = dot(hot, offs_ref[k], NN)
        x_ref[4 + 3 * k] = got[:, :128]
        x_ref[5 + 3 * k] = got[:, 128:256]
        x_ref[6 + 3 * k] = jnp.concatenate([got[:, 256:], tail], axis=1) + dot(
            hot, rows_ref[...].astype(BF16), NT
        )
    live = lax.broadcasted_iota(jnp.int32, blocks_ref.shape, 0) < count_ref[...]
    tile = blocks_ref[...]
    y = tile // LAYERS % NY + (tile % LAYERS) * NY
    lists = (tile // (NY * LAYERS), y)
    lane = lax.broadcasted_iota(jnp.int32, (slots, 128), 1) // B
    slot = lax.broadcasted_iota(jnp.int32, (slots, 128), 0) % CAP
    for n in range(2):
        values = jnp.where(live, lists[n], DEAD).astype(F32)
        for i in range(128 // B):
            rows_ref[i * B : (i + 1) * B] = values
        x_ref[PLANES + n] = jnp.where(lane == slot, dot(hot, rows_ref[...].astype(BF16), NT), 0.0)

    def step(target, carry):
        for r in range(PLANES):
            blk_ref[pl.ds(r * CAP, CAP), :] = x_ref[r, pl.ds(target * CAP, CAP), :]
        for n in range(2):
            blk_ref[pl.ds(PLANES * CAP + n, 1), :] = jnp.sum(
                x_ref[PLANES + n, pl.ds(target * CAP, CAP), :], axis=0, keepdims=True
            )
        send_ref[target] = blk_ref[...].astype(BF16)
        return carry

    lax.fori_loop(0, slab_count, step, 0)


def basis_planes(basis_ref, wide_ref, planes_ref):
    wide_ref[...] = jnp.zeros_like(wide_ref)
    wide_ref[:128, :Q] = basis_ref[:128, :].astype(F32)
    for k in range(3):
        if k > 0:
            wide_ref[128 + (k - 1) * REM : 128 + k * REM, :Q] = jnp.zeros((REM, Q), F32)
        wide_ref[128 + k * REM : 128 + (k + 1) * REM, :Q] = basis_ref[128:, :].astype(F32)
        planes_ref[k] = wide_ref[...].astype(BF16)


def z_weights(pz):
    stride = 8.0 * SCALE
    step = lax.broadcasted_iota(jnp.int32, (8, QP), 0).astype(F32) * SCALE
    d = pz - step - 8.0 * stride
    middle = LOG_NORM - d * d
    twice = d * (2.0 * stride)
    powers = {8: middle}
    for sign, last in ((1, 15), (-1, 0)):
        value, change = middle, sign * twice - stride * stride
        for g in range(8 + sign, last + sign, sign):
            value = value + change
            change = change - 2.0 * stride * stride
            powers[g] = value
    rows = [jnp.exp2(powers[g]) for g in range(16)]
    return [
        jnp.concatenate([row[:, n * 128 : (n + 1) * 128] for row in rows], axis=0).astype(BF16)
        for n in range(QP // 128)
    ]


def columns(row):
    first = lax.broadcasted_iota(jnp.int32, (128, 128), 0)
    second = lax.broadcasted_iota(jnp.int32, (128, 128), 1)
    diagonal = jnp.where(first == second, row, 0.0).astype(BF16)
    return dot(diagonal, jnp.ones((128, 128), BF16), NN)


def split_y(row):
    layer = jnp.where(row >= NY, 1.0, 0.0)
    return row - NY * layer, layer


def xy_weights(px, py, tx, ty):
    parts = []
    for n in range(QP // 128):
        lanes = slice(n * 128, (n + 1) * 128)
        dx = px[:, lanes] - tx
        dy = py[:, lanes] - ty
        parts.append(jnp.exp2(2.0 * LOG_NORM - (dx * dx + dy * dy)))
    return jnp.concatenate(parts, axis=1)


def spread_cells(
    me, syn_ref, send_ref, recv_ref, send_sem, recv_sem, part_ref, wz_ref, wxy_ref, idx_ref,
    blk_ref, r_ref, p_ref, f_ref, lists_ref, next_ref, tx_ref, ty_ref,
    t_ref, t_old_ref, hit_ref, x_old_ref, acc_ref, part32_ref, wide_ref, basis_ref,
):
    slab_count = send_ref.shape[0]

    def send(step, peer):
        pltpu.make_async_remote_copy(
            src_ref=send_ref.at[step],
            dst_ref=recv_ref.at[step],
            send_sem=send_sem,
            recv_sem=recv_sem.at[step],
            device_id={"slab": peer},
            device_id_type=pl.DeviceIdType.MESH,
        ).start()

    each_peer(me, 1, slab_count, send)
    pltpu.make_async_copy(send_ref.at[0], recv_ref.at[0], recv_sem.at[0]).start()
    basis_planes(syn_ref, wide_ref, basis_ref)
    for ref in (acc_ref, t_ref, t_old_ref, hit_ref, x_old_ref):
        ref[...] = jnp.zeros_like(ref)

    per_source = GX // GROUP

    def take(step, h):
        pltpu.make_async_copy(recv_ref.at[step], recv_ref.at[step], recv_sem.at[step]).wait()
        blk_ref[...] = recv_ref[step].astype(F32)
        for r in range(PLANES):
            r_ref[r, pl.ds(h * CAP, CAP), :] = blk_ref[r * CAP : (r + 1) * CAP, :]
        next_ref[h] = blk_ref[PLANES * CAP : PLANES * CAP + 2, :]

    def group(g, take_next):
        lists_ref[...] = next_ref[...]
        for k in range(3):
            anchor = r_ref[6 + 3 * k][:, 112:113]
            for t in range(3):
                p_ref[k, :, t * 128 : (t + 1) * 128] = (r_ref[4 + 3 * k + t] + anchor) * SCALE
            coef = jnp.concatenate([r_ref[k], r_ref[3]], axis=1).astype(BF16)
            f_ref[k] = dot(coef, basis_ref[k], NN)

        def source(h, carry):
            step = g * GROUP + h
            if take_next:
                take(step + GROUP, h)
            x_row, y_row = lists_ref[h, 0:1, :], lists_ref[h, 1:2, :]
            y, layer = split_y(y_row)
            place = jnp.where(x_row < DEAD, (x_row * NY + y) * LINE + layer, 0.0)
            idx_ref[pl.ds(step, 1), :] = jnp.clip(place.astype(jnp.int32), 0, ROWS - LINE + LAYERS - 1)
            tx_ref[...] = columns(x_row) * SCALE
            ty_ref[...] = columns(y) * SCALE
            picked = []
            for d in range(per_source):
                x = (h * per_source + d).astype(F32)
                mask = jnp.where(x_old_ref[...] == x, 1.0, 0.0).astype(BF16)
                picked.append(
                    jnp.concatenate(
                        [hit_ref[n] * mask[:, n * 128 : (n + 1) * 128] for n in range(GROUP)], axis=1
                    )
                )
            joined = dot(
                jnp.concatenate(picked, axis=0),
                jnp.concatenate([t_old_ref[k] for k in range(3)], axis=1),
                NN,
            )
            for d in range(per_source):
                acc_ref[h * per_source + d] += joined[d * NY * LAYERS : (d + 1) * NY * LAYERS]
            for i in range(CAP):
                c = step * CAP + i
                here = pl.ds(h * CAP + i, 1)
                lines = slice(i * B, (i + 1) * B)
                wxy = xy_weights(
                    p_ref[0, here, :], p_ref[1, here, :], tx_ref[lines], ty_ref[lines]
                )
                wxy_ref[c] = wxy
                weighted = jnp.concatenate(
                    [wxy * f_ref[k, here, :] for k in range(3)], axis=0
                ).astype(BF16)
                wz = z_weights(p_ref[2, here, :])
                for n, part in enumerate(wz):
                    wz_ref[c, n] = part
                terms = dot(weighted, jnp.concatenate(wz, axis=1), NT).astype(BF16)
                at = pl.ds(pl.multiple_of(h * 128 + i * B, B), B)
                for k in range(3):
                    t_ref[k, at, :] = terms[k * B : (k + 1) * B]
            return carry

        lax.fori_loop(0, GROUP, source, 0)
        t_old_ref[...] = t_ref[...]
        tile = lax.broadcasted_iota(jnp.int32, (NY * LAYERS, 128), 0).astype(F32)
        for h in range(GROUP):
            lanes = slice(h * 128, (h + 1) * 128)
            x_old_ref[:, lanes] = lists_ref[h, 0:1, :]
            hit_ref[h] = jnp.where(tile == lists_ref[h, 1:2, :], 1.0, 0.0).astype(BF16)

    for h in range(GROUP):
        take(h, h)

    def all_but_last(g, carry):
        group(g, True)
        return carry

    lax.fori_loop(0, slab_count // GROUP - 1, all_but_last, 0)
    group(slab_count // GROUP - 1, False)
    terms = jnp.concatenate([t_old_ref[k] for k in range(3)], axis=1)
    for x in range(GX):
        mask = jnp.where(x_old_ref[...] == float(x), 1.0, 0.0).astype(BF16)
        picked = [hit_ref[n] * mask[:, n * 128 : (n + 1) * 128] for n in range(GROUP)]
        acc_ref[x] += dot(jnp.concatenate(picked, axis=1), terms, NN)
    for x in range(GX):
        for layer in range(LAYERS):
            for k in range(3):
                part32_ref[pl.ds(x * NY * LINE + k * LAYERS + layer, NY, stride=LINE), :] = acc_ref[
                    x, layer * NY : (layer + 1) * NY, k * 128 : (k + 1) * 128
                ]
    for x in range(GX):
        part_ref[x] = part32_ref[x * NY * LINE : (x + 1) * NY * LINE, :].astype(BF16)
    others = pl.ds(1, slab_count - 1)
    pltpu.make_async_copy(send_ref.at[others], send_ref.at[others], send_sem).wait()


def sample_cells(
    me, hot, all_ref, ana_ref, out_ref, wz_ref, wxy_ref, idx_smem,
    v_ref, even_ref, odd_ref, pv_ref, c_ref, blk_ref, send_ref, back_ref, r_ref,
    wide_ref, basis_ref, send_sem, recv_sem,
):
    slab_count = send_ref.shape[0]
    for x in range(GX):
        v_ref[x * NY * LINE : (x + 1) * NY * LINE, :] = all_ref[x].astype(F32)

    def gather(step, to_ref):
        for i in range(CAP):
            for j in range(B):
                start = idx_smem[step, i * B + j]
                to_ref[i, pl.ds(j, 3, stride=B), :] = v_ref[pl.ds(start, 3, stride=LAYERS), :]

    def project(step, h, from_ref):
        for i in range(CAP):
            c = step * CAP + i
            wz = jnp.concatenate([wz_ref[c, n] for n in range(QP // 128)], axis=1)
            projected = dot(from_ref[i].astype(BF16), wz, NN)
            wxy = wxy_ref[c]
            for k in range(3):
                pv_ref[k, pl.ds(h * CAP + i, 1), :] = jnp.sum(
                    projected[k * B : (k + 1) * B] * wxy, axis=0, keepdims=True
                )

    def work(g):
        def pair(n, carry):
            step = g * GROUP + 2 * n
            later = jnp.where(n < GROUP // 2 - 1, step + 2, (g - 1) * GROUP)
            gather(step + 1, odd_ref)
            project(step, 2 * n, even_ref)
            gather(jnp.where(later < 0, 0, later), even_ref)
            project(step + 1, 2 * n + 1, odd_ref)
            return carry

        lax.fori_loop(0, GROUP // 2, pair, 0)
        rem = jnp.zeros((GROUP * CAP, 128), F32)
        for k in range(3):
            got = dot(pv_ref[k].astype(BF16), basis_ref[k], NT)
            c_ref[k] = got[:, :128]
            rem = rem + got[:, 128:]
        c_ref[3] = rem
        for h in range(GROUP):
            for r in range(OUT_PLANES):
                blk_ref[r * CAP : (r + 1) * CAP, :] = c_ref[r, h * CAP : (h + 1) * CAP, :]
            send_ref[g * GROUP + h] = blk_ref[: OUT_PLANES * CAP, :].astype(BF16)

    my_y, my_z, my_core = me // 16, me // 2 % 8, me % 2

    def send(g, first=0):
        dy = g // (16 // GROUP)
        base = wrap(my_y - dy, slab_count // 16) * 16
        for h in range(first, GROUP):
            dz = (g - dy * (16 // GROUP)) * (GROUP // 2) + h // 2
            place = base + 2 * wrap(my_z - dz, 8) + wrap(my_core - h % 2, 2)
            pltpu.make_async_remote_copy(
                src_ref=send_ref.at[g * GROUP + h],
                dst_ref=back_ref.at[g * GROUP + h],
                send_sem=send_sem,
                recv_sem=recv_sem,
                device_id={"slab": place},
                device_id_type=pl.DeviceIdType.MESH,
            ).start()

    groups = slab_count // GROUP
    gather((groups - 1) * GROUP, even_ref)
    work(groups - 1)

    def group(n, carry):
        g = groups - 2 - n
        send(g + 1)
        work(g)
        return carry

    lax.fori_loop(0, groups - 1, group, 0)
    send(0, 1)
    back_ref[0] = send_ref[0]
    others = pl.ds(1, slab_count - 1)
    pltpu.make_async_copy(back_ref.at[others], back_ref.at[others], recv_sem).wait()

    def take(step, carry):
        blk_ref[: OUT_PLANES * CAP, :] = back_ref[step].astype(F32)
        for r in range(OUT_PLANES):
            r_ref[r, pl.ds(step * CAP, CAP), :] = blk_ref[r * CAP : (r + 1) * CAP, :]
        return carry

    lax.fori_loop(0, slab_count, take, 0, unroll=2)
    rem = dot(r_ref[3].astype(BF16), hot, TN)
    for k in range(3):
        main = dot(r_ref[k].astype(BF16), hot, TN)
        out_ref[k, :128] = main
        out_ref[k, 128:] = rem[k * REM : (k + 1) * REM]
    pltpu.make_async_copy(send_ref.at[others], send_ref.at[others], send_sem).wait()


def batch_neighbours():
    batches, b = lax.axis_size("batch"), lax.axis_index("batch")
    return [lax.rem(b + i, batches) for i in range(1, batches)]


def grid_steps(
    part_ref, vel_ref, new_ref, all_ref,
    hop_ref, got_ref, summed_ref, drive_ref, st_ref, own_ref,
    xs_ref, xr_ref, ys_ref, yr_ref, y32_ref, send_sem, recv_sem, local_sem,
):
    planes, mine, _ = vel_ref.shape
    half = planes // 2
    batches, slabs = lax.axis_size("batch"), lax.axis_size("slab")
    b, s = lax.axis_index("batch"), lax.axis_index("slab")
    right, far, left = batch_neighbours()
    above, below = lax.rem(s + 1, slabs), lax.rem(s + slabs - 1, slabs)

    def rows(part):
        return pl.ds(pl.multiple_of(part * mine, mine), mine)

    started = []

    def send(src, dst, **device):
        n = len(started)
        copy = pltpu.make_async_remote_copy(
            src_ref=src, dst_ref=dst, send_sem=send_sem.at[n], recv_sem=recv_sem.at[n],
            device_id=device, device_id_type=pl.DeviceIdType.MESH,
        )
        copy.start()
        started.append(copy)
        return copy

    low, high = pl.ds(0, half), pl.ds(half, half)

    hop_r = send(part_ref.at[low, rows(far)], hop_ref.at[0], batch=right)
    hop_l = send(part_ref.at[high, rows(far)], hop_ref.at[1], batch=left)
    near_r = send(part_ref.at[high, rows(right)], got_ref.at[0], batch=right)
    near_l = send(part_ref.at[low, rows(left)], got_ref.at[1], batch=left)
    hop_r.wait_recv()
    summed_ref[0] = (
        part_ref[low, rows(right), :].astype(F32) + hop_ref[0].astype(F32)
    ).astype(BF16)
    far_r = send(summed_ref.at[0], got_ref.at[2], batch=right)
    hop_l.wait_recv()
    summed_ref[1] = (
        part_ref[high, rows(left), :].astype(F32) + hop_ref[1].astype(F32)
    ).astype(BF16)
    far_l = send(summed_ref.at[1], got_ref.at[3], batch=left)
    drive_ref[...] = vel_ref[...] + part_ref[:, rows(b), :].astype(F32)
    near_r.wait_recv()
    near_l.wait_recv()
    far_r.wait_recv()
    far_l.wait_recv()
    drive_ref[:half] += got_ref[1].astype(F32) + got_ref[2].astype(F32)
    drive_ref[half:] += got_ref[0].astype(F32) + got_ref[3].astype(F32)

    lane = lax.broadcasted_iota(jnp.int32, (mine, 128), 1)
    layer = lax.broadcasted_iota(jnp.int32, (mine, 128), 0) % LAYERS
    at_end, at_start = lane == 127, lane == 0
    has_next, has_previous = layer < LAYERS - 1, layer > 0
    inside = slice(8, 8 + mine)
    for sweep in range(SWEEPS):
        for x in range(planes):
            st_ref[1 + x, inside, :] = drive_ref[x] if sweep == 0 else new_ref[x]
        xs_ref[sweep, 0] = st_ref[planes, inside, :].astype(BF16)
        xs_ref[sweep, 1] = st_ref[1, inside, :].astype(BF16)
        for x in range(planes):
            y32_ref[0, x * LINE : (x + 1) * LINE] = st_ref[1 + x, 2 + mine : 8 + mine, :]
            y32_ref[1, x * LINE : (x + 1) * LINE] = st_ref[1 + x, 8 : 8 + LINE, :]
        for side in range(2):
            ys_ref[sweep, side] = y32_ref[side].astype(BF16)
        copies = [
            send(xs_ref.at[sweep, 0], xr_ref.at[sweep, 0], slab=above),
            send(xs_ref.at[sweep, 1], xr_ref.at[sweep, 1], slab=below),
            send(ys_ref.at[sweep, 0], yr_ref.at[sweep, 0], batch=right),
            send(ys_ref.at[sweep, 1], yr_ref.at[sweep, 1], batch=left),
        ]
        for copy in copies:
            copy.wait_recv()
        x_low, x_high = xr_ref[sweep, 0].astype(F32), xr_ref[sweep, 1].astype(F32)
        st_ref[0, inside, :] = jnp.where(s > 0, x_low, 0.0)
        st_ref[planes + 1, inside, :] = jnp.where(s < slabs - 1, x_high, 0.0)
        y32_ref[0] = jnp.where(b > 0, yr_ref[sweep, 0].astype(F32), 0.0)
        y32_ref[1] = jnp.where(b < batches - 1, yr_ref[sweep, 1].astype(F32), 0.0)
        for x in range(planes):
            st_ref[1 + x, 8 - LINE : 8, :] = y32_ref[0, x * LINE : (x + 1) * LINE]
            st_ref[1 + x, 8 + mine : 8 + mine + LINE, :] = y32_ref[1, x * LINE : (x + 1) * LINE]
        for x in range(planes):
            total = (
                st_ref[x, inside, :]
                + st_ref[x + 2, inside, :]
                + st_ref[x + 1, 8 - LINE : 8 - LINE + mine, :]
                + st_ref[x + 1, 8 + LINE : 8 + LINE + mine, :]
            )
            centre = st_ref[x + 1, inside, :]
            after = jnp.where(has_next, st_ref[x + 1, 9 : 9 + mine, :], 0.0)
            before = jnp.where(has_previous, st_ref[x + 1, 7 : 7 + mine, :], 0.0)
            upper = pltpu.roll(jnp.where(at_start, after, centre), 127, 1)
            lower = pltpu.roll(jnp.where(at_end, before, centre), 1, 1)
            total = total + upper + lower
            new_ref[x] = (drive_ref[x] + coupling * total) * (1.0 / (1.0 + 6.0 * coupling))

    own_ref[...] = new_ref[...].astype(BF16)
    at_right_low = send(own_ref.at[low], all_ref.at[low, rows(b)], batch=right)
    at_left_high = send(own_ref.at[high], all_ref.at[high, rows(b)], batch=left)
    at_right_high = send(own_ref.at[high], all_ref.at[high, rows(b)], batch=right)
    at_left_low = send(own_ref.at[low], all_ref.at[low, rows(b)], batch=left)
    local = pltpu.make_async_copy(own_ref, all_ref.at[:, rows(b)], local_sem)
    local.start()
    at_right_low.wait_recv()
    on_r = send(all_ref.at[low, rows(left)], all_ref.at[low, rows(left)], batch=right)
    at_left_high.wait_recv()
    on_l = send(all_ref.at[high, rows(right)], all_ref.at[high, rows(right)], batch=left)
    for copy in (at_right_high, at_left_low, on_r, on_l):
        copy.wait_recv()
    local.wait()
    for copy in started:
        copy.wait_send()


def step_kernel(
    owner_ref, coef_ref, offs_ref, anchor_ref, blocks_ref, count_ref, syn_ref, ana_ref, vel_ref,
    new_ref, out_ref,
    x_ref, blk_ref, rows_ref, hot_ref, send_ref, recv_ref, send_sem, recv_sem,
    part_ref, wz_ref, wxy_ref, idx_ref, idx_smem,
    r_ref, p_ref, f_ref, lists_ref, next_ref, tx_ref, ty_ref, t_ref, t_old_ref, hit_ref, x_old_ref,
    acc_ref, part32_ref, wide_ref, basis_ref,
    all_ref, hop_ref, got_ref, summed_ref, drive_ref, st_ref, own_ref,
    xs_ref, xr_ref, ys_ref, yr_ref, y32_ref, grid_send_sem, grid_recv_sem, local_sem,
    even_ref, odd_ref, pv_ref, c_ref, coef_send_ref, back_ref, back_send_sem, back_recv_sem,
):
    slab_count = send_ref.shape[0]
    me = lax.axis_index("slab")
    barrier = greet_all(me, slab_count)
    right, _, left = batch_neighbours()
    for device in ({"batch": right}, {"batch": left}):
        pl.semaphore_signal(
            barrier, inc=1, device_id=device, device_id_type=pl.DeviceIdType.MESH
        )
    hot_ref[...] = slot_onehot(owner_ref, slab_count, me)
    pack_blocks(
        hot_ref[...], coef_ref, offs_ref, anchor_ref, blocks_ref, count_ref,
        send_ref, x_ref, blk_ref, rows_ref,
    )
    pl.semaphore_wait(barrier, slab_count + 1)
    spread_cells(
        me, syn_ref, send_ref, recv_ref, send_sem, recv_sem, part_ref, wz_ref, wxy_ref, idx_ref,
        blk_ref, r_ref, p_ref, f_ref, lists_ref, next_ref, tx_ref, ty_ref,
        t_ref, t_old_ref, hit_ref, x_old_ref, acc_ref, part32_ref, wide_ref, basis_ref,
    )
    pltpu.sync_copy(idx_ref, idx_smem)
    basis_planes(ana_ref, wide_ref, basis_ref)
    grid_steps(
        part_ref, vel_ref, new_ref, all_ref,
        hop_ref, got_ref, summed_ref, drive_ref, st_ref, own_ref,
        xs_ref, xr_ref, ys_ref, yr_ref, y32_ref, grid_send_sem, grid_recv_sem, local_sem,
    )
    sample_cells(
        me, hot_ref[...], all_ref, ana_ref, out_ref, wz_ref, wxy_ref, idx_smem,
        part32_ref, even_ref, odd_ref, pv_ref, c_ref, blk_ref, coef_send_ref, back_ref, x_ref,
        wide_ref, basis_ref, back_send_sem, back_recv_sem,
    )


def whole_step(owner, coef, offs, anchor, blocks, count, syn, ana, vel, slab_count):
    planes, mine, _ = vel.shape
    half = planes // 2
    copies = 6 + 4 * SWEEPS + 6
    cells = owner.shape[1]
    slots = slab_count * CAP
    held = GROUP * CAP
    block_rows = PLANES * CAP + 2
    back_rows = OUT_PLANES * CAP
    dma = pltpu.SemaphoreType.DMA
    return pl.pallas_call(
        step_kernel,
        out_shape=(
            jax.ShapeDtypeStruct(vel.shape, F32),
            jax.ShapeDtypeStruct((3, L, cells), F32),
        ),
        in_specs=[VMEM_SPEC] * 9,
        out_specs=(VMEM_SPEC, VMEM_SPEC),
        scratch_shapes=[
            pltpu.VMEM((PLANES + 2, slots, 128), F32),
            pltpu.VMEM((block_rows, 128), F32),
            pltpu.VMEM((128, cells), F32),
            pltpu.VMEM((slots, cells), BF16),
            pltpu.VMEM((slab_count, block_rows, 128), BF16),
            pltpu.VMEM((slab_count, block_rows, 128), BF16),
            dma,
            dma((slab_count,)),
            pltpu.VMEM((planes, NY * LINE, 128), BF16),
            pltpu.VMEM((slots, QP // 128, 128, 128), BF16),
            pltpu.VMEM((slots, B, QP), F32),
            pltpu.VMEM((slab_count, 128), jnp.int32),
            pltpu.SMEM((slab_count, 128), jnp.int32),
            pltpu.VMEM((PLANES, held, 128), F32),
            pltpu.VMEM((3, held, QP), F32),
            pltpu.VMEM((3, held, QP), F32),
            pltpu.VMEM((GROUP, 2, 128), F32),
            pltpu.VMEM((GROUP, 2, 128), F32),
            pltpu.VMEM((128, 128), F32),
            pltpu.VMEM((128, 128), F32),
            pltpu.VMEM((3, GROUP * 128, 128), BF16),
            pltpu.VMEM((3, GROUP * 128, 128), BF16),
            pltpu.VMEM((GROUP, NY * LAYERS, 128), BF16),
            pltpu.VMEM((1, GROUP * 128), F32),
            pltpu.VMEM((GX, NY * LAYERS, QP), F32),
            pltpu.VMEM((ROWS, 128), F32),
            pltpu.VMEM((256, QP), F32),
            pltpu.VMEM((3, 256, QP), BF16),
            pltpu.VMEM((planes, NY * LINE, 128), BF16),
            pltpu.VMEM((2, half, mine, 128), BF16),
            pltpu.VMEM((4, half, mine, 128), BF16),
            pltpu.VMEM((2, half, mine, 128), BF16),
            pltpu.VMEM((planes, mine, 128), F32),
            pltpu.VMEM((planes + 2, mine + 16, 128), F32),
            pltpu.VMEM((planes, mine, 128), BF16),
            pltpu.VMEM((SWEEPS, 2, mine, 128), BF16),
            pltpu.VMEM((SWEEPS, 2, mine, 128), BF16),
            pltpu.VMEM((SWEEPS, 2, planes * LINE, 128), BF16),
            pltpu.VMEM((SWEEPS, 2, planes * LINE, 128), BF16),
            pltpu.VMEM((2, planes * LINE, 128), F32),
            dma((copies,)),
            dma((copies,)),
            dma,
            pltpu.VMEM((CAP, 3 * B, 128), F32),
            pltpu.VMEM((CAP, 3 * B, 128), F32),
            pltpu.VMEM((3, held, QP), F32),
            pltpu.VMEM((OUT_PLANES, held, 128), F32),
            pltpu.VMEM((slab_count, back_rows, 128), BF16),
            pltpu.VMEM((slab_count, back_rows, 128), BF16),
            dma,
            dma,
        ],
        compiler_params=pltpu.CompilerParams(
            collective_id=0, has_side_effects=True, vmem_limit_bytes=67_043_328
        ),
        name="whole_step",
    )(owner, coef, offs, anchor, blocks, count, syn, ana, vel)


def local(
    velocity_old, traction, offsets, owner_slab, anchor, blocks, block_count, synthesis, analysis
):
    slab_count = lax.axis_size("slab")
    owner = owner_slab.T
    planes, lines = velocity_old.shape[:2]
    velocity_new, velocity_coef = whole_step(
        owner,
        traction.transpose(1, 2, 0),
        offsets.transpose(1, 0, 2),
        anchor.T,
        blocks.T,
        block_count[None],
        synthesis,
        analysis,
        velocity_old.transpose(0, 1, 3, 2, 4).reshape(planes, lines * LINE, 128),
        slab_count,
    )
    velocity_new = velocity_new.reshape(planes, lines, 3, LAYERS, 128)
    return (velocity_new.transpose(0, 1, 3, 2, 4), velocity_coef.astype(BF16).transpose(2, 0, 1))


def solution(mesh):
    in_specs = (
        P("slab", "batch", None, None, None),
        P(("slab", "batch"), None, None),
        P(("slab", "batch"), None, None),
        P(("slab", "batch"), None),
        P(("slab", "batch"), None),
        P(("slab", "batch"), None),
        P(("slab", "batch")),
        P(),
        P(),
    )
    out_specs = (P("slab", "batch", None, None, None), P(("slab", "batch"), None, None))
    return jax.shard_map(local, mesh=mesh, in_specs=in_specs, out_specs=out_specs, check_vma=False)
```

```python
import math

import jax
import jax.numpy as jnp
from jax import lax
from jax.experimental import pallas as pl
from jax.experimental.pallas import tpu as pltpu
from jax.sharding import PartitionSpec as P

SWEEPS = 2
GX = 8
NY = 64
NZ = 256
LAYERS = NZ // 128

L = 169
Q = 338
B = 16
REM = L - 128

CAP = 6
PLANES = 13
OUT_PLANES = 4
QP = 384

LINE = 3 * LAYERS
TILES = GX * NY * LAYERS
ROWS = TILES * 3

kernel_width = 0.8
coupling = 2.0
SCALE = math.sqrt(0.5 * math.log2(math.e)) / kernel_width
LOG_NORM = -math.log2(0.8 * math.sqrt(2.0 * math.pi))

F32 = jnp.float32
BF16 = jnp.bfloat16
NT = (((1,), (1,)), ((), ()))
NN = (((1,), (0,)), ((), ()))
TN = (((0,), (0,)), ((), ()))

VMEM_SPEC = pl.BlockSpec(memory_space=pltpu.VMEM)


def dot(a, b, dims):
    return lax.dot_general(a, b, dims, preferred_element_type=F32)


GROUP = 4
LINES = CAP * B
DEAD = 255


def relative(owner, me):
    y = (owner // 16 - me // 16 + 4) % 4
    z = (owner // 2 % 8 - me // 2 % 8 + 8) % 8
    core = (owner % 2 - me % 2 + 2) % 2
    return y * 16 + core * 8 + z


def wrap(value, size):
    value = jnp.where(value >= size, value - size, value)
    return jnp.where(value < 0, value + size, value)


def each_peer(me, sign, count, visit):
    my_y, my_z, my_core = me // 16, me // 2 % 8, me % 2
    for dy in range(count // 16):
        for core in range(2):
            base = wrap(my_y + sign * dy, count // 16) * 16 + wrap(my_core + sign * core, 2)

            def along(dz, carry, dy=dy, core=core, base=base):
                visit(dy * 16 + core * 8 + dz, base + 2 * wrap(my_z + sign * dz, 8))
                return carry

            lax.fori_loop(1 if dy == core == 0 else 0, 8, along, 0)


def slot_onehot(owner_ref, slab_count, me):
    cells = owner_ref.shape[1]
    owner = relative(owner_ref[...], me)
    slab_at = lax.broadcasted_iota(jnp.int32, (slab_count, cells), 0)
    member = jnp.where(slab_at == owner, 1.0, 0.0)
    first = lax.broadcasted_iota(jnp.int32, (cells, cells), 0)
    second = lax.broadcasted_iota(jnp.int32, (cells, cells), 1)
    before = jnp.where(first < second, 1.0, 0.0).astype(BF16)
    rank = jnp.sum(member * dot(member.astype(BF16), before, NN), axis=0, keepdims=True)
    slot = owner * CAP + rank.astype(jnp.int32)
    at = lax.broadcasted_iota(jnp.int32, (slab_count * CAP, cells), 0)
    return jnp.where(at == slot, 1.0, 0.0).astype(BF16)


def greet_all(me, count):
    barrier = pltpu.get_barrier_semaphore()

    def greet(step, carry):
        pl.semaphore_signal(
            barrier, inc=1, device_id={"slab": wrap(me + step, count)},
            device_id_type=pl.DeviceIdType.MESH,
        )
        return carry

    lax.fori_loop(1, count, greet, 0)
    return barrier


def pack_blocks(
    hot, coef_ref, offs_ref, anchor_ref, blocks_ref, count_ref, send_ref, x_ref, blk_ref, rows_ref
):
    slab_count = send_ref.shape[0]
    slots = slab_count * CAP
    rows_ref[...] = jnp.zeros_like(rows_ref)
    for k in range(3):
        x_ref[k] = dot(hot, coef_ref[k, :128, :], NT)
        rows_ref[k * REM : (k + 1) * REM] = coef_ref[k, 128:, :].astype(F32)
    x_ref[3] = dot(hot, rows_ref[...].astype(BF16), NT)
    tail = jnp.zeros((slots, QP - Q), F32)
    rows_ref[...] = jnp.zeros_like(rows_ref)
    for k in range(3):
        place = anchor_ref[k : k + 1, :]
        rows_ref[112:113] = (place % 128 if k == 2 else place).astype(F32)
        got = dot(hot, offs_ref[k], NN)
        x_ref[4 + 3 * k] = got[:, :128]
        x_ref[5 + 3 * k] = got[:, 128:256]
        x_ref[6 + 3 * k] = jnp.concatenate([got[:, 256:], tail], axis=1) + dot(
            hot, rows_ref[...].astype(BF16), NT
        )
    live = lax.broadcasted_iota(jnp.int32, blocks_ref.shape, 0) < count_ref[...]
    tile = blocks_ref[...]
    y = tile // LAYERS % NY + (tile % LAYERS) * NY
    lists = (tile // (NY * LAYERS), y)
    lane = lax.broadcasted_iota(jnp.int32, (slots, 128), 1) // B
    slot = lax.broadcasted_iota(jnp.int32, (slots, 128), 0) % CAP
    for n in range(2):
        values = jnp.where(live, lists[n], DEAD).astype(F32)
        for i in range(128 // B):
            rows_ref[i * B : (i + 1) * B] = values
        x_ref[PLANES + n] = jnp.where(lane == slot, dot(hot, rows_ref[...].astype(BF16), NT), 0.0)

    def step(target, carry):
        for r in range(PLANES):
            blk_ref[0, pl.ds(r * CAP, CAP), :] = x_ref[r, pl.ds(target * CAP, CAP), :]
        for n in range(2):
            blk_ref[0, pl.ds(PLANES * CAP + n, 1), :] = jnp.sum(
                x_ref[PLANES + n, pl.ds(target * CAP, CAP), :], axis=0, keepdims=True
            )
        send_ref[target] = blk_ref[0].astype(BF16)
        return carry

    lax.fori_loop(0, slab_count, step, 0)


def basis_planes(basis_ref, wide_ref, planes_ref):
    wide_ref[...] = jnp.zeros_like(wide_ref)
    wide_ref[:128, :Q] = basis_ref[:128, :].astype(F32)
    for k in range(3):
        if k > 0:
            wide_ref[128 + (k - 1) * REM : 128 + k * REM, :Q] = jnp.zeros((REM, Q), F32)
        wide_ref[128 + k * REM : 128 + (k + 1) * REM, :Q] = basis_ref[128:, :].astype(F32)
        planes_ref[k] = wide_ref[...].astype(BF16)


def z_weights(pz):
    stride = 8.0 * SCALE
    step = lax.broadcasted_iota(jnp.int32, (8, QP), 0).astype(F32) * SCALE
    d = pz - step - 8.0 * stride
    middle = LOG_NORM - d * d
    twice = d * (2.0 * stride)
    powers = {8: middle}
    for sign, last in ((1, 15), (-1, 0)):
        value, change = middle, sign * twice - stride * stride
        for g in range(8 + sign, last + sign, sign):
            value = value + change
            change = change - 2.0 * stride * stride
            powers[g] = value
    rows = [jnp.exp2(powers[g]) for g in range(16)]
    return [
        jnp.concatenate([row[:, n * 128 : (n + 1) * 128] for row in rows], axis=0).astype(BF16)
        for n in range(QP // 128)
    ]


def columns(row):
    first = lax.broadcasted_iota(jnp.int32, (128, 128), 0)
    second = lax.broadcasted_iota(jnp.int32, (128, 128), 1)
    diagonal = jnp.where(first == second, row, 0.0).astype(BF16)
    return dot(diagonal, jnp.ones((128, 128), BF16), NN)


def split_y(row):
    layer = jnp.where(row >= NY, 1.0, 0.0)
    return row - NY * layer, layer


def xy_weights(px, py, tx, ty):
    parts = []
    for n in range(QP // 128):
        lanes = slice(n * 128, (n + 1) * 128)
        dx = px[:, lanes] - tx
        dy = py[:, lanes] - ty
        parts.append(jnp.exp2(2.0 * LOG_NORM - (dx * dx + dy * dy)))
    return jnp.concatenate(parts, axis=1)


def spread_cells(
    me, syn_ref, send_ref, recv_ref, send_sem, recv_sem, part_ref, wz_ref, wxy_ref, idx_ref,
    blk_ref, r_ref, p_ref, f_ref, lists_ref, next_ref, tx_ref, ty_ref,
    t_ref, t_old_ref, hit_ref, x_old_ref, acc_ref, part32_ref, wide_ref, basis_ref,
):
    slab_count = send_ref.shape[0]

    def send(step, peer):
        pltpu.make_async_remote_copy(
            src_ref=send_ref.at[step],
            dst_ref=recv_ref.at[step],
            send_sem=send_sem,
            recv_sem=recv_sem.at[step],
            device_id={"slab": peer},
            device_id_type=pl.DeviceIdType.MESH,
        ).start()

    each_peer(me, 1, slab_count, send)
    pltpu.make_async_copy(send_ref.at[0], recv_ref.at[0], recv_sem.at[0]).start()
    basis_planes(syn_ref, wide_ref, basis_ref)
    for ref in (acc_ref, t_ref, t_old_ref, hit_ref, x_old_ref):
        ref[...] = jnp.zeros_like(ref)


    def take(step, h, side):
        pltpu.make_async_copy(recv_ref.at[step], recv_ref.at[step], recv_sem.at[step]).wait()
        blk_ref[side] = recv_ref[step].astype(F32)
        for r in range(PLANES):
            r_ref[r, pl.ds(h * CAP, CAP), :] = blk_ref[side, r * CAP : (r + 1) * CAP, :]
        next_ref[h] = blk_ref[side, PLANES * CAP : PLANES * CAP + 2, :]

    def group(g, take_next):
        lists_ref[...] = next_ref[...]
        for k in range(3):
            anchor = r_ref[6 + 3 * k][:, 112:113]
            for t in range(3):
                p_ref[k, :, t * 128 : (t + 1) * 128] = (r_ref[4 + 3 * k + t] + anchor) * SCALE
            coef = jnp.concatenate([r_ref[k], r_ref[3]], axis=1).astype(BF16)
            f_ref[k] = dot(coef, basis_ref[k], NN)

        def pair(n, carry):
            sources = [2 * n, 2 * n + 1]
            for side, h in enumerate(sources):
                step = g * GROUP + h
                if take_next:
                    take(step + GROUP, h, side)
                x_row, y_row = lists_ref[h, 0:1, :], lists_ref[h, 1:2, :]
                y, layer = split_y(y_row)
                place = jnp.where(x_row < DEAD, (x_row * NY + y) * LINE + layer, 0.0)
                idx_ref[pl.ds(step, 1), :] = jnp.clip(
                    place.astype(jnp.int32), 0, ROWS - LINE + LAYERS - 1
                )
                tx_ref[side] = columns(x_row) * SCALE
                ty_ref[side] = columns(y) * SCALE
            held = 2 * GX // GROUP
            picked = []
            for d in range(held):
                x = (n * held + d).astype(F32)
                mask = jnp.where(x_old_ref[...] == x, 1.0, 0.0).astype(BF16)
                picked.append(
                    jnp.concatenate(
                        [hit_ref[q] * mask[:, q * 128 : (q + 1) * 128] for q in range(GROUP)], axis=1
                    )
                )
            joined = dot(
                jnp.concatenate(picked, axis=0),
                jnp.concatenate([t_old_ref[k] for k in range(3)], axis=1),
                NN,
            )
            for d in range(held):
                acc_ref[n * held + d] += joined[d * NY * LAYERS : (d + 1) * NY * LAYERS]
            for side, h in enumerate(sources):
                for i in range(CAP):
                    c = (g * GROUP + h) * CAP + i
                    here = pl.ds(h * CAP + i, 1)
                    lines = slice(i * B, (i + 1) * B)
                    wxy = xy_weights(
                        p_ref[0, here, :], p_ref[1, here, :],
                        tx_ref[side, lines, :], ty_ref[side, lines, :],
                    )
                    wxy_ref[c] = wxy
                    weighted = jnp.concatenate(
                        [wxy * f_ref[k, here, :] for k in range(3)], axis=0
                    ).astype(BF16)
                    wz = z_weights(p_ref[2, here, :])
                    for q, part in enumerate(wz):
                        wz_ref[c, q] = part
                    terms = dot(weighted, jnp.concatenate(wz, axis=1), NT).astype(BF16)
                    at = pl.ds(pl.multiple_of(h * 128 + i * B, B), B)
                    for k in range(3):
                        t_ref[k, at, :] = terms[k * B : (k + 1) * B]
            return carry

        lax.fori_loop(0, GROUP // 2, pair, 0)
        t_old_ref[...] = t_ref[...]
        tile = lax.broadcasted_iota(jnp.int32, (NY * LAYERS, 128), 0).astype(F32)
        for h in range(GROUP):
            lanes = slice(h * 128, (h + 1) * 128)
            x_old_ref[:, lanes] = lists_ref[h, 0:1, :]
            hit_ref[h] = jnp.where(tile == lists_ref[h, 1:2, :], 1.0, 0.0).astype(BF16)

    for h in range(GROUP):
        take(h, h, h % 2)

    def all_but_last(g, carry):
        group(g, True)
        return carry

    lax.fori_loop(0, slab_count // GROUP - 1, all_but_last, 0)
    group(slab_count // GROUP - 1, False)
    terms = jnp.concatenate([t_old_ref[k] for k in range(3)], axis=1)
    for x in range(GX):
        mask = jnp.where(x_old_ref[...] == float(x), 1.0, 0.0).astype(BF16)
        picked = [hit_ref[n] * mask[:, n * 128 : (n + 1) * 128] for n in range(GROUP)]
        acc_ref[x] += dot(jnp.concatenate(picked, axis=1), terms, NN)
    for x in range(GX):
        for layer in range(LAYERS):
            for k in range(3):
                part32_ref[pl.ds(x * NY * LINE + k * LAYERS + layer, NY, stride=LINE), :] = acc_ref[
                    x, layer * NY : (layer + 1) * NY, k * 128 : (k + 1) * 128
                ]
    for x in range(GX):
        part_ref[x] = part32_ref[x * NY * LINE : (x + 1) * NY * LINE, :].astype(BF16)
    others = pl.ds(1, slab_count - 1)
    pltpu.make_async_copy(send_ref.at[others], send_ref.at[others], send_sem).wait()


def sample_cells(
    me, hot, all_ref, ana_ref, out_ref, wz_ref, wxy_ref, idx_smem,
    v_ref, even_ref, odd_ref, pv_ref, c_ref, blk_ref, send_ref, back_ref, r_ref,
    wide_ref, basis_ref, send_sem, recv_sem,
):
    slab_count = send_ref.shape[0]
    for x in range(GX):
        v_ref[x * NY * LINE : (x + 1) * NY * LINE, :] = all_ref[x].astype(F32)

    def gather(step, to_ref):
        for i in range(CAP):
            for j in range(B):
                start = idx_smem[step, i * B + j]
                to_ref[i, pl.ds(j, 3, stride=B), :] = v_ref[pl.ds(start, 3, stride=LAYERS), :]

    def project(step, h, from_ref):
        for i in range(CAP):
            c = step * CAP + i
            wz = jnp.concatenate([wz_ref[c, n] for n in range(QP // 128)], axis=1)
            projected = dot(from_ref[i].astype(BF16), wz, NN)
            wxy = wxy_ref[c]
            for k in range(3):
                pv_ref[k, pl.ds(h * CAP + i, 1), :] = jnp.sum(
                    projected[k * B : (k + 1) * B] * wxy, axis=0, keepdims=True
                )

    def work(g):
        buffers = (even_ref, odd_ref)
        for h in range(GROUP):
            step = g * GROUP + h
            if h < GROUP - 1:
                later = step + 1
            else:
                later = jnp.maximum((g - 1) * GROUP, 0)
            gather(later, buffers[(h + 1) % 2])
            project(step, h, buffers[h % 2])

        rem = jnp.zeros((GROUP * CAP, 128), F32)
        for k in range(3):
            got = dot(pv_ref[k].astype(BF16), basis_ref[k], NT)
            c_ref[k] = got[:, :128]
            rem = rem + got[:, 128:]
        c_ref[3] = rem
        for h in range(GROUP):
            for r in range(OUT_PLANES):
                blk_ref[h % 2, r * CAP : (r + 1) * CAP, :] = c_ref[r, h * CAP : (h + 1) * CAP, :]
            send_ref[g * GROUP + h] = blk_ref[h % 2, : OUT_PLANES * CAP, :].astype(BF16)

    my_y, my_z, my_core = me // 16, me // 2 % 8, me % 2

    def send(g, first=0):
        dy = g // (16 // GROUP)
        rest = g - dy * (16 // GROUP)
        core = rest // (8 // GROUP)
        base = wrap(my_y - dy, slab_count // 16) * 16 + wrap(my_core - core, 2)
        for h in range(first, GROUP):
            dz = (rest - core * (8 // GROUP)) * GROUP + h
            place = base + 2 * wrap(my_z - dz, 8)
            pltpu.make_async_remote_copy(
                src_ref=send_ref.at[g * GROUP + h],
                dst_ref=back_ref.at[g * GROUP + h],
                send_sem=send_sem,
                recv_sem=recv_sem,
                device_id={"slab": place},
                device_id_type=pl.DeviceIdType.MESH,
            ).start()

    groups = slab_count // GROUP
    gather((groups - 1) * GROUP, even_ref)
    work(groups - 1)

    def group(n, carry):
        g = groups - 2 - n
        send(g + 1)
        work(g)
        return carry

    lax.fori_loop(0, groups - 1, group, 0)
    send(0, 1)
    back_ref[0] = send_ref[0]
    others = pl.ds(1, slab_count - 1)
    pltpu.make_async_copy(back_ref.at[others], back_ref.at[others], recv_sem).wait()

    def take(step, carry):
        for side in range(2):
            at = 2 * step + side
            blk_ref[side, : OUT_PLANES * CAP, :] = back_ref[at].astype(F32)
            for r in range(OUT_PLANES):
                r_ref[r, pl.ds(at * CAP, CAP), :] = blk_ref[side, r * CAP : (r + 1) * CAP, :]
        return carry

    lax.fori_loop(0, slab_count // 2, take, 0)
    rem = dot(r_ref[3].astype(BF16), hot, TN)
    for k in range(3):
        main = dot(r_ref[k].astype(BF16), hot, TN)
        out_ref[k, :128] = main
        out_ref[k, 128:] = rem[k * REM : (k + 1) * REM]
    pltpu.make_async_copy(send_ref.at[others], send_ref.at[others], send_sem).wait()


def batch_neighbours():
    batches, b = lax.axis_size("batch"), lax.axis_index("batch")
    return [lax.rem(b + i, batches) for i in range(1, batches)]


def grid_steps(
    part_ref, vel_ref, new_ref, all_ref,
    hop_ref, got_ref, summed_ref, drive_ref, st_ref, own_ref,
    xs_ref, xr_ref, ys_ref, yr_ref, y32_ref, send_sem, recv_sem, local_sem,
):
    planes, mine, _ = vel_ref.shape
    half = planes // 2
    batches, slabs = lax.axis_size("batch"), lax.axis_size("slab")
    b, s = lax.axis_index("batch"), lax.axis_index("slab")
    right, far, left = batch_neighbours()
    above, below = lax.rem(s + 1, slabs), lax.rem(s + slabs - 1, slabs)

    def rows(part):
        return pl.ds(pl.multiple_of(part * mine, mine), mine)

    started = []

    def send(src, dst, **device):
        n = len(started)
        copy = pltpu.make_async_remote_copy(
            src_ref=src, dst_ref=dst, send_sem=send_sem.at[n], recv_sem=recv_sem.at[n],
            device_id=device, device_id_type=pl.DeviceIdType.MESH,
        )
        copy.start()
        started.append(copy)
        return copy

    low, high = pl.ds(0, half), pl.ds(half, half)

    hop_r = send(part_ref.at[low, rows(far)], hop_ref.at[0], batch=right)
    hop_l = send(part_ref.at[high, rows(far)], hop_ref.at[1], batch=left)
    near_r = send(part_ref.at[high, rows(right)], got_ref.at[0], batch=right)
    near_l = send(part_ref.at[low, rows(left)], got_ref.at[1], batch=left)
    hop_r.wait_recv()
    summed_ref[0] = (
        part_ref[low, rows(right), :].astype(F32) + hop_ref[0].astype(F32)
    ).astype(BF16)
    far_r = send(summed_ref.at[0], got_ref.at[2], batch=right)
    hop_l.wait_recv()
    summed_ref[1] = (
        part_ref[high, rows(left), :].astype(F32) + hop_ref[1].astype(F32)
    ).astype(BF16)
    far_l = send(summed_ref.at[1], got_ref.at[3], batch=left)
    drive_ref[...] = vel_ref[...] + part_ref[:, rows(b), :].astype(F32)
    near_r.wait_recv()
    near_l.wait_recv()
    far_r.wait_recv()
    far_l.wait_recv()
    drive_ref[:half] += got_ref[1].astype(F32) + got_ref[2].astype(F32)
    drive_ref[half:] += got_ref[0].astype(F32) + got_ref[3].astype(F32)

    lane = lax.broadcasted_iota(jnp.int32, (mine, 128), 1)
    layer = lax.broadcasted_iota(jnp.int32, (mine, 128), 0) % LAYERS
    at_end, at_start = lane == 127, lane == 0
    has_next, has_previous = layer < LAYERS - 1, layer > 0
    inside = slice(8, 8 + mine)
    for sweep in range(SWEEPS):
        for x in range(planes):
            st_ref[1 + x, inside, :] = drive_ref[x] if sweep == 0 else new_ref[x]
        xs_ref[sweep, 0] = st_ref[planes, inside, :].astype(BF16)
        xs_ref[sweep, 1] = st_ref[1, inside, :].astype(BF16)
        for x in range(planes):
            y32_ref[0, x * LINE : (x + 1) * LINE] = st_ref[1 + x, 2 + mine : 8 + mine, :]
            y32_ref[1, x * LINE : (x + 1) * LINE] = st_ref[1 + x, 8 : 8 + LINE, :]
        for side in range(2):
            ys_ref[sweep, side] = y32_ref[side].astype(BF16)
        copies = [
            send(xs_ref.at[sweep, 0], xr_ref.at[sweep, 0], slab=above),
            send(xs_ref.at[sweep, 1], xr_ref.at[sweep, 1], slab=below),
            send(ys_ref.at[sweep, 0], yr_ref.at[sweep, 0], batch=right),
            send(ys_ref.at[sweep, 1], yr_ref.at[sweep, 1], batch=left),
        ]
        for copy in copies:
            copy.wait_recv()
        x_low, x_high = xr_ref[sweep, 0].astype(F32), xr_ref[sweep, 1].astype(F32)
        st_ref[0, inside, :] = jnp.where(s > 0, x_low, 0.0)
        st_ref[planes + 1, inside, :] = jnp.where(s < slabs - 1, x_high, 0.0)
        y32_ref[0] = jnp.where(b > 0, yr_ref[sweep, 0].astype(F32), 0.0)
        y32_ref[1] = jnp.where(b < batches - 1, yr_ref[sweep, 1].astype(F32), 0.0)
        for x in range(planes):
            st_ref[1 + x, 8 - LINE : 8, :] = y32_ref[0, x * LINE : (x + 1) * LINE]
            st_ref[1 + x, 8 + mine : 8 + mine + LINE, :] = y32_ref[1, x * LINE : (x + 1) * LINE]
        for x in range(planes):
            total = (
                st_ref[x, inside, :]
                + st_ref[x + 2, inside, :]
                + st_ref[x + 1, 8 - LINE : 8 - LINE + mine, :]
                + st_ref[x + 1, 8 + LINE : 8 + LINE + mine, :]
            )
            centre = st_ref[x + 1, inside, :]
            after = jnp.where(has_next, st_ref[x + 1, 9 : 9 + mine, :], 0.0)
            before = jnp.where(has_previous, st_ref[x + 1, 7 : 7 + mine, :], 0.0)
            upper = pltpu.roll(jnp.where(at_start, after, centre), 127, 1)
            lower = pltpu.roll(jnp.where(at_end, before, centre), 1, 1)
            total = total + upper + lower
            new_ref[x] = (drive_ref[x] + coupling * total) * (1.0 / (1.0 + 6.0 * coupling))

    own_ref[...] = new_ref[...].astype(BF16)
    at_right_low = send(own_ref.at[low], all_ref.at[low, rows(b)], batch=right)
    at_left_high = send(own_ref.at[high], all_ref.at[high, rows(b)], batch=left)
    at_right_high = send(own_ref.at[high], all_ref.at[high, rows(b)], batch=right)
    at_left_low = send(own_ref.at[low], all_ref.at[low, rows(b)], batch=left)
    local = pltpu.make_async_copy(own_ref, all_ref.at[:, rows(b)], local_sem)
    local.start()
    at_right_low.wait_recv()
    on_r = send(all_ref.at[low, rows(left)], all_ref.at[low, rows(left)], batch=right)
    at_left_high.wait_recv()
    on_l = send(all_ref.at[high, rows(right)], all_ref.at[high, rows(right)], batch=left)
    for copy in (at_right_high, at_left_low, on_r, on_l):
        copy.wait_recv()
    local.wait()
    for copy in started:
        copy.wait_send()


def step_kernel(
    owner_ref, coef_ref, offs_ref, anchor_ref, blocks_ref, count_ref, syn_ref, ana_ref, vel_ref,
    new_ref, out_ref,
    x_ref, blk_ref, rows_ref, hot_ref, send_ref, recv_ref, send_sem, recv_sem,
    part_ref, wz_ref, wxy_ref, idx_ref, idx_smem,
    r_ref, p_ref, f_ref, lists_ref, next_ref, tx_ref, ty_ref, t_ref, t_old_ref, hit_ref, x_old_ref,
    acc_ref, part32_ref, wide_ref, basis_ref,
    all_ref, hop_ref, got_ref, summed_ref, drive_ref, st_ref, own_ref,
    xs_ref, xr_ref, ys_ref, yr_ref, y32_ref, grid_send_sem, grid_recv_sem, local_sem,
    even_ref, odd_ref, pv_ref, c_ref, coef_send_ref, back_ref, back_send_sem, back_recv_sem,
):
    slab_count = send_ref.shape[0]
    me = lax.axis_index("slab")
    barrier = greet_all(me, slab_count)
    right, _, left = batch_neighbours()
    for device in ({"batch": right}, {"batch": left}):
        pl.semaphore_signal(
            barrier, inc=1, device_id=device, device_id_type=pl.DeviceIdType.MESH
        )
    hot_ref[...] = slot_onehot(owner_ref, slab_count, me)
    pack_blocks(
        hot_ref[...], coef_ref, offs_ref, anchor_ref, blocks_ref, count_ref,
        send_ref, x_ref, blk_ref, rows_ref,
    )
    pl.semaphore_wait(barrier, slab_count + 1)
    spread_cells(
        me, syn_ref, send_ref, recv_ref, send_sem, recv_sem, part_ref, wz_ref, wxy_ref, idx_ref,
        blk_ref, r_ref, p_ref, f_ref, lists_ref, next_ref, tx_ref, ty_ref,
        t_ref, t_old_ref, hit_ref, x_old_ref, acc_ref, part32_ref, wide_ref, basis_ref,
    )
    pltpu.sync_copy(idx_ref, idx_smem)
    basis_planes(ana_ref, wide_ref, basis_ref)
    grid_steps(
        part_ref, vel_ref, new_ref, all_ref,
        hop_ref, got_ref, summed_ref, drive_ref, st_ref, own_ref,
        xs_ref, xr_ref, ys_ref, yr_ref, y32_ref, grid_send_sem, grid_recv_sem, local_sem,
    )
    sample_cells(
        me, hot_ref[...], all_ref, ana_ref, out_ref, wz_ref, wxy_ref, idx_smem,
        part32_ref, even_ref, odd_ref, pv_ref, c_ref, blk_ref, coef_send_ref, back_ref, x_ref,
        wide_ref, basis_ref, back_send_sem, back_recv_sem,
    )


def whole_step(owner, coef, offs, anchor, blocks, count, syn, ana, vel, slab_count):
    planes, mine, _ = vel.shape
    half = planes // 2
    copies = 6 + 4 * SWEEPS + 6
    cells = owner.shape[1]
    slots = slab_count * CAP
    held = GROUP * CAP
    block_rows = PLANES * CAP + 2
    back_rows = OUT_PLANES * CAP
    dma = pltpu.SemaphoreType.DMA
    return pl.pallas_call(
        step_kernel,
        out_shape=(
            jax.ShapeDtypeStruct(vel.shape, F32),
            jax.ShapeDtypeStruct((3, L, cells), F32),
        ),
        in_specs=[VMEM_SPEC] * 9,
        out_specs=(VMEM_SPEC, VMEM_SPEC),
        scratch_shapes=[
            pltpu.VMEM((PLANES + 2, slots, 128), F32),
            pltpu.VMEM((2, block_rows, 128), F32),
            pltpu.VMEM((128, cells), F32),
            pltpu.VMEM((slots, cells), BF16),
            pltpu.VMEM((slab_count, block_rows, 128), BF16),
            pltpu.VMEM((slab_count, block_rows, 128), BF16),
            dma,
            dma((slab_count,)),
            pltpu.VMEM((planes, NY * LINE, 128), BF16),
            pltpu.VMEM((slots, QP // 128, 128, 128), BF16),
            pltpu.VMEM((slots, B, QP), F32),
            pltpu.VMEM((slab_count, 128), jnp.int32),
            pltpu.SMEM((slab_count, 128), jnp.int32),
            pltpu.VMEM((PLANES, held, 128), F32),
            pltpu.VMEM((3, held, QP), F32),
            pltpu.VMEM((3, held, QP), F32),
            pltpu.VMEM((GROUP, 2, 128), F32),
            pltpu.VMEM((GROUP, 2, 128), F32),
            pltpu.VMEM((2, 128, 128), F32),
            pltpu.VMEM((2, 128, 128), F32),
            pltpu.VMEM((3, GROUP * 128, 128), BF16),
            pltpu.VMEM((3, GROUP * 128, 128), BF16),
            pltpu.VMEM((GROUP, NY * LAYERS, 128), BF16),
            pltpu.VMEM((1, GROUP * 128), F32),
            pltpu.VMEM((GX, NY * LAYERS, QP), F32),
            pltpu.VMEM((ROWS, 128), F32),
            pltpu.VMEM((256, QP), F32),
            pltpu.VMEM((3, 256, QP), BF16),
            pltpu.VMEM((planes, NY * LINE, 128), BF16),
            pltpu.VMEM((2, half, mine, 128), BF16),
            pltpu.VMEM((4, half, mine, 128), BF16),
            pltpu.VMEM((2, half, mine, 128), BF16),
            pltpu.VMEM((planes, mine, 128), F32),
            pltpu.VMEM((planes + 2, mine + 16, 128), F32),
            pltpu.VMEM((planes, mine, 128), BF16),
            pltpu.VMEM((SWEEPS, 2, mine, 128), BF16),
            pltpu.VMEM((SWEEPS, 2, mine, 128), BF16),
            pltpu.VMEM((SWEEPS, 2, planes * LINE, 128), BF16),
            pltpu.VMEM((SWEEPS, 2, planes * LINE, 128), BF16),
            pltpu.VMEM((2, planes * LINE, 128), F32),
            dma((copies,)),
            dma((copies,)),
            dma,
            pltpu.VMEM((CAP, 3 * B, 128), F32),
            pltpu.VMEM((CAP, 3 * B, 128), F32),
            pltpu.VMEM((3, held, QP), F32),
            pltpu.VMEM((OUT_PLANES, held, 128), F32),
            pltpu.VMEM((slab_count, back_rows, 128), BF16),
            pltpu.VMEM((slab_count, back_rows, 128), BF16),
            dma,
            dma,
        ],
        compiler_params=pltpu.CompilerParams(
            collective_id=0, has_side_effects=True, vmem_limit_bytes=67_043_328
        ),
        name="whole_step",
    )(owner, coef, offs, anchor, blocks, count, syn, ana, vel)


def local(
    velocity_old, traction, offsets, owner_slab, anchor, blocks, block_count, synthesis, analysis
):
    slab_count = lax.axis_size("slab")
    owner = owner_slab.T
    planes, lines = velocity_old.shape[:2]
    velocity_new, velocity_coef = whole_step(
        owner,
        traction.transpose(1, 2, 0),
        offsets.transpose(1, 0, 2),
        anchor.T,
        blocks.T,
        block_count[None],
        synthesis,
        analysis,
        velocity_old.transpose(0, 1, 3, 2, 4).reshape(planes, lines * LINE, 128),
        slab_count,
    )
    velocity_new = velocity_new.reshape(planes, lines, 3, LAYERS, 128)
    return (velocity_new.transpose(0, 1, 3, 2, 4), velocity_coef.astype(BF16).transpose(2, 0, 1))


def solution(mesh):
    in_specs = (
        P("slab", "batch", None, None, None),
        P(("slab", "batch"), None, None),
        P(("slab", "batch"), None, None),
        P(("slab", "batch"), None),
        P(("slab", "batch"), None),
        P(("slab", "batch"), None),
        P(("slab", "batch")),
        P(),
        P(),
    )
    out_specs = (P("slab", "batch", None, None, None), P(("slab", "batch"), None, None))
    return jax.shard_map(local, mesh=mesh, in_specs=in_specs, out_specs=out_specs, check_vma=False)
```
